32 devices in a mesh: rep: 4 (over x, core), shard: 8 (over z, y).
Axes of the slice: x: 2, y: 2, z: 4, core: 2. Of those that a mesh axis runs over, the one named last changes fastest.
Arguments:
- tokens_in: bfloat16 [4, 2048, 768], P('rep', 'shard'), may hold values from -6 to 6
- segment_ids: int32 [4, 2048], P('rep'), may hold values from 0 to 15, never falling along the last dimension, each value on 1 to 1024 neighbouring positions
- w_qkv: bfloat16 [768, 2304], P('shard'), may hold values from -0.21875 to 0.21875
- w_out: bfloat16 [768, 768], P('shard'), may hold values from -2 to 2
- ln1_gain: bfloat16 [768], P('shard'), may hold values from 0.5 to 1.5
- ln1_bias: bfloat16 [768], P('shard'), may hold values from -3 to 3
- w_gate: bfloat16 [768, 3072], P('shard'), may hold values from -0.21875 to 0.21875
- w_up: bfloat16 [768, 3072], P('shard'), may hold values from -0.21875 to 0.21875
- w_down: bfloat16 [3072, 768], P('shard'), may hold values from -0.109375 to 0.109375
- ln2_gain: bfloat16 [768], P('shard'), may hold values from 0.5 to 1.5
- ln2_bias: bfloat16 [768], P('shard'), may hold values from -3 to 3
- out_cotangent: bfloat16 [4, 2048, 768], P('rep', 'shard'), may hold values from -6 to 6
Outputs:
- out: bfloat16 [4, 2048, 768], P('rep', 'shard')
- in_grad: float32 [4, 2048, 768], P('rep', 'shard')
- grad_w_qkv: float32 [768, 2304], P('shard')
- grad_w_out: float32 [768, 768], P('shard')
- grad_ln1_gain: float32 [768], P('shard')
- grad_ln1_bias: float32 [768], P('shard')
- grad_w_gate: float32 [768, 3072], P('shard')
- grad_w_up: float32 [768, 3072], P('shard')
- grad_w_down: float32 [3072, 768], P('shard')
- grad_ln2_gain: float32 [768], P('shard')
- grad_ln2_bias: float32 [768], P('shard')
The draws below stay inside these ranges and needn't reach their ends.
Inputs may be any that keep to these rules, and one draw needn't show every extreme that they name: `segment_ids`: within each sequence the ids never fall; each of the 16 documents holds 1 to 1024 tokens and one holds exactly 1024.
All inputs are finite; a program needn't handle non-finite values.
Results may differ from the reference program's by a relative error of at most 0.023.
Values may be sent and summed in bfloat16 or wider, within the bound.
No kernel may reach another device: no remote copies, remote signals or barrier semaphores. Data moves between devices by JAX's collectives and lax.ppermute only.
A program may use at most 256 MiB of HBM per device.

```python
import math
import jax
import jax.numpy as jnp
import numpy as np
from jax import lax

D = 768
FF = 3072
HEAD_DIM = 64
HEADS = 12
LEN = 2048
SEQS = 4
DOCS = 16
LONGEST = 1024


def shard_levels(rng, dims, pieces, smallest, high):
    loudness, own = 1.0, jax.random.fold_in(rng, 6)
    for dim, blocks in pieces:
        heights = jnp.exp(jax.random.uniform(jax.random.fold_in(own, dim), (blocks,), jnp.float32, smallest / len(pieces), high / len(pieces)))
        loudness = loudness * jnp.repeat(heights, dims[dim] // blocks).reshape([-1 if axis == dim else 1 for axis in range(len(dims))])
    return loudness


def profile(amount, total, limit, skew):
    loads = [(1 << 20) // math.isqrt(rank ** skew) + 1 for rank in range(2, amount + 1)]
    surplus, counts = total - limit - (amount - 1), [1] * (amount - 1)
    while surplus > 0:
        movable = [i for i in range(amount - 1) if counts[i] < limit]
        pool, budget = sum([loads[i] for i in movable]), surplus
        for i in movable:
            addition = min(limit - counts[i], max(1, budget * loads[i] // pool), surplus)
            counts[i] = counts[i] + addition
            surplus = surplus - addition
    return np.array([limit] + counts)


def uneven_parts(own_key, number_of, total, bound, slope):
    if number_of == 2:
        one = jax.random.randint(own_key, (), max(1, total - bound), min(bound, total - 1) + 1)
        return jnp.stack([one, total - one])
    lengths = jnp.asarray(profile(number_of, total, bound, slope), jnp.int32)
    pairs = (number_of - 1) // 2
    giver, receiver = lengths[1:1 + 2 * pairs:2], lengths[2:2 + 2 * pairs:2]
    slack = jnp.minimum(giver - 1, bound - receiver)
    moved = jax.random.randint(jax.random.fold_in(own_key, 1), (pairs,), 0, 1 << 20) % (slack + 1)
    lengths = lengths.at[1:1 + 2 * pairs:2].set(giver - moved).at[2:2 + 2 * pairs:2].set(receiver + moved)
    return lengths[jax.random.permutation(jax.random.fold_in(own_key, 2), number_of)]


def normal_values(key, shape, width, limit, split=(), kind=jnp.bfloat16):
    loudness = shard_levels(key, shape, split, -0.22, 0.18) if split else 1.0
    entries = jax.random.normal(key, shape, jnp.float32) * width * loudness
    return jnp.minimum(jnp.maximum(entries, -limit), limit).astype(kind)


def setup_inputs(seed: int = 0) -> dict:
    key_of = jax.random.split(jax.random.key(seed), 13)
    tokens_in = normal_values(key_of[0], (SEQS, LEN, D), 1.0, 6.0, ((0, 4), (1, 8)))
    segment_ids = jax.vmap(lambda own: jnp.searchsorted(jnp.cumsum(uneven_parts(own, DOCS, LEN, LONGEST, 2)), jnp.arange(LEN), side="right"))(jax.random.split(key_of[1], SEQS)).reshape((SEQS, LEN)).astype(jnp.int32)
    w_qkv = normal_values(key_of[2], (D, 3 * D), D ** -0.5, 0.21875, ((0, 8),))
    w_out = normal_values(key_of[3], (D, D), 8 ** -0.5, 2.0, ((0, 8),))
    ln1_gain = jnp.clip(1.0 + 0.1 * jax.random.normal(key_of[4], (D,), jnp.float32), 0.5, 1.5).astype(jnp.bfloat16)
    ln1_bias = normal_values(key_of[5], (D,), 0.5, 3.0, ((0, 8),))
    w_gate = normal_values(key_of[6], (D, FF), D ** -0.5, 0.21875, ((0, 8),))
    w_up = normal_values(key_of[7], (D, FF), D ** -0.5, 0.21875, ((0, 8),))
    w_down = normal_values(key_of[8], (FF, D), FF ** -0.5, 0.109375, ((0, 8),))
    ln2_gain = jnp.clip(1.0 + 0.1 * jax.random.normal(key_of[9], (D,), jnp.float32), 0.5, 1.5).astype(jnp.bfloat16)
    ln2_bias = normal_values(key_of[10], (D,), 0.5, 3.0, ((0, 8),))
    out_cotangent = normal_values(key_of[11], (SEQS, LEN, D), 1.0, 6.0, ((0, 4), (1, 8)))
    return {"tokens_in": tokens_in, "segment_ids": segment_ids, "w_qkv": w_qkv, "w_out": w_out, "ln1_gain": ln1_gain, "ln1_bias": ln1_bias, "w_gate": w_gate, "w_up": w_up, "w_down": w_down, "ln2_gain": ln2_gain, "ln2_bias": ln2_bias, "out_cotangent": out_cotangent}


@jax.custom_vjp
def low(v):
    return lax.optimization_barrier(v.astype(jnp.bfloat16)).astype(jnp.float32)

@jax.custom_vjp
def low_back(v):
    return v

def low_keep(v):
    return (low(v), None)

def low_pass(kept, grad):
    return (grad,)

def back_keep(v):
    return (v, None)

def back_low(kept, grad):
    return (low(grad),)
low.defvjp(low_keep, low_pass)
low_back.defvjp(back_keep, back_low)
epsilon = 1e-05
rope_base = 1000.0
highest = lax.Precision.HIGHEST

def matmul_high(left, right):
    return jnp.dot(left, right, precision=highest, preferred_element_type=jnp.float32)

def rope_tables(start, count):
    positions = (start + jnp.arange(count, dtype=jnp.int32)).astype(jnp.float32)
    middle = HEAD_DIM // 2
    inverse = rope_base ** (-(2.0 * jnp.arange(middle).astype(jnp.float32)) / HEAD_DIM)
    angles = positions[:, None] * inverse[None, :]
    return (jnp.cos(angles)[:, None, :], jnp.sin(angles)[:, None, :])

def rotate(values_in, cosine, sine):
    middle = values_in.shape[-1] // 2
    first_half = values_in[..., :middle]
    second_half = values_in[..., middle:]
    return jnp.concatenate([first_half * cosine - second_half * sine, second_half * cosine + first_half * sine], axis=-1)

def layer_norm(values_in, gain_vec, shift_vec):
    centred = values_in - lax.optimization_barrier(jnp.mean(values_in, axis=-1, keepdims=True))
    variance = lax.optimization_barrier(jnp.mean(centred * centred, axis=-1, keepdims=True))
    return centred * lax.rsqrt(variance + epsilon) * gain_vec + shift_vec

def head_attention(item):
    query_rows, key_rows, value_rows, doc_ids = item
    scores = low_back(jnp.einsum('qd,kd->qk', query_rows, key_rows, precision=highest) * HEAD_DIM ** (-0.5))
    same_doc = doc_ids[:, None] == doc_ids[None, :]
    weights = jax.nn.softmax(jnp.where(same_doc, scores, -jnp.inf), axis=-1)
    return jnp.einsum('qk,kd->qd', low(weights), value_rows, precision=highest)

def forward(tokens, weight_qkv, weight_out, gain_one, bias_one, weight_gate, weight_up, weight_down, gain_two, bias_two, segments):
    seq_count, length = segments.shape
    flat_rows = tokens.reshape(seq_count * length, D)
    projected = low_back(matmul_high(flat_rows, weight_qkv))
    cosine, sine = rope_tables(0, length)

    def head_major(heads_form):
        return jnp.transpose(low(heads_form), (0, 2, 1, 3)).reshape(seq_count * HEADS, length, HEAD_DIM)
    shape_four = (seq_count, length, HEADS, HEAD_DIM)
    queries = head_major(rotate(projected[:, :D].reshape(shape_four), cosine, sine))
    key_rows = head_major(rotate(projected[:, D:2 * D].reshape(shape_four), cosine, sine))
    value_rows = head_major(projected[:, 2 * D:].reshape(shape_four))
    doc_rows = jnp.repeat(segments, HEADS, axis=0)
    attended = lax.map(jax.checkpoint(head_attention), (queries, key_rows, value_rows, doc_rows))
    attended = jnp.transpose(attended.reshape(seq_count, HEADS, length, HEAD_DIM), (0, 2, 1, 3)).reshape(seq_count * length, D)
    attended = low(low_back(attended))
    branch = low_back(matmul_high(attended, weight_out))
    first_out = layer_norm(flat_rows + branch, gain_one, bias_one)
    first_low = low(first_out)
    gate_act = low_back(matmul_high(first_low, weight_gate))
    up_act = low_back(matmul_high(first_low, weight_up))
    hidden = low(jax.nn.silu(gate_act) * up_act)
    down_act = low_back(matmul_high(hidden, weight_down))
    return layer_norm(first_out + down_act, gain_two, bias_two).reshape(tokens.shape)

def reference(tokens_in, segment_ids, w_qkv, w_out, ln1_gain, ln1_bias, w_gate, w_up, w_down, ln2_gain, ln2_bias, out_cotangent):
    tokens_f = tokens_in.astype(jnp.float32)
    qkv_f = w_qkv.astype(jnp.float32)
    out_f = w_out.astype(jnp.float32)
    gain_one_f = ln1_gain.astype(jnp.float32)
    bias_one_f = ln1_bias.astype(jnp.float32)
    gate_f = w_gate.astype(jnp.float32)
    up_f = w_up.astype(jnp.float32)
    down_f = w_down.astype(jnp.float32)
    gain_two_f = ln2_gain.astype(jnp.float32)
    bias_two_f = ln2_bias.astype(jnp.float32)

    def closed(tokens, weight_qkv, weight_out, gain_one, bias_one, weight_gate, weight_up, weight_down, gain_two, bias_two):
        return forward(tokens, weight_qkv, weight_out, gain_one, bias_one, weight_gate, weight_up, weight_down, gain_two, bias_two, segment_ids)
    result, pullback = jax.vjp(closed, tokens_f, qkv_f, out_f, gain_one_f, bias_one_f, gate_f, up_f, down_f, gain_two_f, bias_two_f)
    grads = pullback(out_cotangent.astype(jnp.float32))
    return (result.astype(jnp.bfloat16), grads[0], grads[1], grads[2], grads[3], grads[4], grads[5], grads[6], grads[7], grads[8], grads[9])
```

```python
import jax
import jax.numpy as jnp
from jax import lax
from jax.experimental import pallas as pl
from jax.experimental.pallas import tpu as pltpu
from jax.sharding import PartitionSpec as P

D = 768
HEAD_DIM = 64
HEADS = 12


epsilon = 1e-05
rope_base = 1000.0


def rope_tables(start, count):
    positions = (start + jnp.arange(count, dtype=jnp.int32)).astype(jnp.float32)
    middle = HEAD_DIM // 2
    inverse = rope_base ** (-(2.0 * jnp.arange(middle).astype(jnp.float32)) / HEAD_DIM)
    angles = positions[:, None] * inverse[None, :]
    return (jnp.cos(angles)[:, None, :], jnp.sin(angles)[:, None, :])


def rotate(values_in, cosine, sine):
    middle = values_in.shape[-1] // 2
    first_half = values_in[..., :middle]
    second_half = values_in[..., middle:]
    return jnp.concatenate(
        [first_half * cosine - second_half * sine, second_half * cosine + first_half * sine],
        axis=-1,
    )


def rotate_back(upstream, cosine, sine):
    middle = upstream.shape[-1] // 2
    first_half = upstream[..., :middle]
    second_half = upstream[..., middle:]
    return jnp.concatenate(
        [first_half * cosine + second_half * sine, second_half * cosine - first_half * sine],
        axis=-1,
    )


def norm_forward(values_in, gain_vec, shift_vec):
    centred = values_in - jnp.mean(values_in, axis=-1, keepdims=True)
    variance = jnp.mean(centred * centred, axis=-1, keepdims=True)
    inverse_scale = lax.rsqrt(variance + epsilon)
    normed = centred * inverse_scale
    return (normed * gain_vec + shift_vec, normed, inverse_scale)


def norm_backward(upstream, normed, inverse_scale, gain_vec):
    scaled = upstream * gain_vec
    return inverse_scale * (
        scaled
        - jnp.mean(scaled, axis=-1, keepdims=True)
        - normed * jnp.mean(scaled * normed, axis=-1, keepdims=True)
    )


def fetch_attention(w_qkv, w_out, ln1_gain, ln1_bias):
    return (
        lax.all_gather(w_qkv, "shard", axis=0, tiled=True),
        lax.all_gather(w_out, "shard", axis=0, tiled=True),
        lax.all_gather(ln1_gain, "shard", axis=0, tiled=True),
        lax.all_gather(ln1_bias, "shard", axis=0, tiled=True),
    )


def fetch_feedforward(w_gate, w_up, w_down, ln2_gain, ln2_bias):
    return (
        lax.all_gather(w_gate, "shard", axis=0, tiled=True),
        lax.all_gather(w_up, "shard", axis=0, tiled=True),
        lax.all_gather(w_down, "shard", axis=0, tiled=True),
        lax.all_gather(ln2_gain, "shard", axis=0, tiled=True),
        lax.all_gather(ln2_bias, "shard", axis=0, tiled=True),
    )


def pair_columns(matrix, pair_index):
    width = 2 * HEAD_DIM
    return lax.dynamic_slice_in_dim(matrix, pair_index * width, width, 1).reshape(
        matrix.shape[0], 2, HEAD_DIM
    )


def pair_scores(pair_index, queries, key_rows, same_doc):
    scores = jnp.einsum(
        "qhd,khd->hqk",
        pair_columns(queries, pair_index),
        pair_columns(key_rows, pair_index),
        preferred_element_type=jnp.float32,
    ) * HEAD_DIM ** (-0.5)
    return jnp.where(same_doc[None], scores, -jnp.inf)


def attention_forward(queries, key_rows, value_rows, same_doc):

    def one_pair(pair_index):
        scores = pair_scores(pair_index, queries, key_rows, same_doc)
        row_max = jnp.max(scores, axis=-1, keepdims=True)
        expons = jnp.exp(scores - row_max)
        row_total = jnp.sum(expons, axis=-1, keepdims=True)
        weights_bf = (expons / row_total).astype(jnp.bfloat16)
        attended = jnp.einsum(
            "hqk,khd->qhd",
            weights_bf,
            pair_columns(value_rows, pair_index),
            preferred_element_type=jnp.float32,
        )
        return (
            attended.reshape(attended.shape[0], 2 * HEAD_DIM),
            (row_max + jnp.log(row_total))[..., 0],
        )

    attended, log_totals = lax.map(one_pair, jnp.arange(HEADS // 2, dtype=jnp.int32))
    return (jnp.transpose(attended, (1, 0, 2)).reshape(queries.shape[0], D), log_totals)


def attention_backward(queries, key_rows, value_rows, grad_attended, log_totals, same_doc):
    scale_factor = HEAD_DIM ** (-0.5)
    width = 2 * HEAD_DIM

    def one_pair(inputs):
        pair_index, pair_logs = inputs
        scores = pair_scores(pair_index, queries, key_rows, same_doc)
        weights = jnp.exp(scores - pair_logs[..., None])
        grad_pair = pair_columns(grad_attended, pair_index)
        grad_weights = jnp.einsum(
            "qhd,khd->hqk",
            grad_pair,
            pair_columns(value_rows, pair_index),
            preferred_element_type=jnp.float32,
        )
        row_delta = jnp.sum(weights * grad_weights, axis=-1, keepdims=True)
        grad_scores = (weights * (grad_weights - row_delta)).astype(jnp.bfloat16)
        grad_query = (
            jnp.einsum(
                "hqk,khd->qhd",
                grad_scores,
                pair_columns(key_rows, pair_index),
                preferred_element_type=jnp.float32,
            )
            * scale_factor
        )
        grad_key = (
            jnp.einsum(
                "hqk,qhd->khd",
                grad_scores,
                pair_columns(queries, pair_index),
                preferred_element_type=jnp.float32,
            )
            * scale_factor
        )
        grad_value = jnp.einsum(
            "hqk,qhd->khd",
            weights.astype(jnp.bfloat16),
            grad_pair,
            preferred_element_type=jnp.float32,
        )
        return (
            grad_query.reshape(-1, width),
            grad_key.reshape(-1, width),
            grad_value.reshape(-1, width),
        )

    pair_grads = lax.map(one_pair, (jnp.arange(HEADS // 2, dtype=jnp.int32), log_totals))
    return tuple(
        (
            jnp.transpose(pair_part, (1, 0, 2)).reshape(pair_part.shape[1], D)
            for pair_part in pair_grads
        )
    )


def per_device(
    tokens_in,
    segment_ids,
    w_qkv,
    w_out,
    ln1_gain,
    ln1_bias,
    w_gate,
    w_up,
    w_down,
    ln2_gain,
    ln2_bias,
    out_cotangent,
):
    inputs_bf = tokens_in.reshape(-1, D)
    token_count = inputs_bf.shape[0]
    doc_ids = segment_ids.reshape(-1)
    start = lax.axis_index("shard") * token_count
    own_docs = lax.dynamic_slice_in_dim(doc_ids, start, token_count)
    same_doc = own_docs[:, None] == doc_ids[None, :]
    cosine, sine = rope_tables(start, token_count)
    heads_shape = (token_count, HEADS, HEAD_DIM)
    qkv_full, out_full, gain_one, bias_one = fetch_attention(w_qkv, w_out, ln1_gain, ln1_bias)
    projected = jnp.dot(inputs_bf, qkv_full, preferred_element_type=jnp.float32)
    queries = (
        rotate(projected[:, :D].reshape(heads_shape), cosine, sine)
        .reshape(token_count, D)
        .astype(jnp.bfloat16)
    )
    own_keys = (
        rotate(projected[:, D : 2 * D].reshape(heads_shape), cosine, sine)
        .reshape(token_count, D)
        .astype(jnp.bfloat16)
    )
    own_values = projected[:, 2 * D :].astype(jnp.bfloat16)
    key_rows, value_rows = (
        lax.all_gather(own_keys, "shard", axis=0, tiled=True),
        lax.all_gather(own_values, "shard", axis=0, tiled=True),
    )
    attended, log_totals = attention_forward(queries, key_rows, value_rows, same_doc)
    attended_bf = attended.astype(jnp.bfloat16)
    branch = jnp.dot(attended_bf, out_full, preferred_element_type=jnp.float32)
    inputs_f = inputs_bf.astype(jnp.float32)
    first_out, first_normed, first_scale = norm_forward(
        inputs_f + branch, gain_one.astype(jnp.float32), bias_one.astype(jnp.float32)
    )
    gate_full, up_full, down_full, gain_two, bias_two = fetch_feedforward(
        w_gate, w_up, w_down, ln2_gain, ln2_bias
    )
    first_bf = first_out.astype(jnp.bfloat16)
    gate_act = jnp.dot(first_bf, gate_full, preferred_element_type=jnp.float32)
    up_act = jnp.dot(first_bf, up_full, preferred_element_type=jnp.float32)
    hidden_bf = (jax.nn.silu(gate_act) * up_act).astype(jnp.bfloat16)
    down_act = jnp.dot(hidden_bf, down_full, preferred_element_type=jnp.float32)
    result, second_normed, second_scale = norm_forward(
        first_out + down_act, gain_two.astype(jnp.float32), bias_two.astype(jnp.float32)
    )
    gate_full, up_full, down_full, gain_two, bias_two = fetch_feedforward(
        w_gate, w_up, w_down, ln2_gain, ln2_bias
    )
    upstream = out_cotangent.reshape(-1, D).astype(jnp.float32)
    grad_gain_two = jnp.sum(upstream * second_normed, axis=0)
    grad_bias_two = jnp.sum(upstream, axis=0)
    grad_second = norm_backward(upstream, second_normed, second_scale, gain_two.astype(jnp.float32))
    grad_down_bf = grad_second.astype(jnp.bfloat16)
    grad_down_w = jnp.einsum(
        "tf,td->fd", hidden_bf, grad_down_bf, preferred_element_type=jnp.float32
    )
    grad_hidden = jnp.einsum(
        "td,fd->tf", grad_down_bf, down_full, preferred_element_type=jnp.float32
    )
    sigmoid_gate = jax.nn.sigmoid(gate_act)
    grad_gate_bf = (
        grad_hidden * up_act * sigmoid_gate * (1.0 + gate_act * (1.0 - sigmoid_gate))
    ).astype(jnp.bfloat16)
    grad_up_bf = (grad_hidden * jax.nn.silu(gate_act)).astype(jnp.bfloat16)
    grad_gate_w = jnp.einsum(
        "td,tf->df", first_bf, grad_gate_bf, preferred_element_type=jnp.float32
    )
    grad_up_w = jnp.einsum("td,tf->df", first_bf, grad_up_bf, preferred_element_type=jnp.float32)
    grad_first = grad_second + jnp.einsum(
        "tf,df->td", grad_gate_bf, gate_full, preferred_element_type=jnp.float32
    )
    grad_first = grad_first + jnp.einsum(
        "tf,df->td", grad_up_bf, up_full, preferred_element_type=jnp.float32
    )
    qkv_full, out_full, gain_one, bias_one = fetch_attention(w_qkv, w_out, ln1_gain, ln1_bias)
    grad_gain_one = jnp.sum(grad_first * first_normed, axis=0)
    grad_bias_one = jnp.sum(grad_first, axis=0)
    grad_res = norm_backward(grad_first, first_normed, first_scale, gain_one.astype(jnp.float32))
    grad_branch_bf = grad_res.astype(jnp.bfloat16)
    grad_out_w = jnp.einsum(
        "tc,td->cd", attended_bf, grad_branch_bf, preferred_element_type=jnp.float32
    )
    grad_attended_bf = jnp.einsum(
        "td,cd->tc", grad_branch_bf, out_full, preferred_element_type=jnp.float32
    ).astype(jnp.bfloat16)
    grad_queries, grad_keys_all, grad_values_all = attention_backward(
        queries, key_rows, value_rows, grad_attended_bf, log_totals, same_doc
    )
    grad_keys, grad_values = (
        lax.psum_scatter(
            grad_keys_all.astype(jnp.bfloat16), "shard", scatter_dimension=0, tiled=True
        ).astype(jnp.float32),
        lax.psum_scatter(
            grad_values_all.astype(jnp.bfloat16), "shard", scatter_dimension=0, tiled=True
        ).astype(jnp.float32),
    )
    grad_projected = jnp.concatenate(
        [
            rotate_back(grad_queries.reshape(heads_shape), cosine, sine).reshape(token_count, D),
            rotate_back(grad_keys.reshape(heads_shape), cosine, sine).reshape(token_count, D),
            grad_values,
        ],
        axis=1,
    ).astype(jnp.bfloat16)
    grad_qkv_w = jnp.einsum(
        "td,tn->dn", inputs_bf, grad_projected, preferred_element_type=jnp.float32
    )
    grad_inputs = grad_res + jnp.einsum(
        "tn,dn->td", grad_projected, qkv_full, preferred_element_type=jnp.float32
    )
    (
        sum_qkv,
        sum_out,
        sum_gain_one,
        sum_bias_one,
        sum_gate,
        sum_up,
        sum_down,
        sum_gain_two,
        sum_bias_two,
    ) = (
        lax.psum_scatter(
            grad_qkv_w.astype(jnp.bfloat16), "shard", scatter_dimension=0, tiled=True
        ).astype(jnp.float32),
        lax.psum_scatter(
            grad_out_w.astype(jnp.bfloat16), "shard", scatter_dimension=0, tiled=True
        ).astype(jnp.float32),
        lax.psum_scatter(
            grad_gain_one.astype(jnp.bfloat16), "shard", scatter_dimension=0, tiled=True
        ).astype(jnp.float32),
        lax.psum_scatter(
            grad_bias_one.astype(jnp.bfloat16), "shard", scatter_dimension=0, tiled=True
        ).astype(jnp.float32),
        lax.psum_scatter(
            grad_gate_w.astype(jnp.bfloat16), "shard", scatter_dimension=0, tiled=True
        ).astype(jnp.float32),
        lax.psum_scatter(
            grad_up_w.astype(jnp.bfloat16), "shard", scatter_dimension=0, tiled=True
        ).astype(jnp.float32),
        lax.psum_scatter(
            grad_down_w.astype(jnp.bfloat16), "shard", scatter_dimension=0, tiled=True
        ).astype(jnp.float32),
        lax.psum_scatter(
            grad_gain_two.astype(jnp.bfloat16), "shard", scatter_dimension=0, tiled=True
        ).astype(jnp.float32),
        lax.psum_scatter(
            grad_bias_two.astype(jnp.bfloat16), "shard", scatter_dimension=0, tiled=True
        ).astype(jnp.float32),
    )
    totals = (
        lax.psum(sum_qkv.astype(jnp.bfloat16), "rep").astype(jnp.float32),
        lax.psum(sum_out.astype(jnp.bfloat16), "rep").astype(jnp.float32),
        lax.psum(sum_gain_one.astype(jnp.bfloat16), "rep").astype(jnp.float32),
        lax.psum(sum_bias_one.astype(jnp.bfloat16), "rep").astype(jnp.float32),
        lax.psum(sum_gate.astype(jnp.bfloat16), "rep").astype(jnp.float32),
        lax.psum(sum_up.astype(jnp.bfloat16), "rep").astype(jnp.float32),
        lax.psum(sum_down.astype(jnp.bfloat16), "rep").astype(jnp.float32),
        lax.psum(sum_gain_two.astype(jnp.bfloat16), "rep").astype(jnp.float32),
        lax.psum(sum_bias_two.astype(jnp.bfloat16), "rep").astype(jnp.float32),
    )
    return (
        result.astype(jnp.bfloat16).reshape(tokens_in.shape),
        grad_inputs.reshape(tokens_in.shape),
        totals[0],
        totals[1],
        totals[2],
        totals[3],
        totals[4],
        totals[5],
        totals[6],
        totals[7],
        totals[8],
    )


BF = jnp.bfloat16
F32 = jnp.float32
AXES = ("rep", "shard")
TILE = 256
GROUP = 4
OWN_HEADS = 3
NARROW = OWN_HEADS * HEAD_DIM
WIDE = 256
LOG2E = 1.4426950408889634
SCORE_FACTOR = HEAD_DIM ** (-0.5) * LOG2E
MASKED = -1e30


def moves(target):
    pairs = []
    for rep in range(4):
        for shard in range(8):
            goal = target(rep // 2, rep % 2, shard // 4, shard % 4)
            if goal is not None:
                x, c, h, j = goal
                pairs.append((rep * 8 + shard, (2 * x + c) * 8 + 4 * h + j))
    return pairs


SPREAD = moves(lambda x, c, h, j: (x, h, c, j))
OTHER_CORE = moves(lambda x, c, h, j: (x, 1 - c, h, j))
OTHER_X = moves(lambda x, c, h, j: (1 - x, c, h, j))
OTHER_HALF = moves(lambda x, c, h, j: (x, c, 1 - h, j))
SQUARE = [moves(lambda x, c, h, j, k=k: (x, c, h, j ^ k)) for k in range(GROUP)]
ROUND = [moves(lambda x, c, h, j, k=k: (x, c, h ^ c, j ^ k)) for k in range(GROUP)]
OUT_FETCH = moves(lambda x, c, h, j: (x, j % 2, c, (4 * h + j) // 2))
OUT_RETURN = moves(lambda x, c, h, j: (x, h, (2 * j + c) // 4, (2 * j + c) % 4))
HOME_HALF = moves(lambda x, c, h, j: (x, c, 1 - h, j) if c != h else None)
HOME_SQUARE = [
    moves(lambda x, c, h, j, k=k: (x, c, h, j ^ k) if c == h else None) for k in range(GROUP)
]
HOME_X = moves(lambda x, c, h, j: (1 - x, c, h, j) if c == h else None)
HOME_CORE = moves(lambda x, c, h, j: (x, 1 - c, h, j) if c == h else None)


def send(value, pairs):
    return lax.ppermute(value, AXES, pairs)


def pick(flag, first, second):
    return jnp.where(flag, second, first)


def unmix(blocks, j):
    bit0 = (j % 2) == 1
    bit1 = (j // 2) == 1
    b = blocks
    b = [pick(bit0, b[0], b[1]), pick(bit0, b[1], b[0]), pick(bit0, b[2], b[3]), pick(bit0, b[3], b[2])]
    return [pick(bit1, b[0], b[2]), pick(bit1, b[1], b[3]), pick(bit1, b[2], b[0]), pick(bit1, b[3], b[1])]


def turned(values):
    lane = lax.broadcasted_iota(jnp.int32, values.shape, 1) % HEAD_DIM
    middle = HEAD_DIM // 2
    return jnp.where(
        lane < middle,
        -pltpu.roll(values, WIDE - middle, 1),
        pltpu.roll(values, middle, 1),
    )


def doubled(table):
    return jnp.concatenate([table, table], axis=1)


def project_kernel(x_ref, w_ref, cos_ref, sin_ref, q_ref, kv_ref):
    projected = jnp.dot(x_ref[...], w_ref[...], preferred_element_type=F32)
    cosine = doubled(cos_ref[...])
    sine = doubled(sin_ref[...])
    for index, ref in ((0, q_ref), (1, kv_ref)):
        part = projected[:, index * WIDE : (index + 1) * WIDE]
        ref[:, :WIDE] = (part * cosine + turned(part) * sine).astype(BF)
    kv_ref[:, WIDE:] = projected[:, 2 * WIDE :].astype(BF)


def project(x_rows, w_qkv, cosine, sine):
    rows = x_rows.shape[0]
    return pl.pallas_call(
        project_kernel,
        grid=(rows // TILE,),
        in_specs=[
            pl.BlockSpec((TILE, D), lambda i: (i, 0)),
            pl.BlockSpec((D, 3 * WIDE), lambda i: (0, 0)),
            pl.BlockSpec((TILE, 128), lambda i: (i, 0)),
            pl.BlockSpec((TILE, 128), lambda i: (i, 0)),
        ],
        out_specs=[
            pl.BlockSpec((TILE, WIDE), lambda i: (i, 0)),
            pl.BlockSpec((TILE, 2 * WIDE), lambda i: (i, 0)),
        ],
        out_shape=[
            jax.ShapeDtypeStruct((rows, WIDE), BF),
            jax.ShapeDtypeStruct((rows, 2 * WIDE), BF),
        ],
        name="project",
    )(x_rows, w_qkv, cosine, sine)


def head_only(values, head):
    lane = lax.broadcasted_iota(jnp.int32, values.shape, 1) // HEAD_DIM
    return jnp.where(lane == head, values, jnp.zeros_like(values))


def share_document(ids_ref, q_tile, kv_tile):
    q_first = ids_ref[q_tile * TILE]
    q_last = ids_ref[q_tile * TILE + TILE - 1]
    k_first = ids_ref[kv_tile * TILE]
    k_last = ids_ref[kv_tile * TILE + TILE - 1]
    return jnp.logical_and(k_first <= q_last, q_first <= k_last)


def contract(left, right, left_dim, right_dim):
    return lax.dot_general(
        left, right, (((left_dim,), (right_dim,)), ((), ())), preferred_element_type=F32
    )


def attend_kernel(
    ids_ref, row_ids_ref, col_ids_ref, q_ref, own_ref, other_ref, out_ref, log_ref,
    v_turned, max_ref, total_ref, acc_ref,
):
    q_tile = pl.program_id(0)
    own_tiles = own_ref.shape[0] // TILE

    @pl.when(q_tile == 0)
    def _():
        for base, ref in ((0, own_ref), (own_tiles, other_ref)):
            for tile in range(own_tiles):
                v_turned[base + tile] = jnp.transpose(
                    ref[pl.ds(tile * TILE, TILE), WIDE:]
                )[:NARROW]

    queries = q_ref[...]
    per_head = [head_only(queries, head) for head in range(OWN_HEADS)]
    q_ids = row_ids_ref[0]
    max_ref[...] = jnp.full(max_ref.shape, MASKED, F32)
    total_ref[...] = jnp.zeros(total_ref.shape, F32)
    acc_ref[...] = jnp.zeros(acc_ref.shape, F32)

    for base, ref in ((0, own_ref), (own_tiles, other_ref)):

        def one_tile(tile, carry, base=base, ref=ref):
            @pl.when(share_document(ids_ref, q_tile, base + tile))
            def _():
                start = pl.multiple_of(tile * TILE, TILE)
                keys = ref[pl.ds(start, TILE), :WIDE]
                same = (
                    col_ids_ref[pl.ds(pl.multiple_of((base + tile) * TILE, TILE), TILE), :] == q_ids
                )
                for head in range(OWN_HEADS):
                    scores = contract(keys, per_head[head], 1, 1) * SCORE_FACTOR
                    scores = jnp.where(same, scores, MASKED)
                    old_max = max_ref[head : head + 1, :]
                    new_max = jnp.maximum(old_max, jnp.max(scores, axis=0, keepdims=True))
                    shrink = jnp.exp2(old_max - new_max)
                    expons = jnp.exp2(scores - new_max)
                    max_ref[head : head + 1, :] = new_max
                    total_ref[head : head + 1, :] = total_ref[
                        head : head + 1, :
                    ] * shrink + jnp.sum(expons, axis=0, keepdims=True)
                    rows = slice(head * HEAD_DIM, (head + 1) * HEAD_DIM)
                    acc_ref[rows, :] = acc_ref[rows, :] * shrink + jnp.dot(
                        v_turned[base + tile, rows, :],
                        expons.astype(BF),
                        preferred_element_type=F32,
                    )

            return carry

        lax.fori_loop(0, own_tiles, one_tile, 0)

    parts = []
    for head in range(OWN_HEADS):
        rows = slice(head * HEAD_DIM, (head + 1) * HEAD_DIM)
        parts.append(acc_ref[rows, :] / total_ref[head : head + 1, :])
    parts.append(jnp.zeros((WIDE - NARROW, TILE), F32))
    out_ref[...] = jnp.transpose(jnp.concatenate(parts, axis=0)).astype(BF)
    row = lax.broadcasted_iota(jnp.int32, log_ref.shape, 0)
    log_ref[...] = jnp.where(
        row < OWN_HEADS,
        max_ref[...] + jnp.log2(jnp.where(row < OWN_HEADS, total_ref[...], 1.0)),
        0.0,
    )


def attend(ids, row_ids, col_ids, queries, kv_own, kv_other):
    rows = queries.shape[0]
    whole = lambda array: pl.BlockSpec(array.shape, lambda i, ids: (0,) * array.ndim)
    return pl.pallas_call(
        attend_kernel,
        grid_spec=pltpu.PrefetchScalarGridSpec(
            num_scalar_prefetch=1,
            grid=(rows // TILE,),
            in_specs=[
                pl.BlockSpec((1, 1, TILE), lambda i, ids: (i, 0, 0)),
                whole(col_ids),
                pl.BlockSpec((TILE, WIDE), lambda i, ids: (i, 0)),
                whole(kv_own),
                whole(kv_other),
            ],
            out_specs=[
                pl.BlockSpec((TILE, WIDE), lambda i, ids: (i, 0)),
                pl.BlockSpec((8, TILE), lambda i, ids: (0, i)),
            ],
            scratch_shapes=[
                pltpu.VMEM((2 * rows // TILE, NARROW, TILE), BF),
                pltpu.VMEM((8, TILE), F32),
                pltpu.VMEM((8, TILE), F32),
                pltpu.VMEM((NARROW, TILE), F32),
            ],
        ),
        out_shape=[
            jax.ShapeDtypeStruct((rows, WIDE), BF),
            jax.ShapeDtypeStruct((8, rows), F32),
        ],
        name="attend",
    )(ids, row_ids, col_ids, queries, kv_own, kv_other)


def attend_back_kernel(
    ids_ref, row_ids_ref, col_ids_ref, q_ref, up_ref, out_ref, log_ref, own_ref, other_ref,
    cos_ref, sin_ref, dq_ref, own_grad_ref, other_grad_ref,
    k_turned, acc_ref, key_acc, value_acc,
):
    q_tile = pl.program_id(0)
    own_tiles = own_ref.shape[0] // TILE

    @pl.when(q_tile == 0)
    def _():
        for base, ref in ((0, own_ref), (own_tiles, other_ref)):
            for tile in range(own_tiles):
                k_turned[base + tile] = jnp.transpose(
                    ref[pl.ds(tile * TILE, TILE), :WIDE]
                )[:NARROW]
        key_acc[...] = jnp.zeros(key_acc.shape, F32)
        value_acc[...] = jnp.zeros(value_acc.shape, F32)

    queries = q_ref[...]
    upstream = up_ref[...]
    q_heads = [head_only(queries, head) for head in range(OWN_HEADS)]
    up_heads = [head_only(upstream, head) for head in range(OWN_HEADS)]
    products = upstream.astype(F32) * out_ref[...].astype(F32)
    lane_head = lax.broadcasted_iota(jnp.int32, (8, WIDE), 1) // HEAD_DIM
    selector = (lane_head == lax.broadcasted_iota(jnp.int32, (8, WIDE), 0)).astype(F32)
    deltas = lax.dot_general(
        selector, products, (((1,), (1,)), ((), ())),
        precision=lax.Precision.HIGHEST, preferred_element_type=F32,
    )
    q_ids = row_ids_ref[0]
    acc_ref[...] = jnp.zeros(acc_ref.shape, F32)

    for base, ref in ((0, own_ref), (own_tiles, other_ref)):

        def one_tile(tile, carry, base=base, ref=ref):
            @pl.when(share_document(ids_ref, q_tile, base + tile))
            def _():
                start = pl.multiple_of(tile * TILE, TILE)
                place = pl.ds(pl.multiple_of((base + tile) * TILE, TILE), TILE)
                keys = ref[pl.ds(start, TILE), :WIDE]
                values = ref[pl.ds(start, TILE), WIDE:]
                same = col_ids_ref[place, :] == q_ids
                for head in range(OWN_HEADS):
                    scores = contract(keys, q_heads[head], 1, 1) * SCORE_FACTOR
                    weights = jnp.where(
                        same, jnp.exp2(scores - log_ref[head : head + 1, :]), 0.0
                    )
                    grad_weights = contract(values, up_heads[head], 1, 1)
                    grad_scores = (
                        weights * (grad_weights - deltas[head : head + 1, :])
                    ).astype(BF)
                    value_acc[place, :] += jnp.dot(
                        weights.astype(BF), up_heads[head], preferred_element_type=F32
                    )
                    key_acc[place, :] += jnp.dot(
                        grad_scores, q_heads[head], preferred_element_type=F32
                    )
                    rows = slice(head * HEAD_DIM, (head + 1) * HEAD_DIM)
                    acc_ref[rows, :] += jnp.dot(
                        k_turned[base + tile, rows, :], grad_scores, preferred_element_type=F32
                    )

            return carry

        lax.fori_loop(0, own_tiles, one_tile, 0)

    factor = HEAD_DIM ** (-0.5)
    grad_query = jnp.transpose(
        jnp.concatenate([acc_ref[...], jnp.zeros((WIDE - NARROW, TILE), F32)], axis=0)
    )
    grad_query = grad_query * factor
    dq_ref[...] = (
        grad_query * doubled(cos_ref[...]) - turned(grad_query) * doubled(sin_ref[...])
    ).astype(BF)

    @pl.when(q_tile == pl.num_programs(0) - 1)
    def _():
        rows = own_grad_ref.shape[0]
        own_grad_ref[:, :WIDE] = key_acc[:rows, :] * factor
        own_grad_ref[:, WIDE:] = value_acc[:rows, :]
        other_grad_ref[:, :WIDE] = (key_acc[rows:, :] * factor).astype(BF)
        other_grad_ref[:, WIDE:] = value_acc[rows:, :].astype(BF)


def attend_back(
    ids, row_ids, col_ids, queries, upstream, attended, logs, kv_own, kv_other, cosine, sine
):
    rows = queries.shape[0]
    whole = lambda array: pl.BlockSpec(array.shape, lambda i, ids: (0,) * array.ndim)
    tiled = lambda width: pl.BlockSpec((TILE, width), lambda i, ids: (i, 0))
    return pl.pallas_call(
        attend_back_kernel,
        grid_spec=pltpu.PrefetchScalarGridSpec(
            num_scalar_prefetch=1,
            grid=(rows // TILE,),
            in_specs=[
                pl.BlockSpec((1, 1, TILE), lambda i, ids: (i, 0, 0)),
                whole(col_ids),
                tiled(WIDE),
                tiled(WIDE),
                tiled(WIDE),
                pl.BlockSpec((8, TILE), lambda i, ids: (0, i)),
                whole(kv_own),
                whole(kv_other),
                tiled(128),
                tiled(128),
            ],
            out_specs=[
                tiled(WIDE),
                pl.BlockSpec((rows, 2 * WIDE), lambda i, ids: (0, 0)),
                pl.BlockSpec((rows, 2 * WIDE), lambda i, ids: (0, 0)),
            ],
            scratch_shapes=[
                pltpu.VMEM((2 * rows // TILE, NARROW, TILE), BF),
                pltpu.VMEM((NARROW, TILE), F32),
                pltpu.VMEM((2 * rows, WIDE), F32),
                pltpu.VMEM((2 * rows, WIDE), F32),
            ],
        ),
        out_shape=[
            jax.ShapeDtypeStruct((rows, WIDE), BF),
            jax.ShapeDtypeStruct((rows, 2 * WIDE), F32),
            jax.ShapeDtypeStruct((rows, 2 * WIDE), BF),
        ],
        name="attend_back",
    )(ids, row_ids, col_ids, queries, upstream, attended, logs, kv_own, kv_other, cosine, sine)


def join_grads_kernel(dq_ref, own_ref, got_ref, cos_ref, sin_ref, out_ref):
    out_ref[:, :WIDE] = dq_ref[...]
    total = own_ref[...] + got_ref[...].astype(F32)
    keys = total[:, :WIDE]
    out_ref[:, WIDE : 2 * WIDE] = (
        keys * doubled(cos_ref[...]) - turned(keys) * doubled(sin_ref[...])
    ).astype(BF)
    out_ref[:, 2 * WIDE :] = total[:, WIDE:].astype(BF)


def join_grads(grad_queries, own, got, cosine, sine):
    rows = grad_queries.shape[0]
    tiled = lambda width: pl.BlockSpec((TILE, width), lambda i: (i, 0))
    return pl.pallas_call(
        join_grads_kernel,
        grid=(rows // TILE,),
        in_specs=[tiled(WIDE), tiled(2 * WIDE), tiled(2 * WIDE), tiled(128), tiled(128)],
        out_specs=tiled(3 * WIDE),
        out_shape=jax.ShapeDtypeStruct((rows, 3 * WIDE), BF),
        name="join_grads",
    )(grad_queries, own, got, cosine, sine)


def gather_square(block):
    return [block] + [send(block, SQUARE[k]) for k in range(1, GROUP)]


def reduce_square(left, weight, weight_dim):
    got = []
    for k in (3, 1, 2):
        part = contract(left[k * TILE : (k + 1) * TILE], weight, 1, weight_dim)
        got.append(send(part.astype(BF), SQUARE[k]))
    total = contract(left[:TILE], weight, 1, weight_dim)
    for part in got:
        total = total + part.astype(F32)
    return total


def per_device_clustered(
    tokens_in,
    segment_ids,
    w_qkv,
    w_out,
    ln1_gain,
    ln1_bias,
    w_gate,
    w_up,
    w_down,
    ln2_gain,
    ln2_bias,
    out_cotangent,
):
    rep = lax.axis_index("rep")
    shard = lax.axis_index("shard")
    x, c = rep // 2, rep % 2
    h, j = shard // 4, shard % 4
    core_is_one = c == 1
    half_is_one = h == 1
    x_is_one = x == 1
    at_home = c == h
    token_count = tokens_in.shape[1]
    length = segment_ids.shape[1]
    rows_d = w_qkv.shape[0]
    rows_f = w_down.shape[0]
    slice_f = 2 * rows_f
    group_rows = GROUP * token_count

    inputs_bf = send(tokens_in.reshape(token_count, D), SPREAD)
    doc_ids = send(segment_ids, SPREAD).reshape(2, GROUP, token_count)

    def by_target(rows_of_targets):
        return [lax.dynamic_index_in_dim(rows_of_targets, j ^ k, 0, False) for k in range(GROUP)]

    def fetch_columns(targets):
        mine = [send(part, ROUND[k]) for k, part in enumerate(by_target(targets))]
        mine = jnp.stack(mine)
        other = send(mine, OTHER_CORE)
        away = c != h
        low = pick(away, mine, other)
        high = pick(away, other, mine)
        return jnp.concatenate([jnp.stack(unmix(low, j)), jnp.stack(unmix(high, j))], axis=0)

    vectors = jnp.stack([ln1_gain, ln1_bias, ln2_gain, ln2_bias], axis=1)
    qkv_targets = jnp.transpose(w_qkv.reshape(rows_d, 3, GROUP, NARROW), (2, 0, 1, 3)).reshape(
        GROUP, rows_d, 3 * NARROW
    )
    qkv_targets = jnp.concatenate(
        [qkv_targets, jnp.broadcast_to(vectors[None], (GROUP, rows_d, 4))], axis=2
    )
    qkv_got = fetch_columns(qkv_targets)
    vectors_full = jnp.transpose(qkv_got[:, :, 3 * NARROW :].reshape(D, 4)).astype(F32)
    gain_one, bias_one, gain_two, bias_two = (vectors_full[i] for i in range(4))
    qkv_own = jnp.pad(
        qkv_got[:, :, : 3 * NARROW].reshape(D, 3, NARROW), ((0, 0), (0, 0), (0, WIDE - NARROW))
    ).reshape(D, 3 * WIDE)

    out_got = send(w_out, OUT_FETCH)
    out_other = send(out_got, OTHER_CORE)
    out_own = jnp.concatenate(
        [
            pick(core_is_one, out_got, out_other),
            pick(core_is_one, out_other, out_got),
            jnp.zeros((WIDE - NARROW, D), BF),
        ],
        axis=0,
    )

    half_f = rows_f // 2
    down_mine = send(lax.dynamic_slice_in_dim(w_down, c * half_f, half_f, 0), OTHER_HALF)
    down_other = send(down_mine, OTHER_CORE)
    down_far = jnp.concatenate(
        [pick(core_is_one, down_mine, down_other), pick(core_is_one, down_other, down_mine)], axis=0
    )
    down_own = jnp.concatenate(
        [pick(half_is_one, w_down, down_far), pick(half_is_one, down_far, w_down)], axis=0
    )

    def column_targets(weight):
        return jnp.transpose(weight.reshape(rows_d, 2, GROUP, rows_f), (2, 0, 1, 3)).reshape(
            GROUP, rows_d, slice_f
        )

    gate_up_got = fetch_columns(
        jnp.concatenate([column_targets(w_gate), column_targets(w_up)], axis=2)
    )
    gate_up_own = gate_up_got.reshape(D, 2 * slice_f)

    tile_index = j ^ jnp.arange(GROUP, dtype=jnp.int32)
    first_row = (c * GROUP + tile_index) * token_count
    positions = (
        first_row[:, None] + jnp.arange(token_count, dtype=jnp.int32)[None, :]
    ).reshape(group_rows).astype(F32)
    middle = HEAD_DIM // 2
    exponents = jnp.arange(128, dtype=jnp.int32) % middle
    inverse = rope_base ** (-(2.0 * exponents.astype(F32)) / HEAD_DIM)
    angles = positions[:, None] * inverse[None, :]
    cosine, sine = jnp.cos(angles), jnp.sin(angles)
    mixed = jnp.stack(unmix([doc_ids[:, k] for k in range(GROUP)], j), axis=1)
    ids = jnp.concatenate(
        [pick(core_is_one, mixed[0], mixed[1]), pick(core_is_one, mixed[1], mixed[0])], axis=0
    )
    flat_ids = ids.reshape(length)
    row_ids = ids.reshape(length // TILE, 1, TILE)
    col_ids = flat_ids[:, None]

    x_rows = jnp.concatenate(gather_square(inputs_bf), axis=0)
    queries, kv_own = project(x_rows, qkv_own, cosine, sine)
    kv_other = send(kv_own, OTHER_CORE)
    attended, logs = attend(flat_ids, row_ids, col_ids, queries, kv_own, kv_other)
    branch = reduce_square(attended, out_own, 0)
    first_out, first_normed, first_scale = norm_forward(
        inputs_bf.astype(F32) + branch, gain_one, bias_one
    )

    first_rows = jnp.concatenate(gather_square(first_out.astype(BF)), axis=0)
    acts = contract(first_rows, gate_up_own, 1, 0)
    gate_act, up_act = acts[:, :slice_f], acts[:, slice_f:]
    hidden_bf = (jax.nn.silu(gate_act) * up_act).astype(BF)
    down_act = reduce_square(hidden_bf, down_own, 0)
    result, second_normed, second_scale = norm_forward(first_out + down_act, gain_two, bias_two)
    result_home = send(result.astype(BF), SPREAD)

    upstream = send(out_cotangent.reshape(token_count, D), SPREAD).astype(F32)
    grad_gain_two = jnp.sum(upstream * second_normed, axis=0)
    grad_bias_two = jnp.sum(upstream, axis=0)
    grad_second = norm_backward(upstream, second_normed, second_scale, gain_two)
    grad_down_rows = jnp.concatenate(gather_square(grad_second.astype(BF)), axis=0)
    grad_hidden = contract(grad_down_rows, down_own, 1, 1)
    sigmoid_gate = jax.nn.sigmoid(gate_act)
    grad_gate_bf = (
        grad_hidden * up_act * sigmoid_gate * (1.0 + gate_act * (1.0 - sigmoid_gate))
    ).astype(BF)
    grad_up_bf = (grad_hidden * (gate_act * sigmoid_gate)).astype(BF)
    grad_acts = jnp.concatenate([grad_gate_bf, grad_up_bf], axis=1)
    grad_first = grad_second + reduce_square(grad_acts, gate_up_own, 1)
    grad_gain_one = jnp.sum(grad_first * first_normed, axis=0)
    grad_bias_one = jnp.sum(grad_first, axis=0)
    grad_res = norm_backward(grad_first, first_normed, first_scale, gain_one)

    grad_branch_rows = jnp.concatenate(gather_square(grad_res.astype(BF)), axis=0)
    grad_attended = contract(grad_branch_rows, out_own, 1, 1).astype(BF)
    grad_queries, kv_grad_own, kv_grad_away = attend_back(
        flat_ids, row_ids, col_ids, queries, grad_attended, attended, logs, kv_own, kv_other,
        cosine, sine,
    )
    kv_grad_got = send(kv_grad_away, OTHER_CORE)
    grad_projected = join_grads(grad_queries, kv_grad_own, kv_grad_got, cosine, sine)
    grad_inputs = grad_res + reduce_square(grad_projected, qkv_own, 1)
    grad_inputs_home = send(grad_inputs.astype(BF), SPREAD).astype(F32)

    quarter = rows_d // 2

    def rows_for_home(partial):
        partial = partial.astype(BF)
        keep = pick(core_is_one, partial[0], partial[1]).astype(F32)
        away = pick(core_is_one, partial[1], partial[0])
        total = keep + send(away, OTHER_CORE).astype(F32)
        total = total.astype(BF).reshape(-1, 2, quarter, total.shape[-1])
        keep = pick(x_is_one, total[:, 0], total[:, 1]).astype(F32)
        away = pick(x_is_one, total[:, 1], total[:, 0])
        total = keep + send(away, OTHER_X).astype(F32)
        total_bf = total.astype(BF)
        return (total + send(total_bf, HOME_HALF).astype(F32)).astype(BF)

    def both_x(mine, axis):
        got = send(mine, HOME_X)
        return jnp.stack(
            [pick(x_is_one, mine, got), pick(x_is_one, got, mine)], axis=axis
        )

    def both_cores(mine):
        return pick(at_home, send(mine, HOME_CORE), mine).astype(F32)

    def to_row_owner(mine):
        parts = by_target(mine)
        return unmix([parts[0]] + [send(parts[k], HOME_SQUARE[k]) for k in range(1, GROUP)], j)

    grad_down_part = contract(hidden_bf, grad_down_rows, 0, 0).reshape(2, rows_f, D)
    down_mine = rows_for_home(grad_down_part)
    grad_w_down = both_cores(both_x(down_mine, 1)).reshape(rows_f, D)

    grad_gate_up_part = contract(first_rows, grad_acts, 0, 0).reshape(2, D // 2, 2 * slice_f)
    gate_up_mine = rows_for_home(grad_gate_up_part)
    gate_up_mine = jnp.stack(to_row_owner(gate_up_mine), axis=1)
    gate_up_all = both_cores(both_x(gate_up_mine, 0)).reshape(rows_d, GROUP, 2, 2, rows_f)
    gate_up_all = jnp.transpose(gate_up_all, (2, 0, 3, 1, 4)).reshape(2, rows_d, w_gate.shape[1])
    grad_w_gate, grad_w_up = gate_up_all[0], gate_up_all[1]

    grad_out_part = contract(attended, grad_branch_rows, 0, 0)[:NARROW].astype(BF)
    grad_out_part = grad_out_part.reshape(2, 2, quarter, D)
    keep = pick(core_is_one, grad_out_part[0], grad_out_part[1]).astype(F32)
    away = pick(core_is_one, grad_out_part[1], grad_out_part[0])
    out_total = (keep + send(away, OTHER_CORE).astype(F32)).astype(BF)
    keep = pick(x_is_one, out_total[0], out_total[1]).astype(F32)
    away = pick(x_is_one, out_total[1], out_total[0])
    out_total = (keep + send(away, OTHER_X).astype(F32)).astype(BF)
    out_total = (out_total.astype(F32) + send(out_total, OTHER_HALF).astype(F32)).astype(BF)
    out_mine = send(out_total, OUT_RETURN)
    out_got = send(out_mine, OTHER_X)
    grad_w_out = jnp.concatenate(
        [pick(x_is_one, out_mine, out_got), pick(x_is_one, out_got, out_mine)], axis=0
    ).astype(F32)

    grad_qkv_part = contract(x_rows, grad_projected, 0, 0).reshape(D, 3, WIDE)[:, :, :NARROW]
    vector_part = jnp.stack([grad_gain_one, grad_bias_one, grad_gain_two, grad_bias_two], axis=1)
    grad_qkv_part = jnp.concatenate([grad_qkv_part.reshape(D, 3 * NARROW), vector_part], axis=1)
    qkv_mine = rows_for_home(grad_qkv_part.reshape(2, D // 2, 3 * NARROW + 4))
    qkv_parts = to_row_owner(qkv_mine)
    vector_sum = sum(part[:, 3 * NARROW :].astype(F32) for part in qkv_parts)
    columns = jnp.stack([part[:, : 3 * NARROW] for part in qkv_parts], axis=1)
    columns = columns.reshape(quarter, GROUP, 3, NARROW)
    columns = jnp.transpose(columns, (0, 2, 1, 3)).reshape(quarter, 3 * D)
    qkv_all = jnp.concatenate([columns, vector_sum.astype(BF)], axis=1)
    qkv_all = both_cores(both_x(qkv_all, 0)).reshape(rows_d, 3 * D + 4)
    grad_w_qkv = qkv_all[:, : 3 * D]
    vector_grads = jnp.transpose(qkv_all[:, 3 * D :])

    return (
        result_home.reshape(tokens_in.shape),
        grad_inputs_home.reshape(tokens_in.shape),
        grad_w_qkv,
        grad_w_out,
        vector_grads[0],
        vector_grads[1],
        grad_w_gate,
        grad_w_up,
        grad_w_down,
        vector_grads[2],
        vector_grads[3],
    )


def solution(mesh):
    sizes = dict(mesh.shape)
    clustered = (sizes["rep"], sizes["shard"]) == (4, 8)
    plan = per_device_clustered if clustered else per_device
    return jax.shard_map(
        plan,
        mesh=mesh,
        in_specs=(
            P("rep", "shard", None),
            P("rep", None),
            P("shard", None),
            P("shard", None),
            P("shard"),
            P("shard"),
            P("shard", None),
            P("shard", None),
            P("shard", None),
            P("shard"),
            P("shard"),
            P("rep", "shard", None),
        ),
        out_specs=(
            P("rep", "shard", None),
            P("rep", "shard", None),
            P("shard", None),
            P("shard", None),
            P("shard"),
            P("shard"),
            P("shard", None),
            P("shard", None),
            P("shard", None),
            P("shard"),
            P("shard"),
        ),
        check_vma=False,
    )
```

```python
import math

import jax
import jax.numpy as jnp
from jax import lax
from jax.experimental import pallas as pl
from jax.experimental.pallas import tpu as pltpu
from jax.sharding import PartitionSpec as P

D = 768
HEAD_DIM = 64
HEADS = 12


epsilon = 1e-05
rope_base = 1000.0


def rope_tables(start, count):
    positions = (start + jnp.arange(count, dtype=jnp.int32)).astype(jnp.float32)
    middle = HEAD_DIM // 2
    inverse = rope_base ** (-(2.0 * jnp.arange(middle).astype(jnp.float32)) / HEAD_DIM)
    angles = positions[:, None] * inverse[None, :]
    return (jnp.cos(angles)[:, None, :], jnp.sin(angles)[:, None, :])


def rotate(values_in, cosine, sine):
    middle = values_in.shape[-1] // 2
    first_half = values_in[..., :middle]
    second_half = values_in[..., middle:]
    return jnp.concatenate(
        [first_half * cosine - second_half * sine, second_half * cosine + first_half * sine],
        axis=-1,
    )


def rotate_back(upstream, cosine, sine):
    middle = upstream.shape[-1] // 2
    first_half = upstream[..., :middle]
    second_half = upstream[..., middle:]
    return jnp.concatenate(
        [first_half * cosine + second_half * sine, second_half * cosine - first_half * sine],
        axis=-1,
    )


def norm_forward(values_in, gain_vec, shift_vec):
    centred = values_in - jnp.mean(values_in, axis=-1, keepdims=True)
    variance = jnp.mean(centred * centred, axis=-1, keepdims=True)
    inverse_scale = lax.rsqrt(variance + epsilon)
    normed = centred * inverse_scale
    return (normed * gain_vec + shift_vec, normed, inverse_scale)


def norm_backward(upstream, normed, inverse_scale, gain_vec):
    scaled = upstream * gain_vec
    return inverse_scale * (
        scaled
        - jnp.mean(scaled, axis=-1, keepdims=True)
        - normed * jnp.mean(scaled * normed, axis=-1, keepdims=True)
    )


def fetch_attention(w_qkv, w_out, ln1_gain, ln1_bias):
    return (
        lax.all_gather(w_qkv, "shard", axis=0, tiled=True),
        lax.all_gather(w_out, "shard", axis=0, tiled=True),
        lax.all_gather(ln1_gain, "shard", axis=0, tiled=True),
        lax.all_gather(ln1_bias, "shard", axis=0, tiled=True),
    )


def fetch_feedforward(w_gate, w_up, w_down, ln2_gain, ln2_bias):
    return (
        lax.all_gather(w_gate, "shard", axis=0, tiled=True),
        lax.all_gather(w_up, "shard", axis=0, tiled=True),
        lax.all_gather(w_down, "shard", axis=0, tiled=True),
        lax.all_gather(ln2_gain, "shard", axis=0, tiled=True),
        lax.all_gather(ln2_bias, "shard", axis=0, tiled=True),
    )


def pair_columns(matrix, pair_index):
    width = 2 * HEAD_DIM
    return lax.dynamic_slice_in_dim(matrix, pair_index * width, width, 1).reshape(
        matrix.shape[0], 2, HEAD_DIM
    )


def pair_scores(pair_index, queries, key_rows, same_doc):
    scores = jnp.einsum(
        "qhd,khd->hqk",
        pair_columns(queries, pair_index),
        pair_columns(key_rows, pair_index),
        preferred_element_type=jnp.float32,
    ) * HEAD_DIM ** (-0.5)
    return jnp.where(same_doc[None], scores, -jnp.inf)


def attention_forward(queries, key_rows, value_rows, same_doc):

    def one_pair(pair_index):
        scores = pair_scores(pair_index, queries, key_rows, same_doc)
        row_max = jnp.max(scores, axis=-1, keepdims=True)
        expons = jnp.exp(scores - row_max)
        row_total = jnp.sum(expons, axis=-1, keepdims=True)
        weights_bf = (expons / row_total).astype(jnp.bfloat16)
        attended = jnp.einsum(
            "hqk,khd->qhd",
            weights_bf,
            pair_columns(value_rows, pair_index),
            preferred_element_type=jnp.float32,
        )
        return (
            attended.reshape(attended.shape[0], 2 * HEAD_DIM),
            (row_max + jnp.log(row_total))[..., 0],
        )

    attended, log_totals = lax.map(one_pair, jnp.arange(HEADS // 2, dtype=jnp.int32))
    return (jnp.transpose(attended, (1, 0, 2)).reshape(queries.shape[0], D), log_totals)


def attention_backward(queries, key_rows, value_rows, grad_attended, log_totals, same_doc):
    scale_factor = HEAD_DIM ** (-0.5)
    width = 2 * HEAD_DIM

    def one_pair(inputs):
        pair_index, pair_logs = inputs
        scores = pair_scores(pair_index, queries, key_rows, same_doc)
        weights = jnp.exp(scores - pair_logs[..., None])
        grad_pair = pair_columns(grad_attended, pair_index)
        grad_weights = jnp.einsum(
            "qhd,khd->hqk",
            grad_pair,
            pair_columns(value_rows, pair_index),
            preferred_element_type=jnp.float32,
        )
        row_delta = jnp.sum(weights * grad_weights, axis=-1, keepdims=True)
        grad_scores = (weights * (grad_weights - row_delta)).astype(jnp.bfloat16)
        grad_query = (
            jnp.einsum(
                "hqk,khd->qhd",
                grad_scores,
                pair_columns(key_rows, pair_index),
                preferred_element_type=jnp.float32,
            )
            * scale_factor
        )
        grad_key = (
            jnp.einsum(
                "hqk,qhd->khd",
                grad_scores,
                pair_columns(queries, pair_index),
                preferred_element_type=jnp.float32,
            )
            * scale_factor
        )
        grad_value = jnp.einsum(
            "hqk,qhd->khd",
            weights.astype(jnp.bfloat16),
            grad_pair,
            preferred_element_type=jnp.float32,
        )
        return (
            grad_query.reshape(-1, width),
            grad_key.reshape(-1, width),
            grad_value.reshape(-1, width),
        )

    pair_grads = lax.map(one_pair, (jnp.arange(HEADS // 2, dtype=jnp.int32), log_totals))
    return tuple(
        (
            jnp.transpose(pair_part, (1, 0, 2)).reshape(pair_part.shape[1], D)
            for pair_part in pair_grads
        )
    )


def per_device(
    tokens_in,
    segment_ids,
    w_qkv,
    w_out,
    ln1_gain,
    ln1_bias,
    w_gate,
    w_up,
    w_down,
    ln2_gain,
    ln2_bias,
    out_cotangent,
):
    inputs_bf = tokens_in.reshape(-1, D)
    token_count = inputs_bf.shape[0]
    doc_ids = segment_ids.reshape(-1)
    start = lax.axis_index("shard") * token_count
    own_docs = lax.dynamic_slice_in_dim(doc_ids, start, token_count)
    same_doc = own_docs[:, None] == doc_ids[None, :]
    cosine, sine = rope_tables(start, token_count)
    heads_shape = (token_count, HEADS, HEAD_DIM)
    qkv_full, out_full, gain_one, bias_one = fetch_attention(w_qkv, w_out, ln1_gain, ln1_bias)
    projected = jnp.dot(inputs_bf, qkv_full, preferred_element_type=jnp.float32)
    queries = (
        rotate(projected[:, :D].reshape(heads_shape), cosine, sine)
        .reshape(token_count, D)
        .astype(jnp.bfloat16)
    )
    own_keys = (
        rotate(projected[:, D : 2 * D].reshape(heads_shape), cosine, sine)
        .reshape(token_count, D)
        .astype(jnp.bfloat16)
    )
    own_values = projected[:, 2 * D :].astype(jnp.bfloat16)
    key_rows, value_rows = (
        lax.all_gather(own_keys, "shard", axis=0, tiled=True),
        lax.all_gather(own_values, "shard", axis=0, tiled=True),
    )
    attended, log_totals = attention_forward(queries, key_rows, value_rows, same_doc)
    attended_bf = attended.astype(jnp.bfloat16)
    branch = jnp.dot(attended_bf, out_full, preferred_element_type=jnp.float32)
    inputs_f = inputs_bf.astype(jnp.float32)
    first_out, first_normed, first_scale = norm_forward(
        inputs_f + branch, gain_one.astype(jnp.float32), bias_one.astype(jnp.float32)
    )
    gate_full, up_full, down_full, gain_two, bias_two = fetch_feedforward(
        w_gate, w_up, w_down, ln2_gain, ln2_bias
    )
    first_bf = first_out.astype(jnp.bfloat16)
    gate_act = jnp.dot(first_bf, gate_full, preferred_element_type=jnp.float32)
    up_act = jnp.dot(first_bf, up_full, preferred_element_type=jnp.float32)
    hidden_bf = (jax.nn.silu(gate_act) * up_act).astype(jnp.bfloat16)
    down_act = jnp.dot(hidden_bf, down_full, preferred_element_type=jnp.float32)
    result, second_normed, second_scale = norm_forward(
        first_out + down_act, gain_two.astype(jnp.float32), bias_two.astype(jnp.float32)
    )
    gate_full, up_full, down_full, gain_two, bias_two = fetch_feedforward(
        w_gate, w_up, w_down, ln2_gain, ln2_bias
    )
    upstream = out_cotangent.reshape(-1, D).astype(jnp.float32)
    grad_gain_two = jnp.sum(upstream * second_normed, axis=0)
    grad_bias_two = jnp.sum(upstream, axis=0)
    grad_second = norm_backward(upstream, second_normed, second_scale, gain_two.astype(jnp.float32))
    grad_down_bf = grad_second.astype(jnp.bfloat16)
    grad_down_w = jnp.einsum(
        "tf,td->fd", hidden_bf, grad_down_bf, preferred_element_type=jnp.float32
    )
    grad_hidden = jnp.einsum(
        "td,fd->tf", grad_down_bf, down_full, preferred_element_type=jnp.float32
    )
    sigmoid_gate = jax.nn.sigmoid(gate_act)
    grad_gate_bf = (
        grad_hidden * up_act * sigmoid_gate * (1.0 + gate_act * (1.0 - sigmoid_gate))
    ).astype(jnp.bfloat16)
    grad_up_bf = (grad_hidden * jax.nn.silu(gate_act)).astype(jnp.bfloat16)
    grad_gate_w = jnp.einsum(
        "td,tf->df", first_bf, grad_gate_bf, preferred_element_type=jnp.float32
    )
    grad_up_w = jnp.einsum("td,tf->df", first_bf, grad_up_bf, preferred_element_type=jnp.float32)
    grad_first = grad_second + jnp.einsum(
        "tf,df->td", grad_gate_bf, gate_full, preferred_element_type=jnp.float32
    )
    grad_first = grad_first + jnp.einsum(
        "tf,df->td", grad_up_bf, up_full, preferred_element_type=jnp.float32
    )
    qkv_full, out_full, gain_one, bias_one = fetch_attention(w_qkv, w_out, ln1_gain, ln1_bias)
    grad_gain_one = jnp.sum(grad_first * first_normed, axis=0)
    grad_bias_one = jnp.sum(grad_first, axis=0)
    grad_res = norm_backward(grad_first, first_normed, first_scale, gain_one.astype(jnp.float32))
    grad_branch_bf = grad_res.astype(jnp.bfloat16)
    grad_out_w = jnp.einsum(
        "tc,td->cd", attended_bf, grad_branch_bf, preferred_element_type=jnp.float32
    )
    grad_attended_bf = jnp.einsum(
        "td,cd->tc", grad_branch_bf, out_full, preferred_element_type=jnp.float32
    ).astype(jnp.bfloat16)
    grad_queries, grad_keys_all, grad_values_all = attention_backward(
        queries, key_rows, value_rows, grad_attended_bf, log_totals, same_doc
    )
    grad_keys, grad_values = (
        lax.psum_scatter(
            grad_keys_all.astype(jnp.bfloat16), "shard", scatter_dimension=0, tiled=True
        ).astype(jnp.float32),
        lax.psum_scatter(
            grad_values_all.astype(jnp.bfloat16), "shard", scatter_dimension=0, tiled=True
        ).astype(jnp.float32),
    )
    grad_projected = jnp.concatenate(
        [
            rotate_back(grad_queries.reshape(heads_shape), cosine, sine).reshape(token_count, D),
            rotate_back(grad_keys.reshape(heads_shape), cosine, sine).reshape(token_count, D),
            grad_values,
        ],
        axis=1,
    ).astype(jnp.bfloat16)
    grad_qkv_w = jnp.einsum(
        "td,tn->dn", inputs_bf, grad_projected, preferred_element_type=jnp.float32
    )
    grad_inputs = grad_res + jnp.einsum(
        "tn,dn->td", grad_projected, qkv_full, preferred_element_type=jnp.float32
    )
    (
        sum_qkv,
        sum_out,
        sum_gain_one,
        sum_bias_one,
        sum_gate,
        sum_up,
        sum_down,
        sum_gain_two,
        sum_bias_two,
    ) = (
        lax.psum_scatter(
            grad_qkv_w.astype(jnp.bfloat16), "shard", scatter_dimension=0, tiled=True
        ).astype(jnp.float32),
        lax.psum_scatter(
            grad_out_w.astype(jnp.bfloat16), "shard", scatter_dimension=0, tiled=True
        ).astype(jnp.float32),
        lax.psum_scatter(
            grad_gain_one.astype(jnp.bfloat16), "shard", scatter_dimension=0, tiled=True
        ).astype(jnp.float32),
        lax.psum_scatter(
            grad_bias_one.astype(jnp.bfloat16), "shard", scatter_dimension=0, tiled=True
        ).astype(jnp.float32),
        lax.psum_scatter(
            grad_gate_w.astype(jnp.bfloat16), "shard", scatter_dimension=0, tiled=True
        ).astype(jnp.float32),
        lax.psum_scatter(
            grad_up_w.astype(jnp.bfloat16), "shard", scatter_dimension=0, tiled=True
        ).astype(jnp.float32),
        lax.psum_scatter(
            grad_down_w.astype(jnp.bfloat16), "shard", scatter_dimension=0, tiled=True
        ).astype(jnp.float32),
        lax.psum_scatter(
            grad_gain_two.astype(jnp.bfloat16), "shard", scatter_dimension=0, tiled=True
        ).astype(jnp.float32),
        lax.psum_scatter(
            grad_bias_two.astype(jnp.bfloat16), "shard", scatter_dimension=0, tiled=True
        ).astype(jnp.float32),
    )
    totals = (
        lax.psum(sum_qkv.astype(jnp.bfloat16), "rep").astype(jnp.float32),
        lax.psum(sum_out.astype(jnp.bfloat16), "rep").astype(jnp.float32),
        lax.psum(sum_gain_one.astype(jnp.bfloat16), "rep").astype(jnp.float32),
        lax.psum(sum_bias_one.astype(jnp.bfloat16), "rep").astype(jnp.float32),
        lax.psum(sum_gate.astype(jnp.bfloat16), "rep").astype(jnp.float32),
        lax.psum(sum_up.astype(jnp.bfloat16), "rep").astype(jnp.float32),
        lax.psum(sum_down.astype(jnp.bfloat16), "rep").astype(jnp.float32),
        lax.psum(sum_gain_two.astype(jnp.bfloat16), "rep").astype(jnp.float32),
        lax.psum(sum_bias_two.astype(jnp.bfloat16), "rep").astype(jnp.float32),
    )
    return (
        result.astype(jnp.bfloat16).reshape(tokens_in.shape),
        grad_inputs.reshape(tokens_in.shape),
        totals[0],
        totals[1],
        totals[2],
        totals[3],
        totals[4],
        totals[5],
        totals[6],
        totals[7],
        totals[8],
    )


BF = jnp.bfloat16
F32 = jnp.float32
AXES = ("rep", "shard")
TILE = 256
GROUP = 4
OWN_HEADS = 3
NARROW = OWN_HEADS * HEAD_DIM
WIDE = 256
LOG2E = 1.4426950408889634
SCORE_FACTOR = HEAD_DIM ** (-0.5) * LOG2E
MASKED = -1e30


def cost(flops, *arrays):
    moved = sum(math.prod(array.shape) * array.dtype.itemsize for array in arrays)
    return pl.CostEstimate(flops=flops, transcendentals=0, bytes_accessed=moved)


def moves(target):
    pairs = []
    for rep in range(4):
        for shard in range(8):
            goal = target(rep // 2, rep % 2, shard // 4, shard % 4)
            if goal is not None:
                x, c, h, j = goal
                pairs.append((rep * 8 + shard, (2 * x + c) * 8 + 4 * h + j))
    return pairs


SPREAD = moves(lambda x, c, h, j: (x, h, c, j))
OTHER_CORE = moves(lambda x, c, h, j: (x, 1 - c, h, j))
OTHER_X = moves(lambda x, c, h, j: (1 - x, c, h, j))
OTHER_HALF = moves(lambda x, c, h, j: (x, c, 1 - h, j))
SQUARE = [moves(lambda x, c, h, j, k=k: (x, c, h, j ^ k)) for k in range(GROUP)]
ROUND = [moves(lambda x, c, h, j, i=i: (x, c, h ^ c, j ^ (2 * x + i))) for i in range(2)]
OUT_FETCH = moves(lambda x, c, h, j: (x, j % 2, c, (4 * h + j) // 2))
OUT_RETURN = moves(lambda x, c, h, j: (x, h, (2 * j + c) // 4, (2 * j + c) % 4))
HOME_HALF = moves(lambda x, c, h, j: (x, c, 1 - h, j) if c != h else None)
HOME_SQUARE = [
    moves(lambda x, c, h, j, k=k: (x, c, h, j ^ k) if c == h else None) for k in range(GROUP)
]
HOME_X = moves(lambda x, c, h, j: (1 - x, c, h, j) if c == h else None)
HOME_CORE = moves(lambda x, c, h, j: (x, 1 - c, h, j) if c == h else None)


def send(value, pairs):
    return lax.ppermute(value, AXES, pairs)


def pick(flag, first, second):
    return jnp.where(flag, second, first)


def unmix(blocks, j):
    bit0 = (j % 2) == 1
    bit1 = (j // 2) == 1
    b = blocks
    b = [pick(bit0, b[0], b[1]), pick(bit0, b[1], b[0]), pick(bit0, b[2], b[3]), pick(bit0, b[3], b[2])]
    return [pick(bit1, b[0], b[2]), pick(bit1, b[1], b[3]), pick(bit1, b[2], b[0]), pick(bit1, b[3], b[1])]


def turned(values):
    lane = lax.broadcasted_iota(jnp.int32, values.shape, 1) % HEAD_DIM
    middle = HEAD_DIM // 2
    return jnp.where(
        lane < middle,
        -pltpu.roll(values, WIDE - middle, 1),
        pltpu.roll(values, middle, 1),
    )


def doubled(table):
    return jnp.concatenate([table, table], axis=1)


def project_kernel(x_ref, w_ref, cos_ref, sin_ref, q_ref, kv_ref):
    projected = jnp.dot(x_ref[...], w_ref[...], preferred_element_type=F32)
    cosine = doubled(cos_ref[...])
    sine = doubled(sin_ref[...])
    for index, ref in ((0, q_ref), (1, kv_ref)):
        part = projected[:, index * WIDE : (index + 1) * WIDE]
        ref[:, :WIDE] = (part * cosine + turned(part) * sine).astype(BF)
    kv_ref[:, WIDE:] = projected[:, 2 * WIDE :].astype(BF)


def project(x_rows, w_qkv, cosine, sine):
    rows = x_rows.shape[0]
    return pl.pallas_call(
        project_kernel,
        grid=(rows // TILE,),
        in_specs=[
            pl.BlockSpec((TILE, D), lambda i: (i, 0)),
            pl.BlockSpec((D, 3 * WIDE), lambda i: (0, 0)),
            pl.BlockSpec((TILE, 128), lambda i: (i, 0)),
            pl.BlockSpec((TILE, 128), lambda i: (i, 0)),
        ],
        out_specs=[
            pl.BlockSpec((TILE, WIDE), lambda i: (i, 0)),
            pl.BlockSpec((TILE, 2 * WIDE), lambda i: (i, 0)),
        ],
        out_shape=[
            jax.ShapeDtypeStruct((rows, WIDE), BF),
            jax.ShapeDtypeStruct((rows, 2 * WIDE), BF),
        ],
        cost_estimate=cost(2 * rows * w_qkv.size, x_rows, w_qkv, x_rows, cosine, sine),
        name="project",
    )(x_rows, w_qkv, cosine, sine)


def head_only(values, head):
    lane = lax.broadcasted_iota(jnp.int32, values.shape, 1) // HEAD_DIM
    return jnp.where(lane == head, values, jnp.zeros_like(values))


def share_document(ids_ref, q_tile, kv_tile):
    q_first = ids_ref[q_tile * TILE]
    q_last = ids_ref[q_tile * TILE + TILE - 1]
    k_first = ids_ref[kv_tile * TILE]
    k_last = ids_ref[kv_tile * TILE + TILE - 1]
    return jnp.logical_and(k_first <= q_last, q_first <= k_last)


def contract(left, right, left_dim, right_dim):
    return lax.dot_general(
        left, right, (((left_dim,), (right_dim,)), ((), ())), preferred_element_type=F32
    )


def attend_kernel(
    ids_ref, row_ids_ref, col_ids_ref, q_ref, own_ref, other_ref, out_ref, log_ref,
    v_turned, max_ref, total_ref, acc_ref,
):
    q_tile = pl.program_id(0)
    own_tiles = own_ref.shape[0] // TILE

    @pl.when(q_tile == 0)
    def _():
        for base, ref in ((0, own_ref), (own_tiles, other_ref)):
            for tile in range(own_tiles):
                v_turned[base + tile] = jnp.transpose(
                    ref[pl.ds(tile * TILE, TILE), WIDE:]
                )[:NARROW]

    queries = q_ref[...]
    per_head = [head_only(queries, head) for head in range(OWN_HEADS)]
    q_ids = row_ids_ref[0]
    max_ref[...] = jnp.full(max_ref.shape, MASKED, F32)
    total_ref[...] = jnp.zeros(total_ref.shape, F32)
    acc_ref[...] = jnp.zeros(acc_ref.shape, F32)

    for base, ref in ((0, own_ref), (own_tiles, other_ref)):

        def one_tile(tile, carry, base=base, ref=ref):
            @pl.when(share_document(ids_ref, q_tile, base + tile))
            def _():
                start = pl.multiple_of(tile * TILE, TILE)
                keys = ref[pl.ds(start, TILE), :WIDE]
                same = (
                    col_ids_ref[pl.ds(pl.multiple_of((base + tile) * TILE, TILE), TILE), :] == q_ids
                )
                for head in range(OWN_HEADS):
                    scores = contract(keys, per_head[head], 1, 1) * SCORE_FACTOR
                    scores = jnp.where(same, scores, MASKED)
                    old_max = max_ref[head : head + 1, :]
                    new_max = jnp.maximum(old_max, jnp.max(scores, axis=0, keepdims=True))
                    shrink = jnp.exp2(old_max - new_max)
                    expons = jnp.exp2(scores - new_max)
                    max_ref[head : head + 1, :] = new_max
                    total_ref[head : head + 1, :] = total_ref[
                        head : head + 1, :
                    ] * shrink + jnp.sum(expons, axis=0, keepdims=True)
                    rows = slice(head * HEAD_DIM, (head + 1) * HEAD_DIM)
                    acc_ref[rows, :] = acc_ref[rows, :] * shrink + jnp.dot(
                        v_turned[base + tile, rows, :],
                        expons.astype(BF),
                        preferred_element_type=F32,
                    )

            return carry

        lax.fori_loop(0, own_tiles, one_tile, 0)

    parts = []
    for head in range(OWN_HEADS):
        rows = slice(head * HEAD_DIM, (head + 1) * HEAD_DIM)
        parts.append(acc_ref[rows, :] / total_ref[head : head + 1, :])
    parts.append(jnp.zeros((WIDE - NARROW, TILE), F32))
    out_ref[...] = jnp.transpose(jnp.concatenate(parts, axis=0)).astype(BF)
    row = lax.broadcasted_iota(jnp.int32, log_ref.shape, 0)
    log_ref[...] = jnp.where(
        row < OWN_HEADS,
        max_ref[...] + jnp.log2(jnp.where(row < OWN_HEADS, total_ref[...], 1.0)),
        0.0,
    )


def attend(ids, row_ids, col_ids, queries, kv_own, kv_other):
    rows = queries.shape[0]
    whole = lambda array: pl.BlockSpec(array.shape, lambda i, ids: (0,) * array.ndim)
    return pl.pallas_call(
        attend_kernel,
        grid_spec=pltpu.PrefetchScalarGridSpec(
            num_scalar_prefetch=1,
            grid=(rows // TILE,),
            in_specs=[
                pl.BlockSpec((1, 1, TILE), lambda i, ids: (i, 0, 0)),
                whole(col_ids),
                pl.BlockSpec((TILE, WIDE), lambda i, ids: (i, 0)),
                whole(kv_own),
                whole(kv_other),
            ],
            out_specs=[
                pl.BlockSpec((TILE, WIDE), lambda i, ids: (i, 0)),
                pl.BlockSpec((8, TILE), lambda i, ids: (0, i)),
            ],
            scratch_shapes=[
                pltpu.VMEM((2 * rows // TILE, NARROW, TILE), BF),
                pltpu.VMEM((8, TILE), F32),
                pltpu.VMEM((8, TILE), F32),
                pltpu.VMEM((NARROW, TILE), F32),
            ],
        ),
        out_shape=[
            jax.ShapeDtypeStruct((rows, WIDE), BF),
            jax.ShapeDtypeStruct((8, rows), F32),
        ],
        cost_estimate=cost(
            4 * OWN_HEADS * WIDE * rows * 2 * rows, queries, kv_own, kv_other, queries
        ),
        name="attend",
    )(ids, row_ids, col_ids, queries, kv_own, kv_other)


def attend_back_kernel(
    ids_ref, row_ids_ref, col_ids_ref, q_ref, up_ref, out_ref, log_ref, own_ref, other_ref,
    cos_ref, sin_ref, dq_ref, own_grad_ref, other_grad_ref,
    k_turned, acc_ref, key_acc, value_acc,
):
    q_tile = pl.program_id(0)
    own_tiles = own_ref.shape[0] // TILE

    @pl.when(q_tile == 0)
    def _():
        for base, ref in ((0, own_ref), (own_tiles, other_ref)):
            for tile in range(own_tiles):
                k_turned[base + tile] = jnp.transpose(
                    ref[pl.ds(tile * TILE, TILE), :WIDE]
                )[:NARROW]
        key_acc[...] = jnp.zeros(key_acc.shape, F32)
        value_acc[...] = jnp.zeros(value_acc.shape, F32)

    queries = q_ref[...]
    upstream = up_ref[...]
    q_heads = [head_only(queries, head) for head in range(OWN_HEADS)]
    up_heads = [head_only(upstream, head) for head in range(OWN_HEADS)]
    products = upstream.astype(F32) * out_ref[...].astype(F32)
    lane_head = lax.broadcasted_iota(jnp.int32, (8, WIDE), 1) // HEAD_DIM
    selector = (lane_head == lax.broadcasted_iota(jnp.int32, (8, WIDE), 0)).astype(F32)
    deltas = lax.dot_general(
        selector, products, (((1,), (1,)), ((), ())),
        precision=lax.Precision.HIGHEST, preferred_element_type=F32,
    )
    q_ids = row_ids_ref[0]
    acc_ref[...] = jnp.zeros(acc_ref.shape, F32)

    for base, ref in ((0, own_ref), (own_tiles, other_ref)):

        def one_tile(tile, carry, base=base, ref=ref):
            @pl.when(share_document(ids_ref, q_tile, base + tile))
            def _():
                start = pl.multiple_of(tile * TILE, TILE)
                place = pl.ds(pl.multiple_of((base + tile) * TILE, TILE), TILE)
                keys = ref[pl.ds(start, TILE), :WIDE]
                values = ref[pl.ds(start, TILE), WIDE:]
                same = col_ids_ref[place, :] == q_ids
                for head in range(OWN_HEADS):
                    scores = contract(keys, q_heads[head], 1, 1) * SCORE_FACTOR
                    weights = jnp.where(
                        same, jnp.exp2(scores - log_ref[head : head + 1, :]), 0.0
                    )
                    grad_weights = contract(values, up_heads[head], 1, 1)
                    grad_scores = (
                        weights * (grad_weights - deltas[head : head + 1, :])
                    ).astype(BF)
                    value_acc[place, :] += jnp.dot(
                        weights.astype(BF), up_heads[head], preferred_element_type=F32
                    )
                    key_acc[place, :] += jnp.dot(
                        grad_scores, q_heads[head], preferred_element_type=F32
                    )
                    rows = slice(head * HEAD_DIM, (head + 1) * HEAD_DIM)
                    acc_ref[rows, :] += jnp.dot(
                        k_turned[base + tile, rows, :], grad_scores, preferred_element_type=F32
                    )

            return carry

        lax.fori_loop(0, own_tiles, one_tile, 0)

    factor = HEAD_DIM ** (-0.5)
    grad_query = jnp.transpose(
        jnp.concatenate([acc_ref[...], jnp.zeros((WIDE - NARROW, TILE), F32)], axis=0)
    )
    grad_query = grad_query * factor
    dq_ref[...] = (
        grad_query * doubled(cos_ref[...]) - turned(grad_query) * doubled(sin_ref[...])
    ).astype(BF)

    @pl.when(q_tile == pl.num_programs(0) - 1)
    def _():
        rows = own_grad_ref.shape[0]
        own_grad_ref[:, :WIDE] = key_acc[:rows, :] * factor
        own_grad_ref[:, WIDE:] = value_acc[:rows, :]
        other_grad_ref[:, :WIDE] = (key_acc[rows:, :] * factor).astype(BF)
        other_grad_ref[:, WIDE:] = value_acc[rows:, :].astype(BF)


def attend_back(
    ids, row_ids, col_ids, queries, upstream, attended, logs, kv_own, kv_other, cosine, sine
):
    rows = queries.shape[0]
    whole = lambda array: pl.BlockSpec(array.shape, lambda i, ids: (0,) * array.ndim)
    tiled = lambda width: pl.BlockSpec((TILE, width), lambda i, ids: (i, 0))
    return pl.pallas_call(
        attend_back_kernel,
        grid_spec=pltpu.PrefetchScalarGridSpec(
            num_scalar_prefetch=1,
            grid=(rows // TILE,),
            in_specs=[
                pl.BlockSpec((1, 1, TILE), lambda i, ids: (i, 0, 0)),
                whole(col_ids),
                tiled(WIDE),
                tiled(WIDE),
                tiled(WIDE),
                pl.BlockSpec((8, TILE), lambda i, ids: (0, i)),
                whole(kv_own),
                whole(kv_other),
                tiled(128),
                tiled(128),
            ],
            out_specs=[
                tiled(WIDE),
                pl.BlockSpec((rows, 2 * WIDE), lambda i, ids: (0, 0)),
                pl.BlockSpec((rows, 2 * WIDE), lambda i, ids: (0, 0)),
            ],
            scratch_shapes=[
                pltpu.VMEM((2 * rows // TILE, NARROW, TILE), BF),
                pltpu.VMEM((NARROW, TILE), F32),
                pltpu.VMEM((2 * rows, WIDE), F32),
                pltpu.VMEM((2 * rows, WIDE), F32),
            ],
        ),
        out_shape=[
            jax.ShapeDtypeStruct((rows, WIDE), BF),
            jax.ShapeDtypeStruct((rows, 2 * WIDE), F32),
            jax.ShapeDtypeStruct((rows, 2 * WIDE), BF),
        ],
        cost_estimate=cost(
            10 * OWN_HEADS * WIDE * rows * 2 * rows, queries, kv_own, kv_other, queries
        ),
        name="attend_back",
    )(ids, row_ids, col_ids, queries, upstream, attended, logs, kv_own, kv_other, cosine, sine)


def join_grads_kernel(dq_ref, own_ref, got_ref, cos_ref, sin_ref, out_ref):
    out_ref[:, :WIDE] = dq_ref[...]
    total = own_ref[...] + got_ref[...].astype(F32)
    keys = total[:, :WIDE]
    out_ref[:, WIDE : 2 * WIDE] = (
        keys * doubled(cos_ref[...]) - turned(keys) * doubled(sin_ref[...])
    ).astype(BF)
    out_ref[:, 2 * WIDE :] = total[:, WIDE:].astype(BF)


def join_grads(grad_queries, own, got, cosine, sine):
    rows = grad_queries.shape[0]
    tiled = lambda width: pl.BlockSpec((TILE, width), lambda i: (i, 0))
    return pl.pallas_call(
        join_grads_kernel,
        grid=(rows // TILE,),
        in_specs=[tiled(WIDE), tiled(2 * WIDE), tiled(2 * WIDE), tiled(128), tiled(128)],
        out_specs=tiled(3 * WIDE),
        out_shape=jax.ShapeDtypeStruct((rows, 3 * WIDE), BF),
        cost_estimate=cost(8 * own.size, own, own, got, grad_queries),
        name="join_grads",
    )(grad_queries, own, got, cosine, sine)


def after(value, *others):
    return lax.optimization_barrier((value,) + others)[0]


def join(*values):
    return lax.optimization_barrier(values)


def pack_qkv_kernel(target_ref, w_ref, vectors_ref, *refs):
    packed = refs[-1]
    for target in range(GROUP):
        for part in range(3):
            start = part * D + target * NARROW
            packed[target, :, part * NARROW : (part + 1) * NARROW] = w_ref[
                :, start : start + NARROW
            ]
        packed[target, :, 3 * NARROW :] = vectors_ref[...]
    for index, ref in enumerate(refs[:-1]):
        ref[...] = packed[target_ref[index]]


def pack_qkv(targets, w_qkv, vectors):
    rows = w_qkv.shape[0]
    width = 3 * NARROW + vectors.shape[1]
    return pl.pallas_call(
        pack_qkv_kernel,
        in_specs=[
            pl.BlockSpec(memory_space=pltpu.SMEM),
            pl.BlockSpec(memory_space=pltpu.VMEM),
            pl.BlockSpec(memory_space=pltpu.VMEM),
        ],
        out_specs=[pl.BlockSpec(memory_space=pltpu.VMEM)] * 2,
        out_shape=[jax.ShapeDtypeStruct((rows, width), BF)] * 2,
        scratch_shapes=[pltpu.VMEM((GROUP, rows, width), BF)],
        name="pack_qkv",
    )(targets, w_qkv, vectors)


def pack_gate_up_kernel(target_ref, gate_ref, up_ref, *refs):
    packed = refs[-1]
    width = packed.shape[2] // 4
    for target in range(GROUP):
        for index in range(4):
            source = (gate_ref, up_ref)[index // 2]
            start = (index % 2 * GROUP + target) * width
            packed[target, :, index * width : (index + 1) * width] = source[
                :, start : start + width
            ]
    for index, ref in enumerate(refs[:-1]):
        ref[...] = packed[target_ref[index]]


def pack_gate_up(targets, w_gate, w_up):
    rows = w_gate.shape[0]
    width = 2 * w_gate.shape[1] // GROUP
    return pl.pallas_call(
        pack_gate_up_kernel,
        in_specs=[
            pl.BlockSpec(memory_space=pltpu.SMEM),
            pl.BlockSpec(memory_space=pltpu.VMEM),
            pl.BlockSpec(memory_space=pltpu.VMEM),
        ],
        out_specs=[pl.BlockSpec(memory_space=pltpu.VMEM)] * 2,
        out_shape=[jax.ShapeDtypeStruct((rows, width), BF)] * 2,
        scratch_shapes=[pltpu.VMEM((GROUP, rows, width), BF)],
        name="pack_gate_up",
    )(targets, w_gate, w_up)


def unpack_qkv_kernel(place_ref, near_ref, far_ref, out_ref, vectors_ref):
    zeros = jnp.zeros((near_ref.shape[1], WIDE - NARROW), BF)
    for index in range(2 * GROUP):
        source = (near_ref, far_ref)[index // GROUP]
        place = place_ref[index]
        for part in range(3):
            out_ref[place, :, part * WIDE : part * WIDE + NARROW] = source[
                index % GROUP, :, part * NARROW : (part + 1) * NARROW
            ]
            out_ref[place, :, part * WIDE + NARROW : (part + 1) * WIDE] = zeros
        vectors_ref[place] = source[index % GROUP, :, 3 * NARROW :]


def unpack_qkv(places, near, far):
    _, rows, width = near.shape
    return pl.pallas_call(
        unpack_qkv_kernel,
        in_specs=[
            pl.BlockSpec(memory_space=pltpu.SMEM),
            pl.BlockSpec(memory_space=pltpu.VMEM),
            pl.BlockSpec(memory_space=pltpu.VMEM),
        ],
        out_specs=[pl.BlockSpec(memory_space=pltpu.VMEM)] * 2,
        out_shape=[
            jax.ShapeDtypeStruct((2 * GROUP, rows, 3 * WIDE), BF),
            jax.ShapeDtypeStruct((2 * GROUP, rows, width - 3 * NARROW), BF),
        ],
        name="unpack_qkv",
    )(places, near, far)


def unpack_kernel(place_ref, near_ref, far_ref, out_ref):
    first = pl.program_id(0) < GROUP
    out_ref[...] = jnp.where(first, near_ref[...], far_ref[...])


def unpack(places, near, far):
    count, rows, width = near.shape
    return pl.pallas_call(
        unpack_kernel,
        grid_spec=pltpu.PrefetchScalarGridSpec(
            num_scalar_prefetch=1,
            grid=(2 * count,),
            in_specs=[
                pl.BlockSpec((1, rows, width), lambda i, p: (jnp.minimum(i, count - 1), 0, 0)),
                pl.BlockSpec((1, rows, width), lambda i, p: (jnp.maximum(i - count, 0), 0, 0)),
            ],
            out_specs=pl.BlockSpec((1, rows, width), lambda i, p: (p[i], 0, 0)),
        ),
        out_shape=jax.ShapeDtypeStruct((2 * count, rows, width), BF),
        name="unpack",
    )(places, near, far)


def split_feed_kernel(x_ref, down_ref, down_got_ref, gate_up_ref, gate_up_got_ref, keep_ref, away_ref):
    mine = x_ref[0]
    width = down_ref.shape[-1]
    for block in range(GROUP):
        for side, ref in ((mine, keep_ref), (1 - mine, away_ref)):
            ref[block] = (
                down_ref[block, side] + down_got_ref[block, side].astype(F32)
            ).astype(BF)
            total = gate_up_ref[block, side] + gate_up_got_ref[block, side].astype(F32)
            ref[GROUP + block] = total[:, :width].astype(BF)
            ref[2 * GROUP + block] = total[:, width:].astype(BF)


def whole_call(kernel, name, shapes, scalars, *arrays):
    return pl.pallas_call(
        kernel,
        in_specs=[pl.BlockSpec(memory_space=pltpu.SMEM)]
        + [pl.BlockSpec(memory_space=pltpu.VMEM)] * len(arrays),
        out_specs=[pl.BlockSpec(memory_space=pltpu.VMEM)] * len(shapes),
        out_shape=[jax.ShapeDtypeStruct(shape, dtype) for shape, dtype in shapes],
        cost_estimate=cost(sum(a.size for a in arrays), *arrays, *arrays),
        name=name,
    )(scalars, *arrays)


def square_feed_kernel(index_ref, mine_ref, got_ref, kept_ref, *send_refs):
    for k in range(GROUP):
        target = index_ref[k]
        for part in range(2):
            slot = (part + 1) * GROUP + target
            block = mine_ref[slot] + got_ref[slot]
            if k == 0:
                kept_ref[GROUP + part] = block
            else:
                send_refs[k - 1][part] = block
        kept_ref[k] = mine_ref[k] + got_ref[k]


def join_feed_kernel(index_ref, kept_ref, *refs):
    out_ref = refs[-1]
    for k in range(GROUP):
        out_ref[k] = kept_ref[k]
        for part in range(2):
            slot = (part + 1) * GROUP + index_ref[k]
            out_ref[slot] = kept_ref[GROUP + part] if k == 0 else refs[k - 1][part]


def finish_feed_kernel(flag_ref, own_ref, other_ref, far_own_ref, far_other_ref, down_ref, gate_ref, up_ref):
    mine, at_home = flag_ref[0], flag_ref[1] == 1
    rows = own_ref.shape[1]
    half = own_ref.shape[2] // 2
    for slot in range(3 * GROUP):
        for near, far, side in ((own_ref, far_own_ref, mine), (other_ref, far_other_ref, 1 - mine)):
            block = jnp.where(at_home, near[slot], far[slot]).astype(F32)
            if slot < GROUP:
                down_ref[slot, side] = block
            else:
                ref = gate_ref if slot < 2 * GROUP else up_ref
                start = slot % GROUP * half
                width = GROUP * half
                ref[side, :, start : start + half] = block[:, :half]
                ref[side, :, width + start : width + start + half] = block[:, half:]


def split_cores_kernel(c_ref, part_ref, vectors_ref, away_ref):
    rows = part_ref.shape[1]
    away_ref[:rows] = part_ref[1 - c_ref[0]].astype(BF)
    away_ref[rows:] = jnp.zeros((16, part_ref.shape[2]), BF)
    away_ref[rows : rows + 8] = vectors_ref[...].astype(BF)


def split_x_kernel(flag_ref, part_ref, vectors_ref, got_ref, keep_ref, away_ref):
    core, mine = flag_ref[0], flag_ref[1]
    rows = part_ref.shape[1]
    step = rows // (2 * GROUP)
    for block in range(GROUP):
        for side, ref in ((mine, keep_ref), (1 - mine, away_ref)):
            place = pl.ds(pl.multiple_of((2 * block + side) * step, step), step)
            ref[block * step : (block + 1) * step] = (
                part_ref[core, place] + got_ref[place].astype(F32)
            ).astype(BF)
    for ref in (keep_ref, away_ref):
        ref[GROUP * step :] = got_ref[rows:]
        ref[GROUP * step : GROUP * step + 8] = (
            vectors_ref[...] + got_ref[rows : rows + 8].astype(F32)
        ).astype(BF)


def square_qkv_kernel(index_ref, mine_ref, got_ref, *refs):
    step = (mine_ref.shape[0] - 16) // GROUP
    vectors = mine_ref[GROUP * step :] + got_ref[GROUP * step :]
    for k in range(GROUP):
        place = pl.ds(pl.multiple_of(index_ref[k] * step, step), step)
        refs[k][:step] = mine_ref[place] + got_ref[place]
        refs[k][step:] = vectors


def join_qkv_kernel(index_ref, *refs):
    out_ref = refs[-1]
    step = refs[0].shape[0] - 16
    vectors = refs[0][step:].astype(F32)
    for k in range(GROUP):
        place = pl.ds(pl.multiple_of(index_ref[k] * step, step), step)
        out_ref[place] = refs[k][:step]
        if k:
            vectors += refs[k][step:].astype(F32)
    out_ref[GROUP * step :] = vectors.astype(BF)


def finish_qkv_kernel(flag_ref, own_ref, other_ref, far_own_ref, far_other_ref, out_ref, vectors_ref):
    mine, at_home = flag_ref[0], flag_ref[1] == 1
    step = (own_ref.shape[0] - 16) // GROUP
    for block in range(GROUP):
        rows = slice(block * step, (block + 1) * step)
        for near, far, side in ((own_ref, far_own_ref, mine), (other_ref, far_other_ref, 1 - mine)):
            values = jnp.where(at_home, near[rows], far[rows]).astype(F32)
            for part in range(3):
                start = part * D + block * NARROW
                out_ref[side, :, start : start + NARROW] = values[
                    :, part * WIDE : part * WIDE + NARROW
                ]
    rows = slice(GROUP * step, GROUP * step + 8)
    vectors_ref[...] = jnp.where(at_home, own_ref[rows], far_own_ref[rows]).astype(F32)


def gather_square(block):
    return [block] + [send(block, SQUARE[k]) for k in range(1, GROUP)]


def square_parts(left, weight, weight_dim):
    return [
        contract(left[k * TILE : (k + 1) * TILE], weight, 1, weight_dim).astype(BF)
        for k in range(1, GROUP)
    ]


def reduce_square(left, weight, weight_dim, parts=None):
    if parts is None:
        parts = square_parts(left, weight, weight_dim)
    got = [send(part, SQUARE[k + 1]) for k, part in enumerate(parts)]
    total = contract(left[:TILE], weight, 1, weight_dim)
    for part in got:
        total = total + part.astype(F32)
    return total


def per_device_clustered(
    tokens_in,
    segment_ids,
    w_qkv,
    w_out,
    ln1_gain,
    ln1_bias,
    w_gate,
    w_up,
    w_down,
    ln2_gain,
    ln2_bias,
    out_cotangent,
):
    rep = lax.axis_index("rep")
    shard = lax.axis_index("shard")
    x, c = rep // 2, rep % 2
    h, j = shard // 4, shard % 4
    core_is_one = c == 1
    half_is_one = h == 1
    x_is_one = x == 1
    at_home = c == h
    token_count = tokens_in.shape[1]
    length = segment_ids.shape[1]
    rows_d = w_qkv.shape[0]
    rows_f = w_down.shape[0]
    slice_f = 2 * rows_f
    group_rows = GROUP * token_count

    inputs_bf = send(tokens_in.reshape(token_count, D), SPREAD)
    doc_ids = send(segment_ids, SPREAD).reshape(2, GROUP, token_count)

    by_x = jnp.stack([2 * x, 2 * x + 1, 2 - 2 * x, 3 - 2 * x]) ^ j
    targets = by_x[:2]
    places = jnp.concatenate([GROUP * (h ^ c) + by_x, GROUP * (1 - (h ^ c)) + by_x])

    vectors = jnp.stack([ln1_gain, ln1_bias, ln2_gain, ln2_bias], axis=1)
    qkv_packed = pack_qkv(targets, w_qkv, vectors)
    qkv_mine = after(
        jnp.stack([send(part, ROUND[i]) for i, part in enumerate(qkv_packed)]), inputs_bf
    )
    x_tiles = gather_square(inputs_bf)
    qkv_near = jnp.concatenate([qkv_mine, send(qkv_mine, OTHER_X)], axis=0)
    qkv_far = send(qkv_near, OTHER_CORE)
    qkv_own, vectors_got = unpack_qkv(places, qkv_near, qkv_far)
    qkv_own = qkv_own.reshape(D, 3 * WIDE)
    x_rows = jnp.concatenate(x_tiles, axis=0)
    x_rows, qkv_own, vectors_got, w_out = join(x_rows, qkv_own, vectors_got, w_out)

    tile_index = j ^ jnp.arange(GROUP, dtype=jnp.int32)
    first_row = (c * GROUP + tile_index) * token_count
    positions = (
        first_row[:, None] + jnp.arange(token_count, dtype=jnp.int32)[None, :]
    ).reshape(group_rows).astype(F32)
    middle = HEAD_DIM // 2
    exponents = jnp.arange(128, dtype=jnp.int32) % middle
    inverse = rope_base ** (-(2.0 * exponents.astype(F32)) / HEAD_DIM)
    angles = positions[:, None] * inverse[None, :]
    cosine, sine = jnp.cos(angles), jnp.sin(angles)
    mixed = jnp.stack(unmix([doc_ids[:, k] for k in range(GROUP)], j), axis=1)
    ids = jnp.concatenate(
        [pick(core_is_one, mixed[0], mixed[1]), pick(core_is_one, mixed[1], mixed[0])], axis=0
    )
    flat_ids = ids.reshape(length)
    row_ids = ids.reshape(length // TILE, 1, TILE)
    col_ids = flat_ids[:, None]

    part_f = rows_f // 4
    gate_up_packed = pack_gate_up(targets, w_gate, w_up)
    down_sent = lax.dynamic_slice_in_dim(w_down, (2 * c + x) * part_f, part_f, 0)

    queries, kv_own = project(x_rows, qkv_own, cosine, sine)
    kv_other = send(kv_own, OTHER_CORE)
    kv_other, w_out, down_sent, *gate_up_packed = join(kv_other, w_out, down_sent, *gate_up_packed)
    attended, logs = attend(flat_ids, row_ids, col_ids, queries, kv_own, kv_other)
    out_got = send(w_out, OUT_FETCH)
    gate_up_first = [send(part, ROUND[i]) for i, part in enumerate(gate_up_packed)]
    down_mine = send(down_sent, OTHER_HALF)
    attended, logs, out_got, down_mine, *gate_up_first = join(
        attended, logs, out_got, down_mine, *gate_up_first
    )
    out_other = send(out_got, OTHER_CORE)
    out_own = jnp.concatenate(
        [
            pick(core_is_one, out_got, out_other),
            pick(core_is_one, out_other, out_got),
            jnp.zeros((WIDE - NARROW, D), BF),
        ],
        axis=0,
    )

    branch_parts = square_parts(attended, out_own, 0)
    gate_up_mine, down_mine, *branch_parts = join(
        jnp.stack(gate_up_first), down_mine, *branch_parts
    )
    gate_up_second = send(gate_up_mine, OTHER_X)
    down_got = send(down_mine, OTHER_X)
    branch = reduce_square(attended, out_own, 0, branch_parts)
    vectors_full = jnp.transpose(vectors_got.reshape(D, 4)).astype(F32)
    gain_one, bias_one, gain_two, bias_two = (vectors_full[i] for i in range(4))
    first_out, first_normed, first_scale = norm_forward(
        inputs_bf.astype(F32) + branch, gain_one, bias_one
    )
    first_bf, gate_up_second, down_got, out_cotangent = join(
        first_out.astype(BF), gate_up_second, down_got, out_cotangent
    )

    first_tiles = gather_square(first_bf)
    gate_up_near = jnp.concatenate([gate_up_mine, gate_up_second], axis=0)
    gate_up_far = send(gate_up_near, OTHER_CORE)
    gate_up_own = unpack(places, gate_up_near, gate_up_far).reshape(D, 2 * slice_f)
    down_pair = jnp.concatenate(
        [pick(x_is_one, down_mine, down_got), pick(x_is_one, down_got, down_mine)], axis=0
    )
    down_other = send(down_pair, OTHER_CORE)
    down_far = jnp.concatenate(
        [pick(core_is_one, down_pair, down_other), pick(core_is_one, down_other, down_pair)], axis=0
    )
    down_own = jnp.concatenate(
        [pick(half_is_one, w_down, down_far), pick(half_is_one, down_far, w_down)], axis=0
    )
    first_rows = jnp.concatenate(first_tiles, axis=0)
    acts = contract(first_rows, gate_up_own, 1, 0)
    gate_act, up_act = acts[:, :slice_f], acts[:, slice_f:]
    hidden_bf = (jax.nn.silu(gate_act) * up_act).astype(BF)
    cotangent = send(after(out_cotangent, hidden_bf).reshape(token_count, D), SPREAD)
    down_act = reduce_square(hidden_bf, down_own, 0)
    result, second_normed, second_scale = norm_forward(first_out + down_act, gain_two, bias_two)

    upstream = cotangent.astype(F32)
    grad_gain_two = jnp.sum(upstream * second_normed, axis=0, keepdims=True)
    grad_bias_two = jnp.sum(upstream, axis=0, keepdims=True)
    grad_second = norm_backward(upstream, second_normed, second_scale, gain_two)
    grad_down_rows = jnp.concatenate(gather_square(grad_second.astype(BF)), axis=0)
    grad_hidden = contract(grad_down_rows, down_own, 1, 1)
    sigmoid_gate = jax.nn.sigmoid(gate_act)
    grad_gate_bf = (
        grad_hidden * up_act * sigmoid_gate * (1.0 + gate_act * (1.0 - sigmoid_gate))
    ).astype(BF)
    grad_up_bf = (grad_hidden * (gate_act * sigmoid_gate)).astype(BF)
    grad_acts = jnp.concatenate([grad_gate_bf, grad_up_bf], axis=1)
    first_parts = square_parts(grad_acts, gate_up_own, 1)

    quarter = rows_d // 2
    step_square = jnp.arange(GROUP, dtype=jnp.int32) ^ j
    x_flag = x.reshape(1)
    home_flags = jnp.stack([x, at_home.astype(jnp.int32)])

    def over_cores(partial):
        keep = pick(core_is_one, partial[0], partial[1])
        away = pick(core_is_one, partial[1], partial[0])
        return keep, send(away.astype(BF), OTHER_CORE)

    by_x_rows = (GROUP, 2, quarter)
    gate_up_keep, gate_up_got = over_cores(
        contract(first_rows, after(grad_acts, *first_parts), 0, 0).reshape(
            2, D // 2, 2 * slice_f
        )
    )
    down_keep, down_got = over_cores(
        contract(hidden_bf, after(grad_down_rows, *first_parts), 0, 0).reshape(2, rows_f, D)
    )
    bundle_shape = ((3 * GROUP, quarter, D), BF)
    feed_keep, feed_away = whole_call(
        split_feed_kernel, "split_feed", [bundle_shape] * 2, x_flag,
        down_keep.reshape(by_x_rows + (D,)), down_got.reshape(by_x_rows + (D,)),
        gate_up_keep.reshape(by_x_rows + (2 * slice_f,)),
        gate_up_got.reshape(by_x_rows + (2 * slice_f,)),
    )
    grad_first = grad_second + reduce_square(grad_acts, gate_up_own, 1, first_parts)
    grad_first, feed_away = join(grad_first, feed_away)
    feed_got = send(feed_away, OTHER_X)
    grad_gain_one = jnp.sum(grad_first * first_normed, axis=0, keepdims=True)
    grad_bias_one = jnp.sum(grad_first, axis=0, keepdims=True)
    grad_res = norm_backward(grad_first, first_normed, first_scale, gain_one)

    grad_branch_rows = jnp.concatenate(gather_square(grad_res.astype(BF)), axis=0)
    grad_attended = contract(grad_branch_rows, out_own, 1, 1).astype(BF)
    out_keep, out_got = over_cores(
        contract(attended, grad_branch_rows, 0, 0)[:NARROW].reshape(2, rows_d, D)
    )
    grad_attended, feed_got, out_got = join(grad_attended, feed_got, out_got)
    feed_mine = feed_keep + feed_got
    out_total = (out_keep + out_got.astype(F32)).astype(BF)
    grad_attended, feed_mine, out_total, result_bf = join(
        grad_attended, feed_mine, out_total, result.astype(BF)
    )
    grad_queries, kv_grad_own, kv_grad_away = attend_back(
        flat_ids, row_ids, col_ids, queries, grad_attended, attended, logs, kv_own, kv_other,
        cosine, sine,
    )
    feed_home = send(feed_mine, HOME_HALF)
    out_far = send(out_total, OTHER_X)
    result_home = send(result_bf, SPREAD)
    grad_queries, kv_grad_own, kv_grad_away, feed_home, out_far, result_home = join(
        grad_queries, kv_grad_own, kv_grad_away, feed_home, out_far, result_home
    )
    kv_grad_got = send(kv_grad_away, OTHER_CORE)
    grad_projected = join_grads(grad_queries, kv_grad_own, kv_grad_got, cosine, sine)

    input_parts = square_parts(grad_projected, qkv_own, 1)
    grad_projected, x_rows, *input_parts = join(grad_projected, x_rows, *input_parts)
    qkv_part = contract(x_rows, grad_projected, 0, 0).reshape(2, D // 2, 3 * WIDE)
    vector_part = jnp.concatenate(
        [grad_gain_one, grad_bias_one, grad_gain_two, grad_bias_two]
        + [jnp.zeros((4, D), F32)], axis=0
    )
    moved_rows = D // 4 + 16
    (qkv_away,) = whole_call(
        split_cores_kernel, "split_cores", [((D // 2 + 16, 3 * WIDE), BF)], c.reshape(1),
        qkv_part, vector_part,
    )
    qkv_away, feed_mine, feed_home = join(qkv_away, feed_mine, feed_home)
    qkv_got = send(qkv_away, OTHER_CORE)
    feed_kept, *feed_sends = whole_call(
        square_feed_kernel, "square_feed",
        [((GROUP + 2, quarter, D), BF)] + [((2, quarter, D), BF)] * 3,
        step_square, feed_mine, feed_home,
    )
    qkv_got, *feed_sends = join(qkv_got, *feed_sends)
    feed_gots = [send(part, HOME_SQUARE[k + 1]) for k, part in enumerate(feed_sends)]
    qkv_keep, qkv_away = whole_call(
        split_x_kernel, "split_x", [((moved_rows, 3 * WIDE), BF)] * 2, jnp.stack([c, x]),
        qkv_part, vector_part, qkv_got,
    )
    qkv_away, *feed_gots = join(qkv_away, *feed_gots)
    qkv_got = send(qkv_away, OTHER_X)
    (feed_bundle,) = whole_call(
        join_feed_kernel, "join_feed", [bundle_shape], step_square, feed_kept, *feed_gots
    )
    grad_inputs = grad_res + reduce_square(grad_projected, qkv_own, 1, input_parts)
    inputs_back, feed_bundle, qkv_got, out_total, out_far = join(
        grad_inputs.astype(BF), feed_bundle, qkv_got, out_total, out_far
    )
    grad_inputs_home = send(inputs_back, SPREAD)
    feed_other = send(feed_bundle, HOME_X)
    feed_far = send(feed_bundle, HOME_CORE)
    qkv_mine = qkv_keep + qkv_got
    qkv_home = send(qkv_mine, HOME_HALF)
    out_total = (out_total.astype(F32) + out_far.astype(F32)).astype(BF)
    out_got = send(out_total, OTHER_HALF)
    qkv_home, out_got, feed_other, feed_far = join(qkv_home, out_got, feed_other, feed_far)
    feed_far_other = send(feed_other, HOME_CORE)
    qkv_sends = whole_call(
        square_qkv_kernel, "square_qkv", [((quarter + 16, 3 * WIDE), BF)] * GROUP,
        step_square, qkv_mine, qkv_home,
    )
    qkv_sends, out_total, feed_far_other = join(qkv_sends, out_total + out_got, feed_far_other)
    qkv_gots = [qkv_sends[0]] + [send(qkv_sends[k], HOME_SQUARE[k]) for k in range(1, GROUP)]
    grad_w_out = send(out_total, OUT_RETURN)
    grad_w_down, grad_w_gate, grad_w_up = whole_call(
        finish_feed_kernel, "finish_feed",
        [(by_x_rows + (D,), F32)] + [((2, quarter, w_gate.shape[1]), F32)] * 2,
        home_flags, feed_bundle, feed_other, feed_far, feed_far_other,
    )
    (qkv_bundle,) = whole_call(
        join_qkv_kernel, "join_qkv", [((moved_rows, 3 * WIDE), BF)], step_square, *qkv_gots
    )
    qkv_other = send(qkv_bundle, HOME_X)
    grad_w_qkv, vector_grads = whole_call(
        finish_qkv_kernel, "finish_qkv", [((2, quarter, 3 * D), F32), ((8, D), F32)],
        home_flags, qkv_bundle, qkv_other, send(qkv_bundle, HOME_CORE), send(qkv_other, HOME_CORE),
    )
    vector_grads = lax.dynamic_slice_in_dim(vector_grads, shard * rows_d, rows_d, 1)

    return (
        result_home.reshape(tokens_in.shape),
        grad_inputs_home.astype(F32).reshape(tokens_in.shape),
        grad_w_qkv.reshape(w_qkv.shape),
        grad_w_out.astype(F32),
        vector_grads[0],
        vector_grads[1],
        grad_w_gate.reshape(w_gate.shape),
        grad_w_up.reshape(w_up.shape),
        grad_w_down.reshape(w_down.shape),
        vector_grads[2],
        vector_grads[3],
    )


def solution(mesh):
    sizes = dict(mesh.shape)
    clustered = (sizes["rep"], sizes["shard"]) == (4, 8)
    plan = per_device_clustered if clustered else per_device
    return jax.shard_map(
        plan,
        mesh=mesh,
        in_specs=(
            P("rep", "shard", None),
            P("rep", None),
            P("shard", None),
            P("shard", None),
            P("shard"),
            P("shard"),
            P("shard", None),
            P("shard", None),
            P("shard", None),
            P("shard"),
            P("shard"),
            P("rep", "shard", None),
        ),
        out_specs=(
            P("rep", "shard", None),
            P("rep", "shard", None),
            P("shard", None),
            P("shard", None),
            P("shard"),
            P("shard"),
            P("shard", None),
            P("shard", None),
            P("shard", None),
            P("shard"),
            P("shard"),
        ),
        check_vma=False,
    )
```

```python
import math

import jax
import jax.numpy as jnp
from jax import lax
from jax.experimental import pallas as pl
from jax.experimental.pallas import tpu as pltpu
from jax.sharding import PartitionSpec as P

D = 768
HEAD_DIM = 64
HEADS = 12


epsilon = 1e-05
rope_base = 1000.0


def rope_tables(start, count):
    positions = (start + jnp.arange(count, dtype=jnp.int32)).astype(jnp.float32)
    middle = HEAD_DIM // 2
    inverse = rope_base ** (-(2.0 * jnp.arange(middle).astype(jnp.float32)) / HEAD_DIM)
    angles = positions[:, None] * inverse[None, :]
    return (jnp.cos(angles)[:, None, :], jnp.sin(angles)[:, None, :])


def rotate(values_in, cosine, sine):
    middle = values_in.shape[-1] // 2
    first_half = values_in[..., :middle]
    second_half = values_in[..., middle:]
    return jnp.concatenate(
        [first_half * cosine - second_half * sine, second_half * cosine + first_half * sine],
        axis=-1,
    )


def rotate_back(upstream, cosine, sine):
    middle = upstream.shape[-1] // 2
    first_half = upstream[..., :middle]
    second_half = upstream[..., middle:]
    return jnp.concatenate(
        [first_half * cosine + second_half * sine, second_half * cosine - first_half * sine],
        axis=-1,
    )


def norm_forward(values_in, gain_vec, shift_vec):
    centred = values_in - jnp.mean(values_in, axis=-1, keepdims=True)
    variance = jnp.mean(centred * centred, axis=-1, keepdims=True)
    inverse_scale = lax.rsqrt(variance + epsilon)
    normed = centred * inverse_scale
    return (normed * gain_vec + shift_vec, normed, inverse_scale)


def norm_backward(upstream, normed, inverse_scale, gain_vec):
    scaled = upstream * gain_vec
    return inverse_scale * (
        scaled
        - jnp.mean(scaled, axis=-1, keepdims=True)
        - normed * jnp.mean(scaled * normed, axis=-1, keepdims=True)
    )


def fetch_attention(w_qkv, w_out, ln1_gain, ln1_bias):
    return (
        lax.all_gather(w_qkv, "shard", axis=0, tiled=True),
        lax.all_gather(w_out, "shard", axis=0, tiled=True),
        lax.all_gather(ln1_gain, "shard", axis=0, tiled=True),
        lax.all_gather(ln1_bias, "shard", axis=0, tiled=True),
    )


def fetch_feedforward(w_gate, w_up, w_down, ln2_gain, ln2_bias):
    return (
        lax.all_gather(w_gate, "shard", axis=0, tiled=True),
        lax.all_gather(w_up, "shard", axis=0, tiled=True),
        lax.all_gather(w_down, "shard", axis=0, tiled=True),
        lax.all_gather(ln2_gain, "shard", axis=0, tiled=True),
        lax.all_gather(ln2_bias, "shard", axis=0, tiled=True),
    )


def pair_columns(matrix, pair_index):
    width = 2 * HEAD_DIM
    return lax.dynamic_slice_in_dim(matrix, pair_index * width, width, 1).reshape(
        matrix.shape[0], 2, HEAD_DIM
    )


def pair_scores(pair_index, queries, key_rows, same_doc):
    scores = jnp.einsum(
        "qhd,khd->hqk",
        pair_columns(queries, pair_index),
        pair_columns(key_rows, pair_index),
        preferred_element_type=jnp.float32,
    ) * HEAD_DIM ** (-0.5)
    return jnp.where(same_doc[None], scores, -jnp.inf)


def attention_forward(queries, key_rows, value_rows, same_doc):

    def one_pair(pair_index):
        scores = pair_scores(pair_index, queries, key_rows, same_doc)
        row_max = jnp.max(scores, axis=-1, keepdims=True)
        expons = jnp.exp(scores - row_max)
        row_total = jnp.sum(expons, axis=-1, keepdims=True)
        weights_bf = (expons / row_total).astype(jnp.bfloat16)
        attended = jnp.einsum(
            "hqk,khd->qhd",
            weights_bf,
            pair_columns(value_rows, pair_index),
            preferred_element_type=jnp.float32,
        )
        return (
            attended.reshape(attended.shape[0], 2 * HEAD_DIM),
            (row_max + jnp.log(row_total))[..., 0],
        )

    attended, log_totals = lax.map(one_pair, jnp.arange(HEADS // 2, dtype=jnp.int32))
    return (jnp.transpose(attended, (1, 0, 2)).reshape(queries.shape[0], D), log_totals)


def attention_backward(queries, key_rows, value_rows, grad_attended, log_totals, same_doc):
    scale_factor = HEAD_DIM ** (-0.5)
    width = 2 * HEAD_DIM

    def one_pair(inputs):
        pair_index, pair_logs = inputs
        scores = pair_scores(pair_index, queries, key_rows, same_doc)
        weights = jnp.exp(scores - pair_logs[..., None])
        grad_pair = pair_columns(grad_attended, pair_index)
        grad_weights = jnp.einsum(
            "qhd,khd->hqk",
            grad_pair,
            pair_columns(value_rows, pair_index),
            preferred_element_type=jnp.float32,
        )
        row_delta = jnp.sum(weights * grad_weights, axis=-1, keepdims=True)
        grad_scores = (weights * (grad_weights - row_delta)).astype(jnp.bfloat16)
        grad_query = (
            jnp.einsum(
                "hqk,khd->qhd",
                grad_scores,
                pair_columns(key_rows, pair_index),
                preferred_element_type=jnp.float32,
            )
            * scale_factor
        )
        grad_key = (
            jnp.einsum(
                "hqk,qhd->khd",
                grad_scores,
                pair_columns(queries, pair_index),
                preferred_element_type=jnp.float32,
            )
            * scale_factor
        )
        grad_value = jnp.einsum(
            "hqk,qhd->khd",
            weights.astype(jnp.bfloat16),
            grad_pair,
            preferred_element_type=jnp.float32,
        )
        return (
            grad_query.reshape(-1, width),
            grad_key.reshape(-1, width),
            grad_value.reshape(-1, width),
        )

    pair_grads = lax.map(one_pair, (jnp.arange(HEADS // 2, dtype=jnp.int32), log_totals))
    return tuple(
        (
            jnp.transpose(pair_part, (1, 0, 2)).reshape(pair_part.shape[1], D)
            for pair_part in pair_grads
        )
    )


def per_device(
    tokens_in,
    segment_ids,
    w_qkv,
    w_out,
    ln1_gain,
    ln1_bias,
    w_gate,
    w_up,
    w_down,
    ln2_gain,
    ln2_bias,
    out_cotangent,
):
    inputs_bf = tokens_in.reshape(-1, D)
    token_count = inputs_bf.shape[0]
    doc_ids = segment_ids.reshape(-1)
    start = lax.axis_index("shard") * token_count
    own_docs = lax.dynamic_slice_in_dim(doc_ids, start, token_count)
    same_doc = own_docs[:, None] == doc_ids[None, :]
    cosine, sine = rope_tables(start, token_count)
    heads_shape = (token_count, HEADS, HEAD_DIM)
    qkv_full, out_full, gain_one, bias_one = fetch_attention(w_qkv, w_out, ln1_gain, ln1_bias)
    projected = jnp.dot(inputs_bf, qkv_full, preferred_element_type=jnp.float32)
    queries = (
        rotate(projected[:, :D].reshape(heads_shape), cosine, sine)
        .reshape(token_count, D)
        .astype(jnp.bfloat16)
    )
    own_keys = (
        rotate(projected[:, D : 2 * D].reshape(heads_shape), cosine, sine)
        .reshape(token_count, D)
        .astype(jnp.bfloat16)
    )
    own_values = projected[:, 2 * D :].astype(jnp.bfloat16)
    key_rows, value_rows = (
        lax.all_gather(own_keys, "shard", axis=0, tiled=True),
        lax.all_gather(own_values, "shard", axis=0, tiled=True),
    )
    attended, log_totals = attention_forward(queries, key_rows, value_rows, same_doc)
    attended_bf = attended.astype(jnp.bfloat16)
    branch = jnp.dot(attended_bf, out_full, preferred_element_type=jnp.float32)
    inputs_f = inputs_bf.astype(jnp.float32)
    first_out, first_normed, first_scale = norm_forward(
        inputs_f + branch, gain_one.astype(jnp.float32), bias_one.astype(jnp.float32)
    )
    gate_full, up_full, down_full, gain_two, bias_two = fetch_feedforward(
        w_gate, w_up, w_down, ln2_gain, ln2_bias
    )
    first_bf = first_out.astype(jnp.bfloat16)
    gate_act = jnp.dot(first_bf, gate_full, preferred_element_type=jnp.float32)
    up_act = jnp.dot(first_bf, up_full, preferred_element_type=jnp.float32)
    hidden_bf = (jax.nn.silu(gate_act) * up_act).astype(jnp.bfloat16)
    down_act = jnp.dot(hidden_bf, down_full, preferred_element_type=jnp.float32)
    result, second_normed, second_scale = norm_forward(
        first_out + down_act, gain_two.astype(jnp.float32), bias_two.astype(jnp.float32)
    )
    gate_full, up_full, down_full, gain_two, bias_two = fetch_feedforward(
        w_gate, w_up, w_down, ln2_gain, ln2_bias
    )
    upstream = out_cotangent.reshape(-1, D).astype(jnp.float32)
    grad_gain_two = jnp.sum(upstream * second_normed, axis=0)
    grad_bias_two = jnp.sum(upstream, axis=0)
    grad_second = norm_backward(upstream, second_normed, second_scale, gain_two.astype(jnp.float32))
    grad_down_bf = grad_second.astype(jnp.bfloat16)
    grad_down_w = jnp.einsum(
        "tf,td->fd", hidden_bf, grad_down_bf, preferred_element_type=jnp.float32
    )
    grad_hidden = jnp.einsum(
        "td,fd->tf", grad_down_bf, down_full, preferred_element_type=jnp.float32
    )
    sigmoid_gate = jax.nn.sigmoid(gate_act)
    grad_gate_bf = (
        grad_hidden * up_act * sigmoid_gate * (1.0 + gate_act * (1.0 - sigmoid_gate))
    ).astype(jnp.bfloat16)
    grad_up_bf = (grad_hidden * jax.nn.silu(gate_act)).astype(jnp.bfloat16)
    grad_gate_w = jnp.einsum(
        "td,tf->df", first_bf, grad_gate_bf, preferred_element_type=jnp.float32
    )
    grad_up_w = jnp.einsum("td,tf->df", first_bf, grad_up_bf, preferred_element_type=jnp.float32)
    grad_first = grad_second + jnp.einsum(
        "tf,df->td", grad_gate_bf, gate_full, preferred_element_type=jnp.float32
    )
    grad_first = grad_first + jnp.einsum(
        "tf,df->td", grad_up_bf, up_full, preferred_element_type=jnp.float32
    )
    qkv_full, out_full, gain_one, bias_one = fetch_attention(w_qkv, w_out, ln1_gain, ln1_bias)
    grad_gain_one = jnp.sum(grad_first * first_normed, axis=0)
    grad_bias_one = jnp.sum(grad_first, axis=0)
    grad_res = norm_backward(grad_first, first_normed, first_scale, gain_one.astype(jnp.float32))
    grad_branch_bf = grad_res.astype(jnp.bfloat16)
    grad_out_w = jnp.einsum(
        "tc,td->cd", attended_bf, grad_branch_bf, preferred_element_type=jnp.float32
    )
    grad_attended_bf = jnp.einsum(
        "td,cd->tc", grad_branch_bf, out_full, preferred_element_type=jnp.float32
    ).astype(jnp.bfloat16)
    grad_queries, grad_keys_all, grad_values_all = attention_backward(
        queries, key_rows, value_rows, grad_attended_bf, log_totals, same_doc
    )
    grad_keys, grad_values = (
        lax.psum_scatter(
            grad_keys_all.astype(jnp.bfloat16), "shard", scatter_dimension=0, tiled=True
        ).astype(jnp.float32),
        lax.psum_scatter(
            grad_values_all.astype(jnp.bfloat16), "shard", scatter_dimension=0, tiled=True
        ).astype(jnp.float32),
    )
    grad_projected = jnp.concatenate(
        [
            rotate_back(grad_queries.reshape(heads_shape), cosine, sine).reshape(token_count, D),
            rotate_back(grad_keys.reshape(heads_shape), cosine, sine).reshape(token_count, D),
            grad_values,
        ],
        axis=1,
    ).astype(jnp.bfloat16)
    grad_qkv_w = jnp.einsum(
        "td,tn->dn", inputs_bf, grad_projected, preferred_element_type=jnp.float32
    )
    grad_inputs = grad_res + jnp.einsum(
        "tn,dn->td", grad_projected, qkv_full, preferred_element_type=jnp.float32
    )
    (
        sum_qkv,
        sum_out,
        sum_gain_one,
        sum_bias_one,
        sum_gate,
        sum_up,
        sum_down,
        sum_gain_two,
        sum_bias_two,
    ) = (
        lax.psum_scatter(
            grad_qkv_w.astype(jnp.bfloat16), "shard", scatter_dimension=0, tiled=True
        ).astype(jnp.float32),
        lax.psum_scatter(
            grad_out_w.astype(jnp.bfloat16), "shard", scatter_dimension=0, tiled=True
        ).astype(jnp.float32),
        lax.psum_scatter(
            grad_gain_one.astype(jnp.bfloat16), "shard", scatter_dimension=0, tiled=True
        ).astype(jnp.float32),
        lax.psum_scatter(
            grad_bias_one.astype(jnp.bfloat16), "shard", scatter_dimension=0, tiled=True
        ).astype(jnp.float32),
        lax.psum_scatter(
            grad_gate_w.astype(jnp.bfloat16), "shard", scatter_dimension=0, tiled=True
        ).astype(jnp.float32),
        lax.psum_scatter(
            grad_up_w.astype(jnp.bfloat16), "shard", scatter_dimension=0, tiled=True
        ).astype(jnp.float32),
        lax.psum_scatter(
            grad_down_w.astype(jnp.bfloat16), "shard", scatter_dimension=0, tiled=True
        ).astype(jnp.float32),
        lax.psum_scatter(
            grad_gain_two.astype(jnp.bfloat16), "shard", scatter_dimension=0, tiled=True
        ).astype(jnp.float32),
        lax.psum_scatter(
            grad_bias_two.astype(jnp.bfloat16), "shard", scatter_dimension=0, tiled=True
        ).astype(jnp.float32),
    )
    totals = (
        lax.psum(sum_qkv.astype(jnp.bfloat16), "rep").astype(jnp.float32),
        lax.psum(sum_out.astype(jnp.bfloat16), "rep").astype(jnp.float32),
        lax.psum(sum_gain_one.astype(jnp.bfloat16), "rep").astype(jnp.float32),
        lax.psum(sum_bias_one.astype(jnp.bfloat16), "rep").astype(jnp.float32),
        lax.psum(sum_gate.astype(jnp.bfloat16), "rep").astype(jnp.float32),
        lax.psum(sum_up.astype(jnp.bfloat16), "rep").astype(jnp.float32),
        lax.psum(sum_down.astype(jnp.bfloat16), "rep").astype(jnp.float32),
        lax.psum(sum_gain_two.astype(jnp.bfloat16), "rep").astype(jnp.float32),
        lax.psum(sum_bias_two.astype(jnp.bfloat16), "rep").astype(jnp.float32),
    )
    return (
        result.astype(jnp.bfloat16).reshape(tokens_in.shape),
        grad_inputs.reshape(tokens_in.shape),
        totals[0],
        totals[1],
        totals[2],
        totals[3],
        totals[4],
        totals[5],
        totals[6],
        totals[7],
        totals[8],
    )


BF = jnp.bfloat16
F32 = jnp.float32
AXES = ("rep", "shard")
TILE = 256
GROUP = 4
OWN_HEADS = 3
NARROW = OWN_HEADS * HEAD_DIM
WIDE = 256
LANES = 128
LOG2E = 1.4426950408889634
SCORE_FACTOR = HEAD_DIM ** (-0.5) * LOG2E
MASKED = -1e30


def cost(flops, *arrays):
    moved = sum(math.prod(array.shape) * array.dtype.itemsize for array in arrays)
    return pl.CostEstimate(flops=flops, transcendentals=0, bytes_accessed=moved)


def moves(target):
    pairs = []
    for rep in range(4):
        for shard in range(8):
            goal = target(rep // 2, rep % 2, shard // 4, shard % 4)
            if goal is not None:
                x, c, h, j = goal
                pairs.append((rep * 8 + shard, (2 * x + c) * 8 + 4 * h + j))
    return pairs


SPREAD = moves(lambda x, c, h, j: (x, h, c, j))
OTHER_CORE = moves(lambda x, c, h, j: (x, 1 - c, h, j))
OTHER_X = moves(lambda x, c, h, j: (1 - x, c, h, j))
OTHER_HALF = moves(lambda x, c, h, j: (x, c, 1 - h, j))
SQUARE = [moves(lambda x, c, h, j, k=k: (x, c, h, j ^ k)) for k in range(GROUP)]
ROUND = [moves(lambda x, c, h, j, i=i: (x, c, h ^ c, j ^ (2 * x + i))) for i in range(2)]
OUT_FETCH = moves(lambda x, c, h, j: (x, j % 2, c, (4 * h + j) // 2))
OUT_RETURN = moves(lambda x, c, h, j: (x, h, (2 * j + c) // 4, (2 * j + c) % 4))
HOME_HALF = moves(lambda x, c, h, j: (x, c, 1 - h, j) if c != h else None)
HOME_SQUARE = [
    moves(lambda x, c, h, j, k=k: (x, c, h, j ^ k) if c == h else None) for k in range(GROUP)
]
HOME_X = moves(lambda x, c, h, j: (1 - x, c, h, j) if c == h else None)
HOME_CORE = moves(lambda x, c, h, j: (x, 1 - c, h, j) if c == h else None)


def send(value, pairs):
    return lax.ppermute(value, AXES, pairs)


def pick(flag, first, second):
    return jnp.where(flag, second, first)


def unmix(blocks, j):
    bit0 = (j % 2) == 1
    bit1 = (j // 2) == 1
    b = blocks
    b = [pick(bit0, b[0], b[1]), pick(bit0, b[1], b[0]), pick(bit0, b[2], b[3]), pick(bit0, b[3], b[2])]
    return [pick(bit1, b[0], b[2]), pick(bit1, b[1], b[3]), pick(bit1, b[2], b[0]), pick(bit1, b[3], b[1])]


def turned(values):
    lane = lax.broadcasted_iota(jnp.int32, values.shape, 1) % HEAD_DIM
    middle = HEAD_DIM // 2
    return jnp.where(
        lane < middle,
        -pltpu.roll(values, WIDE - middle, 1),
        pltpu.roll(values, middle, 1),
    )


def doubled(table):
    return jnp.concatenate([table, table], axis=1)


def project_kernel(x_ref, w_ref, cos_ref, sin_ref, q_ref, kv_ref):
    projected = jnp.dot(x_ref[...], w_ref[...], preferred_element_type=F32)
    cosine = doubled(cos_ref[...])
    sine = doubled(sin_ref[...])
    for index, ref in ((0, q_ref), (1, kv_ref)):
        part = projected[:, index * WIDE : (index + 1) * WIDE]
        ref[:, :WIDE] = (part * cosine + turned(part) * sine).astype(BF)
    kv_ref[:, WIDE:] = projected[:, 2 * WIDE :].astype(BF)


def project(x_rows, w_qkv, cosine, sine):
    rows = x_rows.shape[0]
    return pl.pallas_call(
        project_kernel,
        grid=(rows // TILE,),
        in_specs=[
            pl.BlockSpec((TILE, D), lambda i: (i, 0)),
            pl.BlockSpec((D, 3 * WIDE), lambda i: (0, 0)),
            pl.BlockSpec((TILE, 128), lambda i: (i, 0)),
            pl.BlockSpec((TILE, 128), lambda i: (i, 0)),
        ],
        out_specs=[
            pl.BlockSpec((TILE, WIDE), lambda i: (i, 0)),
            pl.BlockSpec((TILE, 2 * WIDE), lambda i: (i, 0)),
        ],
        out_shape=[
            jax.ShapeDtypeStruct((rows, WIDE), BF),
            jax.ShapeDtypeStruct((rows, 2 * WIDE), BF),
        ],
        cost_estimate=cost(2 * rows * w_qkv.size, x_rows, w_qkv, x_rows, cosine, sine),
        name="project",
    )(x_rows, w_qkv, cosine, sine)


def head_only(values, head):
    lane = lax.broadcasted_iota(jnp.int32, values.shape, 1) // HEAD_DIM
    return jnp.where(lane == head, values, jnp.zeros_like(values))


def share_document(ids_ref, q_tile, kv_tile):
    q_first = ids_ref[q_tile * TILE]
    q_last = ids_ref[q_tile * TILE + TILE - 1]
    k_first = ids_ref[kv_tile * TILE]
    k_last = ids_ref[kv_tile * TILE + TILE - 1]
    return jnp.logical_and(k_first <= q_last, q_first <= k_last)


def contract(left, right, left_dim, right_dim):
    return lax.dot_general(
        left, right, (((left_dim,), (right_dim,)), ((), ())), preferred_element_type=F32
    )


def attend_kernel(
    ids_ref, row_ids_ref, col_ids_ref, q_ref, own_ref, other_ref, out_ref, log_ref,
    v_turned, max_ref, total_ref, acc_ref,
):
    q_tile = pl.program_id(0)
    own_tiles = own_ref.shape[0] // TILE

    @pl.when(q_tile == 0)
    def _():
        for base, ref in ((0, own_ref), (own_tiles, other_ref)):
            for tile in range(own_tiles):
                v_turned[base + tile] = jnp.transpose(
                    ref[pl.ds(tile * TILE, TILE), WIDE:]
                )[:NARROW]

    queries = q_ref[...]
    per_head = [head_only(queries, head) for head in range(OWN_HEADS)]
    q_ids = row_ids_ref[0]
    max_ref[...] = jnp.full(max_ref.shape, MASKED, F32)
    total_ref[...] = jnp.zeros(total_ref.shape, F32)
    acc_ref[...] = jnp.zeros(acc_ref.shape, F32)

    for base, ref in ((0, own_ref), (own_tiles, other_ref)):

        def one_tile(tile, carry, base=base, ref=ref):
            @pl.when(share_document(ids_ref, q_tile, base + tile))
            def _():
                start = pl.multiple_of(tile * TILE, TILE)
                keys = ref[pl.ds(start, TILE), :WIDE]
                same = (
                    col_ids_ref[pl.ds(pl.multiple_of((base + tile) * TILE, TILE), TILE), :] == q_ids
                )
                for head in range(OWN_HEADS):
                    scores = contract(keys, per_head[head], 1, 1) * SCORE_FACTOR
                    scores = jnp.where(same, scores, MASKED)
                    old_max = max_ref[head : head + 1, :]
                    new_max = jnp.maximum(old_max, jnp.max(scores, axis=0, keepdims=True))
                    shrink = jnp.exp2(old_max - new_max)
                    expons = jnp.exp2(scores - new_max)
                    max_ref[head : head + 1, :] = new_max
                    total_ref[head : head + 1, :] = total_ref[
                        head : head + 1, :
                    ] * shrink + jnp.sum(expons, axis=0, keepdims=True)
                    rows = slice(head * HEAD_DIM, (head + 1) * HEAD_DIM)
                    acc_ref[rows, :] = acc_ref[rows, :] * shrink + jnp.dot(
                        v_turned[base + tile, rows, :],
                        expons.astype(BF),
                        preferred_element_type=F32,
                    )

            return carry

        lax.fori_loop(0, own_tiles, one_tile, 0)

    parts = []
    for head in range(OWN_HEADS):
        rows = slice(head * HEAD_DIM, (head + 1) * HEAD_DIM)
        parts.append(acc_ref[rows, :] / total_ref[head : head + 1, :])
    parts.append(jnp.zeros((WIDE - NARROW, TILE), F32))
    out_ref[...] = jnp.transpose(jnp.concatenate(parts, axis=0)).astype(BF)
    row = lax.broadcasted_iota(jnp.int32, log_ref.shape, 0)
    log_ref[...] = jnp.where(
        row < OWN_HEADS,
        max_ref[...] + jnp.log2(jnp.where(row < OWN_HEADS, total_ref[...], 1.0)),
        0.0,
    )


def attend(ids, row_ids, col_ids, queries, kv_own, kv_other):
    rows = queries.shape[0]
    whole = lambda array: pl.BlockSpec(array.shape, lambda i, ids: (0,) * array.ndim)
    return pl.pallas_call(
        attend_kernel,
        grid_spec=pltpu.PrefetchScalarGridSpec(
            num_scalar_prefetch=1,
            grid=(rows // TILE,),
            in_specs=[
                pl.BlockSpec((1, 1, TILE), lambda i, ids: (i, 0, 0)),
                whole(col_ids),
                pl.BlockSpec((TILE, WIDE), lambda i, ids: (i, 0)),
                whole(kv_own),
                whole(kv_other),
            ],
            out_specs=[
                pl.BlockSpec((TILE, WIDE), lambda i, ids: (i, 0)),
                pl.BlockSpec((8, TILE), lambda i, ids: (0, i)),
            ],
            scratch_shapes=[
                pltpu.VMEM((2 * rows // TILE, NARROW, TILE), BF),
                pltpu.VMEM((8, TILE), F32),
                pltpu.VMEM((8, TILE), F32),
                pltpu.VMEM((NARROW, TILE), F32),
            ],
        ),
        out_shape=[
            jax.ShapeDtypeStruct((rows, WIDE), BF),
            jax.ShapeDtypeStruct((8, rows), F32),
        ],
        cost_estimate=cost(
            4 * OWN_HEADS * WIDE * rows * 2 * rows, queries, kv_own, kv_other, queries
        ),
        name="attend",
    )(ids, row_ids, col_ids, queries, kv_own, kv_other)


def attend_back_kernel(
    ids_ref, row_ids_ref, col_ids_ref, q_ref, up_ref, out_ref, log_ref, own_ref, other_ref,
    cos_ref, sin_ref, dq_ref, own_grad_ref, other_grad_ref,
    k_turned, acc_ref, key_acc, value_acc,
):
    q_tile = pl.program_id(0)
    own_tiles = own_ref.shape[0] // TILE

    @pl.when(q_tile == 0)
    def _():
        for base, ref in ((0, own_ref), (own_tiles, other_ref)):
            for tile in range(own_tiles):
                k_turned[base + tile] = jnp.transpose(
                    ref[pl.ds(tile * TILE, TILE), :WIDE]
                )[:NARROW]
        key_acc[...] = jnp.zeros(key_acc.shape, F32)
        value_acc[...] = jnp.zeros(value_acc.shape, F32)

    queries = q_ref[...]
    upstream = up_ref[...]
    sides = (slice(0, LANES), slice(LANES, WIDE))
    members = ((0, 1), (2,))
    split = lambda values: [
        [head_only(values[:, side], head % 2) for head in inside]
        for side, inside in zip(sides, members)
    ]
    q_heads, up_heads = split(queries), split(upstream)
    q_stacks = [jnp.concatenate(parts, axis=0) for parts in q_heads]
    up_stacks = [jnp.concatenate(parts, axis=0) for parts in up_heads]
    products = upstream.astype(F32) * out_ref[...].astype(F32)
    lane_head = lax.broadcasted_iota(jnp.int32, (8, WIDE), 1) // HEAD_DIM
    selector = (lane_head == lax.broadcasted_iota(jnp.int32, (8, WIDE), 0)).astype(F32)
    deltas = lax.dot_general(
        selector, products, (((1,), (1,)), ((), ())),
        precision=lax.Precision.HIGHEST, preferred_element_type=F32,
    )
    q_ids = row_ids_ref[0]
    acc_ref[...] = jnp.zeros(acc_ref.shape, F32)

    for base, ref in ((0, own_ref), (own_tiles, other_ref)):

        def one_tile(tile, carry, base=base, ref=ref):
            @pl.when(share_document(ids_ref, q_tile, base + tile))
            def _():
                start = pl.multiple_of(tile * TILE, TILE)
                place = pl.ds(pl.multiple_of((base + tile) * TILE, TILE), TILE)
                keys = ref[pl.ds(start, TILE), :WIDE]
                values = ref[pl.ds(start, TILE), WIDE:]
                same = col_ids_ref[place, :] == q_ids
                for side, inside, q_side, up_side, q_stack, up_stack in zip(
                    sides, members, q_heads, up_heads, q_stacks, up_stacks
                ):
                    all_weights, all_grads = [], []
                    for head, query, grad in zip(inside, q_side, up_side):
                        scores = contract(keys[:, side], query, 1, 1) * SCORE_FACTOR
                        weights = jnp.where(
                            same, jnp.exp2(scores - log_ref[head : head + 1, :]), 0.0
                        )
                        grad_weights = contract(values[:, side], grad, 1, 1)
                        grad_scores = (
                            weights * (grad_weights - deltas[head : head + 1, :])
                        ).astype(BF)
                        all_weights.append(weights.astype(BF))
                        all_grads.append(grad_scores)
                        rows = slice(head * HEAD_DIM, (head + 1) * HEAD_DIM)
                        acc_ref[rows, :] += jnp.dot(
                            k_turned[base + tile, rows, :], grad_scores,
                            preferred_element_type=F32,
                        )
                    value_acc[place, side] += jnp.dot(
                        jnp.concatenate(all_weights, axis=1), up_stack, preferred_element_type=F32
                    )
                    key_acc[place, side] += jnp.dot(
                        jnp.concatenate(all_grads, axis=1), q_stack, preferred_element_type=F32
                    )

            return carry

        lax.fori_loop(0, own_tiles, one_tile, 0)

    factor = HEAD_DIM ** (-0.5)
    grad_query = jnp.transpose(
        jnp.concatenate([acc_ref[...], jnp.zeros((WIDE - NARROW, TILE), F32)], axis=0)
    )
    grad_query = grad_query * factor
    dq_ref[...] = (
        grad_query * doubled(cos_ref[...]) - turned(grad_query) * doubled(sin_ref[...])
    ).astype(BF)

    @pl.when(q_tile == pl.num_programs(0) - 1)
    def _():
        rows = own_grad_ref.shape[0]
        own_grad_ref[:, :WIDE] = key_acc[:rows, :] * factor
        own_grad_ref[:, WIDE:] = value_acc[:rows, :]
        other_grad_ref[:, :WIDE] = (key_acc[rows:, :] * factor).astype(BF)
        other_grad_ref[:, WIDE:] = value_acc[rows:, :].astype(BF)


def attend_back(
    ids, row_ids, col_ids, queries, upstream, attended, logs, kv_own, kv_other, cosine, sine
):
    rows = queries.shape[0]
    whole = lambda array: pl.BlockSpec(array.shape, lambda i, ids: (0,) * array.ndim)
    tiled = lambda width: pl.BlockSpec((TILE, width), lambda i, ids: (i, 0))
    return pl.pallas_call(
        attend_back_kernel,
        grid_spec=pltpu.PrefetchScalarGridSpec(
            num_scalar_prefetch=1,
            grid=(rows // TILE,),
            in_specs=[
                pl.BlockSpec((1, 1, TILE), lambda i, ids: (i, 0, 0)),
                whole(col_ids),
                tiled(WIDE),
                tiled(WIDE),
                tiled(WIDE),
                pl.BlockSpec((8, TILE), lambda i, ids: (0, i)),
                whole(kv_own),
                whole(kv_other),
                tiled(128),
                tiled(128),
            ],
            out_specs=[
                tiled(WIDE),
                pl.BlockSpec((rows, 2 * WIDE), lambda i, ids: (0, 0)),
                pl.BlockSpec((rows, 2 * WIDE), lambda i, ids: (0, 0)),
            ],
            scratch_shapes=[
                pltpu.VMEM((2 * rows // TILE, NARROW, TILE), BF),
                pltpu.VMEM((NARROW, TILE), F32),
                pltpu.VMEM((2 * rows, WIDE), F32),
                pltpu.VMEM((2 * rows, WIDE), F32),
            ],
        ),
        out_shape=[
            jax.ShapeDtypeStruct((rows, WIDE), BF),
            jax.ShapeDtypeStruct((rows, 2 * WIDE), F32),
            jax.ShapeDtypeStruct((rows, 2 * WIDE), BF),
        ],
        cost_estimate=cost(
            10 * OWN_HEADS * WIDE * rows * 2 * rows, queries, kv_own, kv_other, queries
        ),
        name="attend_back",
    )(ids, row_ids, col_ids, queries, upstream, attended, logs, kv_own, kv_other, cosine, sine)


def join_grads_kernel(dq_ref, own_ref, got_ref, cos_ref, sin_ref, out_ref):
    out_ref[:, :WIDE] = dq_ref[...]
    total = own_ref[...] + got_ref[...].astype(F32)
    keys = total[:, :WIDE]
    out_ref[:, WIDE : 2 * WIDE] = (
        keys * doubled(cos_ref[...]) - turned(keys) * doubled(sin_ref[...])
    ).astype(BF)
    out_ref[:, 2 * WIDE :] = total[:, WIDE:].astype(BF)


def join_grads(grad_queries, own, got, cosine, sine):
    rows = grad_queries.shape[0]
    tiled = lambda width: pl.BlockSpec((TILE, width), lambda i: (i, 0))
    return pl.pallas_call(
        join_grads_kernel,
        grid=(rows // TILE,),
        in_specs=[tiled(WIDE), tiled(2 * WIDE), tiled(2 * WIDE), tiled(128), tiled(128)],
        out_specs=tiled(3 * WIDE),
        out_shape=jax.ShapeDtypeStruct((rows, 3 * WIDE), BF),
        cost_estimate=cost(8 * own.size, own, own, got, grad_queries),
        name="join_grads",
    )(grad_queries, own, got, cosine, sine)


def after(value, *others):
    return lax.optimization_barrier((value,) + others)[0]


def join(*values):
    return lax.optimization_barrier(values)


def pack_qkv_kernel(target_ref, w_ref, vectors_ref, *refs):
    packed = refs[-1]
    for target in range(GROUP):
        for part in range(3):
            start = part * D + target * NARROW
            packed[target, :, part * NARROW : (part + 1) * NARROW] = w_ref[
                :, start : start + NARROW
            ]
        packed[target, :, 3 * NARROW :] = vectors_ref[...]
    for index, ref in enumerate(refs[:-1]):
        ref[...] = packed[target_ref[index]]


def pack_qkv(targets, w_qkv, vectors):
    rows = w_qkv.shape[0]
    width = 3 * NARROW + vectors.shape[1]
    return pl.pallas_call(
        pack_qkv_kernel,
        in_specs=[
            pl.BlockSpec(memory_space=pltpu.SMEM),
            pl.BlockSpec(memory_space=pltpu.VMEM),
            pl.BlockSpec(memory_space=pltpu.VMEM),
        ],
        out_specs=[pl.BlockSpec(memory_space=pltpu.VMEM)] * 2,
        out_shape=[jax.ShapeDtypeStruct((rows, width), BF)] * 2,
        scratch_shapes=[pltpu.VMEM((GROUP, rows, width), BF)],
        name="pack_qkv",
    )(targets, w_qkv, vectors)


def pack_gate_up_kernel(target_ref, gate_ref, up_ref, *refs):
    packed = refs[-1]
    width = packed.shape[2] // 4
    for target in range(GROUP):
        for index in range(4):
            source = (gate_ref, up_ref)[index // 2]
            start = (index % 2 * GROUP + target) * width
            packed[target, :, index * width : (index + 1) * width] = source[
                :, start : start + width
            ]
    for index, ref in enumerate(refs[:-1]):
        ref[...] = packed[target_ref[index]]


def pack_gate_up(targets, w_gate, w_up):
    rows = w_gate.shape[0]
    width = 2 * w_gate.shape[1] // GROUP
    return pl.pallas_call(
        pack_gate_up_kernel,
        in_specs=[
            pl.BlockSpec(memory_space=pltpu.SMEM),
            pl.BlockSpec(memory_space=pltpu.VMEM),
            pl.BlockSpec(memory_space=pltpu.VMEM),
        ],
        out_specs=[pl.BlockSpec(memory_space=pltpu.VMEM)] * 2,
        out_shape=[jax.ShapeDtypeStruct((rows, width), BF)] * 2,
        scratch_shapes=[pltpu.VMEM((GROUP, rows, width), BF)],
        name="pack_gate_up",
    )(targets, w_gate, w_up)


def unpack_qkv_kernel(place_ref, near_ref, far_ref, out_ref, vectors_ref):
    zeros = jnp.zeros((near_ref.shape[1], WIDE - NARROW), BF)
    for index in range(2 * GROUP):
        source = (near_ref, far_ref)[index // GROUP]
        place = place_ref[index]
        for part in range(3):
            out_ref[place, :, part * WIDE : part * WIDE + NARROW] = source[
                index % GROUP, :, part * NARROW : (part + 1) * NARROW
            ]
            out_ref[place, :, part * WIDE + NARROW : (part + 1) * WIDE] = zeros
        vectors_ref[place] = source[index % GROUP, :, 3 * NARROW :]


def unpack_qkv(places, near, far):
    _, rows, width = near.shape
    return pl.pallas_call(
        unpack_qkv_kernel,
        in_specs=[
            pl.BlockSpec(memory_space=pltpu.SMEM),
            pl.BlockSpec(memory_space=pltpu.VMEM),
            pl.BlockSpec(memory_space=pltpu.VMEM),
        ],
        out_specs=[pl.BlockSpec(memory_space=pltpu.VMEM)] * 2,
        out_shape=[
            jax.ShapeDtypeStruct((2 * GROUP, rows, 3 * WIDE), BF),
            jax.ShapeDtypeStruct((2 * GROUP, rows, width - 3 * NARROW), BF),
        ],
        name="unpack_qkv",
    )(places, near, far)


def unpack_kernel(place_ref, near_ref, far_ref, out_ref):
    for index in range(2 * GROUP):
        out_ref[place_ref[index]] = (near_ref, far_ref)[index // GROUP][index % GROUP]


def unpack(places, near, far):
    count, rows, width = near.shape
    return pl.pallas_call(
        unpack_kernel,
        in_specs=[
            pl.BlockSpec(memory_space=pltpu.SMEM),
            pl.BlockSpec(memory_space=pltpu.VMEM),
            pl.BlockSpec(memory_space=pltpu.VMEM),
        ],
        out_specs=pl.BlockSpec(memory_space=pltpu.VMEM),
        out_shape=jax.ShapeDtypeStruct((2 * count, rows, width), BF),
        name="unpack",
    )(places, near, far)


def split_feed_kernel(x_ref, down_ref, down_got_ref, gate_up_ref, gate_up_got_ref, keep_ref, away_ref):
    mine = x_ref[0]
    width = down_ref.shape[-1]
    for block in range(GROUP):
        for side, ref in ((mine, keep_ref), (1 - mine, away_ref)):
            ref[block] = (
                down_ref[block, side] + down_got_ref[block, side].astype(F32)
            ).astype(BF)
            total = gate_up_ref[block, side] + gate_up_got_ref[block, side].astype(F32)
            ref[GROUP + block] = total[:, :width].astype(BF)
            ref[2 * GROUP + block] = total[:, width:].astype(BF)


def whole_call(kernel, name, shapes, scalars, *arrays):
    return pl.pallas_call(
        kernel,
        in_specs=[pl.BlockSpec(memory_space=pltpu.SMEM)]
        + [pl.BlockSpec(memory_space=pltpu.VMEM)] * len(arrays),
        out_specs=[pl.BlockSpec(memory_space=pltpu.VMEM)] * len(shapes),
        out_shape=[jax.ShapeDtypeStruct(shape, dtype) for shape, dtype in shapes],
        cost_estimate=cost(sum(a.size for a in arrays), *arrays, *arrays),
        name=name,
    )(scalars, *arrays)


def square_feed_kernel(index_ref, mine_ref, got_ref, kept_ref, *send_refs):
    for k in range(GROUP):
        target = index_ref[k]
        for part in range(2):
            slot = (part + 1) * GROUP + target
            block = mine_ref[slot] + got_ref[slot]
            if k == 0:
                kept_ref[GROUP + part] = block
            else:
                send_refs[k - 1][part] = block
        kept_ref[k] = mine_ref[k] + got_ref[k]


def join_feed_kernel(index_ref, kept_ref, *refs):
    out_ref = refs[-1]
    for k in range(GROUP):
        out_ref[k] = kept_ref[k]
        for part in range(2):
            slot = (part + 1) * GROUP + index_ref[k]
            out_ref[slot] = kept_ref[GROUP + part] if k == 0 else refs[k - 1][part]


def finish_feed_kernel(flag_ref, own_ref, other_ref, far_own_ref, far_other_ref, down_ref, gate_ref, up_ref):
    mine, at_home = flag_ref[0], flag_ref[1] == 1
    rows = own_ref.shape[1]
    half = own_ref.shape[2] // 2
    for slot in range(3 * GROUP):
        for near, far, side in ((own_ref, far_own_ref, mine), (other_ref, far_other_ref, 1 - mine)):
            block = jnp.where(at_home, near[slot], far[slot]).astype(F32)
            if slot < GROUP:
                down_ref[slot, side] = block
            else:
                ref = gate_ref if slot < 2 * GROUP else up_ref
                start = slot % GROUP * half
                width = GROUP * half
                ref[side, :, start : start + half] = block[:, :half]
                ref[side, :, width + start : width + start + half] = block[:, half:]


def split_cores_kernel(c_ref, part_ref, vectors_ref, away_ref):
    rows = part_ref.shape[1]
    away_ref[:rows] = part_ref[1 - c_ref[0]].astype(BF)
    away_ref[rows:] = jnp.zeros((16, part_ref.shape[2]), BF)
    away_ref[rows : rows + 8] = vectors_ref[...].astype(BF)


def split_x_kernel(flag_ref, part_ref, vectors_ref, got_ref, keep_ref, away_ref):
    core, mine = flag_ref[0], flag_ref[1]
    rows = part_ref.shape[1]
    step = rows // (2 * GROUP)
    for block in range(GROUP):
        for side, ref in ((mine, keep_ref), (1 - mine, away_ref)):
            place = pl.ds(pl.multiple_of((2 * block + side) * step, step), step)
            ref[block * step : (block + 1) * step] = (
                part_ref[core, place] + got_ref[place].astype(F32)
            ).astype(BF)
    for ref in (keep_ref, away_ref):
        ref[GROUP * step :] = got_ref[rows:]
        ref[GROUP * step : GROUP * step + 8] = (
            vectors_ref[...] + got_ref[rows : rows + 8].astype(F32)
        ).astype(BF)


def square_qkv_kernel(index_ref, mine_ref, got_ref, *refs):
    step = (mine_ref.shape[0] - 16) // GROUP
    vectors = mine_ref[GROUP * step :] + got_ref[GROUP * step :]
    for k in range(GROUP):
        place = pl.ds(pl.multiple_of(index_ref[k] * step, step), step)
        refs[k][:step] = mine_ref[place] + got_ref[place]
        refs[k][step:] = vectors


def join_qkv_kernel(index_ref, *refs):
    out_ref = refs[-1]
    step = refs[0].shape[0] - 16
    vectors = refs[0][step:].astype(F32)
    for k in range(GROUP):
        place = pl.ds(pl.multiple_of(index_ref[k] * step, step), step)
        out_ref[place] = refs[k][:step]
        if k:
            vectors += refs[k][step:].astype(F32)
    out_ref[GROUP * step :] = vectors.astype(BF)


def finish_qkv_kernel(flag_ref, own_ref, other_ref, far_own_ref, far_other_ref, out_ref, vectors_ref):
    mine, at_home = flag_ref[0], flag_ref[1] == 1
    step = (own_ref.shape[0] - 16) // GROUP
    for block in range(GROUP):
        rows = slice(block * step, (block + 1) * step)
        for near, far, side in ((own_ref, far_own_ref, mine), (other_ref, far_other_ref, 1 - mine)):
            values = jnp.where(at_home, near[rows], far[rows]).astype(F32)
            for part in range(3):
                start = part * D + block * NARROW
                out_ref[side, :, start : start + NARROW] = values[
                    :, part * WIDE : part * WIDE + NARROW
                ]
    rows = slice(GROUP * step, GROUP * step + 8)
    vectors_ref[...] = jnp.where(at_home, own_ref[rows], far_own_ref[rows]).astype(F32)


def gather_square(block):
    return [block] + [send(block, SQUARE[k]) for k in range(1, GROUP)]


def square_parts(left, weight, weight_dim):
    return [
        contract(left[k * TILE : (k + 1) * TILE], weight, 1, weight_dim).astype(BF)
        for k in range(1, GROUP)
    ]


def reduce_square(left, weight, weight_dim, parts=None):
    if parts is None:
        parts = square_parts(left, weight, weight_dim)
    got = [send(part, SQUARE[k + 1]) for k, part in enumerate(parts)]
    (total,) = join(contract(left[:TILE], weight, 1, weight_dim))
    for part in got:
        total = total + part.astype(F32)
    return total


def per_device_clustered(
    tokens_in,
    segment_ids,
    w_qkv,
    w_out,
    ln1_gain,
    ln1_bias,
    w_gate,
    w_up,
    w_down,
    ln2_gain,
    ln2_bias,
    out_cotangent,
):
    rep = lax.axis_index("rep")
    shard = lax.axis_index("shard")
    x, c = rep // 2, rep % 2
    h, j = shard // 4, shard % 4
    core_is_one = c == 1
    half_is_one = h == 1
    x_is_one = x == 1
    at_home = c == h
    token_count = tokens_in.shape[1]
    length = segment_ids.shape[1]
    rows_d = w_qkv.shape[0]
    rows_f = w_down.shape[0]
    slice_f = 2 * rows_f
    group_rows = GROUP * token_count

    inputs_bf = send(tokens_in.reshape(token_count, D), SPREAD)
    doc_ids = send(segment_ids, SPREAD).reshape(2, GROUP, token_count)

    by_x = jnp.stack([2 * x, 2 * x + 1, 2 - 2 * x, 3 - 2 * x]) ^ j
    targets = by_x[:2]
    places = jnp.concatenate([GROUP * (h ^ c) + by_x, GROUP * (1 - (h ^ c)) + by_x])

    out_got = send(w_out, OUT_FETCH)
    vectors = jnp.stack([ln1_gain, ln1_bias, ln2_gain, ln2_bias], axis=1)
    qkv_packed = pack_qkv(targets, w_qkv, vectors)
    qkv_mine = after(
        jnp.stack([send(part, ROUND[i]) for i, part in enumerate(qkv_packed)]), inputs_bf
    )
    x_tiles = gather_square(inputs_bf)
    qkv_second = send(qkv_mine, OTHER_X)
    qkv_near = jnp.concatenate([qkv_mine, qkv_second], axis=0)
    qkv_second, w_gate, w_up, down_whole, doc_ids, j = join(
        qkv_second, w_gate, w_up, w_down, doc_ids, j
    )
    qkv_far = send(qkv_near, OTHER_CORE)
    qkv_own, vectors_got = unpack_qkv(places, qkv_near, qkv_far)
    qkv_own = qkv_own.reshape(D, 3 * WIDE)
    x_rows = jnp.concatenate(x_tiles, axis=0)

    tile_index = j ^ jnp.arange(GROUP, dtype=jnp.int32)
    first_row = (c * GROUP + tile_index) * token_count
    positions = (
        first_row[:, None] + jnp.arange(token_count, dtype=jnp.int32)[None, :]
    ).reshape(group_rows).astype(F32)
    middle = HEAD_DIM // 2
    exponents = jnp.arange(128, dtype=jnp.int32) % middle
    inverse = rope_base ** (-(2.0 * exponents.astype(F32)) / HEAD_DIM)
    angles = positions[:, None] * inverse[None, :]
    cosine, sine = jnp.cos(angles), jnp.sin(angles)
    mixed = jnp.stack(unmix([doc_ids[:, k] for k in range(GROUP)], j), axis=1)
    ids = jnp.concatenate(
        [pick(core_is_one, mixed[0], mixed[1]), pick(core_is_one, mixed[1], mixed[0])], axis=0
    )
    flat_ids = ids.reshape(length)
    row_ids = ids.reshape(length // TILE, 1, TILE)
    col_ids = flat_ids[:, None]

    part_f = rows_f // 4
    gate_up_packed = pack_gate_up(targets, w_gate, w_up)
    down_sent = lax.dynamic_slice_in_dim(down_whole, (2 * c + x) * part_f, part_f, 0)
    (
        x_rows, qkv_own, vectors_got, out_got, flat_ids, row_ids, col_ids, cosine, sine, down_sent,
        *gate_up_packed,
    ) = join(
        x_rows, qkv_own, vectors_got, out_got, flat_ids, row_ids, col_ids, cosine, sine, down_sent,
        *gate_up_packed,
    )

    queries, kv_own = project(x_rows, qkv_own, cosine, sine)
    kv_other = send(kv_own, OTHER_CORE)
    out_other = send(out_got, OTHER_CORE)
    kv_other, out_other, down_sent, *gate_up_packed = join(
        kv_other, out_other, down_sent, *gate_up_packed
    )
    attended, logs = attend(flat_ids, row_ids, col_ids, queries, kv_own, kv_other)
    gate_up_first = [send(part, ROUND[i]) for i, part in enumerate(gate_up_packed)]
    down_mine = send(down_sent, OTHER_HALF)
    attended, logs, down_mine, *gate_up_first = join(attended, logs, down_mine, *gate_up_first)
    out_own = jnp.concatenate(
        [
            pick(core_is_one, out_got, out_other),
            pick(core_is_one, out_other, out_got),
            jnp.zeros((WIDE - NARROW, D), BF),
        ],
        axis=0,
    )

    branch_parts = square_parts(attended, out_own, 0)
    gate_up_mine, down_mine, *branch_parts = join(
        jnp.stack(gate_up_first), down_mine, *branch_parts
    )
    gate_up_second = send(gate_up_mine, OTHER_X)
    down_got = send(down_mine, OTHER_X)
    branch = reduce_square(attended, out_own, 0, branch_parts)
    vectors_full = jnp.transpose(vectors_got.reshape(D, 4)).astype(F32)
    gain_one, bias_one, gain_two, bias_two = (vectors_full[i] for i in range(4))
    first_out, first_normed, first_scale = norm_forward(
        inputs_bf.astype(F32) + branch, gain_one, bias_one
    )
    first_bf, gate_up_second, down_got, out_cotangent = join(
        first_out.astype(BF), gate_up_second, down_got, out_cotangent
    )

    first_tiles = gather_square(first_bf)
    gate_up_near = jnp.concatenate([gate_up_mine, gate_up_second], axis=0)
    gate_up_far = send(gate_up_near, OTHER_CORE)
    gate_up_own = unpack(places, gate_up_near, gate_up_far).reshape(D, 2 * slice_f)
    down_got = after(down_got, first_tiles[1])
    down_pair = jnp.concatenate(
        [pick(x_is_one, down_mine, down_got), pick(x_is_one, down_got, down_mine)], axis=0
    )
    down_other = send(down_pair, OTHER_CORE)
    down_far = jnp.concatenate(
        [pick(core_is_one, down_pair, down_other), pick(core_is_one, down_other, down_pair)], axis=0
    )
    down_own = jnp.concatenate(
        [pick(half_is_one, w_down, down_far), pick(half_is_one, down_far, w_down)], axis=0
    )
    first_rows = jnp.concatenate(first_tiles, axis=0)
    acts = contract(first_rows, gate_up_own, 1, 0)
    gate_act, up_act = acts[:, :slice_f], acts[:, slice_f:]
    hidden_bf = (jax.nn.silu(gate_act) * up_act).astype(BF)
    cotangent = send(after(out_cotangent, hidden_bf).reshape(token_count, D), SPREAD)
    down_act = reduce_square(hidden_bf, down_own, 0)
    result, second_normed, second_scale = norm_forward(first_out + down_act, gain_two, bias_two)

    upstream = cotangent.astype(F32)
    grad_gain_two = jnp.sum(upstream * second_normed, axis=0, keepdims=True)
    grad_bias_two = jnp.sum(upstream, axis=0, keepdims=True)
    grad_second = norm_backward(upstream, second_normed, second_scale, gain_two)
    grad_down_rows = jnp.concatenate(gather_square(grad_second.astype(BF)), axis=0)
    grad_hidden = contract(grad_down_rows, down_own, 1, 1)
    sigmoid_gate = jax.nn.sigmoid(gate_act)
    grad_gate_bf = (
        grad_hidden * up_act * sigmoid_gate * (1.0 + gate_act * (1.0 - sigmoid_gate))
    ).astype(BF)
    grad_up_bf = (grad_hidden * (gate_act * sigmoid_gate)).astype(BF)
    grad_acts = jnp.concatenate([grad_gate_bf, grad_up_bf], axis=1)
    first_parts = square_parts(grad_acts, gate_up_own, 1)

    quarter = rows_d // 2
    step_square = jnp.arange(GROUP, dtype=jnp.int32) ^ j
    x_flag = x.reshape(1)
    home_flags = jnp.stack([x, at_home.astype(jnp.int32)])

    def over_cores(partial):
        keep = pick(core_is_one, partial[0], partial[1])
        away = pick(core_is_one, partial[1], partial[0])
        return keep, send(away.astype(BF), OTHER_CORE)

    by_x_rows = (GROUP, 2, quarter)
    gate_up_keep, gate_up_got = over_cores(
        contract(first_rows, after(grad_acts, *first_parts), 0, 0).reshape(
            2, D // 2, 2 * slice_f
        )
    )
    down_keep, down_got = over_cores(
        contract(hidden_bf, after(grad_down_rows, *first_parts), 0, 0).reshape(2, rows_f, D)
    )
    bundle_shape = ((3 * GROUP, quarter, D), BF)
    grad_first = grad_second + reduce_square(grad_acts, gate_up_own, 1, first_parts)
    grad_gain_one = jnp.sum(grad_first * first_normed, axis=0, keepdims=True)
    grad_bias_one = jnp.sum(grad_first, axis=0, keepdims=True)
    grad_res = norm_backward(grad_first, first_normed, first_scale, gain_one)
    grad_res_bf, down_got, gate_up_got = join(grad_res.astype(BF), down_got, gate_up_got)
    grad_branch_tiles = gather_square(grad_res_bf)
    feed_keep, feed_away = whole_call(
        split_feed_kernel, "split_feed", [bundle_shape] * 2, x_flag,
        down_keep.reshape(by_x_rows + (D,)), down_got.reshape(by_x_rows + (D,)),
        gate_up_keep.reshape(by_x_rows + (2 * slice_f,)),
        gate_up_got.reshape(by_x_rows + (2 * slice_f,)),
    )
    feed_got = send(feed_away, OTHER_X)

    grad_branch_rows = jnp.concatenate(grad_branch_tiles, axis=0)
    grad_attended = contract(grad_branch_rows, out_own, 1, 1).astype(BF)
    out_keep, out_got = over_cores(
        contract(attended, grad_branch_rows, 0, 0)[:NARROW].reshape(2, rows_d, D)
    )
    grad_attended, feed_got, out_got = join(grad_attended, feed_got, out_got)
    feed_mine = feed_keep + feed_got
    out_total = (out_keep + out_got.astype(F32)).astype(BF)
    grad_attended, feed_mine, out_total, result_bf = join(
        grad_attended, feed_mine, out_total, result.astype(BF)
    )
    grad_queries, kv_grad_own, kv_grad_away = attend_back(
        flat_ids, row_ids, col_ids, queries, grad_attended, attended, logs, kv_own, kv_other,
        cosine, sine,
    )
    feed_home = send(feed_mine, HOME_HALF)
    out_far = send(out_total, OTHER_X)
    result_home = send(result_bf, SPREAD)
    grad_queries, kv_grad_own, kv_grad_away, feed_home, out_far, result_home = join(
        grad_queries, kv_grad_own, kv_grad_away, feed_home, out_far, result_home
    )
    kv_grad_got = send(kv_grad_away, OTHER_CORE)
    feed_kept, *feed_sends = whole_call(
        square_feed_kernel, "square_feed",
        [((GROUP + 2, quarter, D), BF)] + [((2, quarter, D), BF)] * 3,
        step_square, feed_mine, feed_home,
    )
    out_total = (out_total.astype(F32) + out_far.astype(F32)).astype(BF)
    kv_grad_got, out_total, *feed_sends = join(kv_grad_got, out_total, *feed_sends)
    feed_gots = [send(part, HOME_SQUARE[k + 1]) for k, part in enumerate(feed_sends)]
    out_got = send(out_total, OTHER_HALF)
    grad_projected = join_grads(grad_queries, kv_grad_own, kv_grad_got, cosine, sine)

    qkv_part = contract(x_rows, grad_projected, 0, 0).reshape(2, D // 2, 3 * WIDE)
    vector_part = jnp.concatenate(
        [grad_gain_one, grad_bias_one, grad_gain_two, grad_bias_two]
        + [jnp.zeros((4, D), F32)], axis=0
    )
    moved_rows = D // 4 + 16
    (qkv_away,) = whole_call(
        split_cores_kernel, "split_cores", [((D // 2 + 16, 3 * WIDE), BF)], c.reshape(1),
        qkv_part, vector_part,
    )
    qkv_away, out_got, *feed_gots = join(qkv_away, out_got, *feed_gots)
    qkv_got = send(qkv_away, OTHER_CORE)
    (feed_bundle,) = whole_call(
        join_feed_kernel, "join_feed", [bundle_shape], step_square, feed_kept, *feed_gots
    )
    qkv_got, feed_bundle, out_total = join(qkv_got, feed_bundle, out_total + out_got)
    qkv_keep, qkv_away = whole_call(
        split_x_kernel, "split_x", [((moved_rows, 3 * WIDE), BF)] * 2, jnp.stack([c, x]),
        qkv_part, vector_part, qkv_got,
    )
    grad_projected, qkv_away = join(grad_projected, qkv_away)
    qkv_got = send(qkv_away, OTHER_X)
    input_parts = square_parts(grad_projected, qkv_own, 1)
    input_parts = join(*input_parts)

    input_sum = reduce_square(grad_projected, qkv_own, 1, input_parts)
    qkv_mine = qkv_keep + qkv_got
    qkv_home = send(qkv_mine, HOME_HALF)
    feed_other = send(feed_bundle, HOME_X)
    feed_far = send(feed_bundle, HOME_CORE)
    grad_w_out = send(out_total, OUT_RETURN)
    inputs_back, qkv_home, feed_other, feed_far, grad_w_out = join(
        (grad_res + input_sum).astype(BF), qkv_home, feed_other, feed_far, grad_w_out
    )
    grad_inputs_home = send(inputs_back, SPREAD)
    feed_far_other = send(feed_other, HOME_CORE)
    qkv_sends = whole_call(
        square_qkv_kernel, "square_qkv", [((quarter + 16, 3 * WIDE), BF)] * GROUP,
        step_square, qkv_mine, qkv_home,
    )
    feed_far_other, *qkv_sends = join(feed_far_other, *qkv_sends)
    qkv_gots = [qkv_sends[0]] + [send(qkv_sends[k], HOME_SQUARE[k]) for k in range(1, GROUP)]
    grad_w_down, grad_w_gate, grad_w_up = whole_call(
        finish_feed_kernel, "finish_feed",
        [(by_x_rows + (D,), F32)] + [((2, quarter, w_gate.shape[1]), F32)] * 2,
        home_flags, feed_bundle, feed_other, feed_far, feed_far_other,
    )
    grad_inputs_home, grad_w_down, grad_w_gate, grad_w_up, *qkv_gots = join(
        grad_inputs_home, grad_w_down, grad_w_gate, grad_w_up, *qkv_gots
    )
    (qkv_bundle,) = whole_call(
        join_qkv_kernel, "join_qkv", [((moved_rows, 3 * WIDE), BF)], step_square, *qkv_gots
    )
    qkv_other = send(qkv_bundle, HOME_X)
    grad_w_qkv, vector_grads = whole_call(
        finish_qkv_kernel, "finish_qkv", [((2, quarter, 3 * D), F32), ((8, D), F32)],
        home_flags, qkv_bundle, qkv_other, send(qkv_bundle, HOME_CORE), send(qkv_other, HOME_CORE),
    )
    vector_grads = lax.dynamic_slice_in_dim(vector_grads, shard * rows_d, rows_d, 1)

    return (
        result_home.reshape(tokens_in.shape),
        grad_inputs_home.astype(F32).reshape(tokens_in.shape),
        grad_w_qkv.reshape(w_qkv.shape),
        grad_w_out.astype(F32),
        vector_grads[0],
        vector_grads[1],
        grad_w_gate.reshape(w_gate.shape),
        grad_w_up.reshape(w_up.shape),
        grad_w_down.reshape(w_down.shape),
        vector_grads[2],
        vector_grads[3],
    )


def solution(mesh):
    sizes = dict(mesh.shape)
    clustered = (sizes["rep"], sizes["shard"]) == (4, 8)
    plan = per_device_clustered if clustered else per_device
    return jax.shard_map(
        plan,
        mesh=mesh,
        in_specs=(
            P("rep", "shard", None),
            P("rep", None),
            P("shard", None),
            P("shard", None),
            P("shard"),
            P("shard"),
            P("shard", None),
            P("shard", None),
            P("shard", None),
            P("shard"),
            P("shard"),
            P("rep", "shard", None),
        ),
        out_specs=(
            P("rep", "shard", None),
            P("rep", "shard", None),
            P("shard", None),
            P("shard", None),
            P("shard"),
            P("shard"),
            P("shard", None),
            P("shard", None),
            P("shard", None),
            P("shard"),
            P("shard"),
        ),
        check_vma=False,
    )
```

```python
import math

import jax
import jax.numpy as jnp
from jax import lax
from jax.experimental import pallas as pl
from jax.experimental.pallas import tpu as pltpu
from jax.sharding import PartitionSpec as P

D = 768
HEAD_DIM = 64
HEADS = 12


epsilon = 1e-05
rope_base = 1000.0


def rope_tables(start, count):
    positions = (start + jnp.arange(count, dtype=jnp.int32)).astype(jnp.float32)
    middle = HEAD_DIM // 2
    inverse = rope_base ** (-(2.0 * jnp.arange(middle).astype(jnp.float32)) / HEAD_DIM)
    angles = positions[:, None] * inverse[None, :]
    return (jnp.cos(angles)[:, None, :], jnp.sin(angles)[:, None, :])


def rotate(values_in, cosine, sine):
    middle = values_in.shape[-1] // 2
    first_half = values_in[..., :middle]
    second_half = values_in[..., middle:]
    return jnp.concatenate(
        [first_half * cosine - second_half * sine, second_half * cosine + first_half * sine],
        axis=-1,
    )


def rotate_back(upstream, cosine, sine):
    middle = upstream.shape[-1] // 2
    first_half = upstream[..., :middle]
    second_half = upstream[..., middle:]
    return jnp.concatenate(
        [first_half * cosine + second_half * sine, second_half * cosine - first_half * sine],
        axis=-1,
    )


def norm_forward(values_in, gain_vec, shift_vec):
    centred = values_in - jnp.mean(values_in, axis=-1, keepdims=True)
    variance = jnp.mean(centred * centred, axis=-1, keepdims=True)
    inverse_scale = lax.rsqrt(variance + epsilon)
    normed = centred * inverse_scale
    return (normed * gain_vec + shift_vec, normed, inverse_scale)


def norm_backward(upstream, normed, inverse_scale, gain_vec):
    scaled = upstream * gain_vec
    return inverse_scale * (
        scaled
        - jnp.mean(scaled, axis=-1, keepdims=True)
        - normed * jnp.mean(scaled * normed, axis=-1, keepdims=True)
    )


def fetch_attention(w_qkv, w_out, ln1_gain, ln1_bias):
    return (
        lax.all_gather(w_qkv, "shard", axis=0, tiled=True),
        lax.all_gather(w_out, "shard", axis=0, tiled=True),
        lax.all_gather(ln1_gain, "shard", axis=0, tiled=True),
        lax.all_gather(ln1_bias, "shard", axis=0, tiled=True),
    )


def fetch_feedforward(w_gate, w_up, w_down, ln2_gain, ln2_bias):
    return (
        lax.all_gather(w_gate, "shard", axis=0, tiled=True),
        lax.all_gather(w_up, "shard", axis=0, tiled=True),
        lax.all_gather(w_down, "shard", axis=0, tiled=True),
        lax.all_gather(ln2_gain, "shard", axis=0, tiled=True),
        lax.all_gather(ln2_bias, "shard", axis=0, tiled=True),
    )


def pair_columns(matrix, pair_index):
    width = 2 * HEAD_DIM
    return lax.dynamic_slice_in_dim(matrix, pair_index * width, width, 1).reshape(
        matrix.shape[0], 2, HEAD_DIM
    )


def pair_scores(pair_index, queries, key_rows, same_doc):
    scores = jnp.einsum(
        "qhd,khd->hqk",
        pair_columns(queries, pair_index),
        pair_columns(key_rows, pair_index),
        preferred_element_type=jnp.float32,
    ) * HEAD_DIM ** (-0.5)
    return jnp.where(same_doc[None], scores, -jnp.inf)


def attention_forward(queries, key_rows, value_rows, same_doc):

    def one_pair(pair_index):
        scores = pair_scores(pair_index, queries, key_rows, same_doc)
        row_max = jnp.max(scores, axis=-1, keepdims=True)
        expons = jnp.exp(scores - row_max)
        row_total = jnp.sum(expons, axis=-1, keepdims=True)
        weights_bf = (expons / row_total).astype(jnp.bfloat16)
        attended = jnp.einsum(
            "hqk,khd->qhd",
            weights_bf,
            pair_columns(value_rows, pair_index),
            preferred_element_type=jnp.float32,
        )
        return (
            attended.reshape(attended.shape[0], 2 * HEAD_DIM),
            (row_max + jnp.log(row_total))[..., 0],
        )

    attended, log_totals = lax.map(one_pair, jnp.arange(HEADS // 2, dtype=jnp.int32))
    return (jnp.transpose(attended, (1, 0, 2)).reshape(queries.shape[0], D), log_totals)


def attention_backward(queries, key_rows, value_rows, grad_attended, log_totals, same_doc):
    scale_factor = HEAD_DIM ** (-0.5)
    width = 2 * HEAD_DIM

    def one_pair(inputs):
        pair_index, pair_logs = inputs
        scores = pair_scores(pair_index, queries, key_rows, same_doc)
        weights = jnp.exp(scores - pair_logs[..., None])
        grad_pair = pair_columns(grad_attended, pair_index)
        grad_weights = jnp.einsum(
            "qhd,khd->hqk",
            grad_pair,
            pair_columns(value_rows, pair_index),
            preferred_element_type=jnp.float32,
        )
        row_delta = jnp.sum(weights * grad_weights, axis=-1, keepdims=True)
        grad_scores = (weights * (grad_weights - row_delta)).astype(jnp.bfloat16)
        grad_query = (
            jnp.einsum(
                "hqk,khd->qhd",
                grad_scores,
                pair_columns(key_rows, pair_index),
                preferred_element_type=jnp.float32,
            )
            * scale_factor
        )
        grad_key = (
            jnp.einsum(
                "hqk,qhd->khd",
                grad_scores,
                pair_columns(queries, pair_index),
                preferred_element_type=jnp.float32,
            )
            * scale_factor
        )
        grad_value = jnp.einsum(
            "hqk,qhd->khd",
            weights.astype(jnp.bfloat16),
            grad_pair,
            preferred_element_type=jnp.float32,
        )
        return (
            grad_query.reshape(-1, width),
            grad_key.reshape(-1, width),
            grad_value.reshape(-1, width),
        )

    pair_grads = lax.map(one_pair, (jnp.arange(HEADS // 2, dtype=jnp.int32), log_totals))
    return tuple(
        (
            jnp.transpose(pair_part, (1, 0, 2)).reshape(pair_part.shape[1], D)
            for pair_part in pair_grads
        )
    )


def per_device(
    tokens_in,
    segment_ids,
    w_qkv,
    w_out,
    ln1_gain,
    ln1_bias,
    w_gate,
    w_up,
    w_down,
    ln2_gain,
    ln2_bias,
    out_cotangent,
):
    inputs_bf = tokens_in.reshape(-1, D)
    token_count = inputs_bf.shape[0]
    doc_ids = segment_ids.reshape(-1)
    start = lax.axis_index("shard") * token_count
    own_docs = lax.dynamic_slice_in_dim(doc_ids, start, token_count)
    same_doc = own_docs[:, None] == doc_ids[None, :]
    cosine, sine = rope_tables(start, token_count)
    heads_shape = (token_count, HEADS, HEAD_DIM)
    qkv_full, out_full, gain_one, bias_one = fetch_attention(w_qkv, w_out, ln1_gain, ln1_bias)
    projected = jnp.dot(inputs_bf, qkv_full, preferred_element_type=jnp.float32)
    queries = (
        rotate(projected[:, :D].reshape(heads_shape), cosine, sine)
        .reshape(token_count, D)
        .astype(jnp.bfloat16)
    )
    own_keys = (
        rotate(projected[:, D : 2 * D].reshape(heads_shape), cosine, sine)
        .reshape(token_count, D)
        .astype(jnp.bfloat16)
    )
    own_values = projected[:, 2 * D :].astype(jnp.bfloat16)
    key_rows, value_rows = (
        lax.all_gather(own_keys, "shard", axis=0, tiled=True),
        lax.all_gather(own_values, "shard", axis=0, tiled=True),
    )
    attended, log_totals = attention_forward(queries, key_rows, value_rows, same_doc)
    attended_bf = attended.astype(jnp.bfloat16)
    branch = jnp.dot(attended_bf, out_full, preferred_element_type=jnp.float32)
    inputs_f = inputs_bf.astype(jnp.float32)
    first_out, first_normed, first_scale = norm_forward(
        inputs_f + branch, gain_one.astype(jnp.float32), bias_one.astype(jnp.float32)
    )
    gate_full, up_full, down_full, gain_two, bias_two = fetch_feedforward(
        w_gate, w_up, w_down, ln2_gain, ln2_bias
    )
    first_bf = first_out.astype(jnp.bfloat16)
    gate_act = jnp.dot(first_bf, gate_full, preferred_element_type=jnp.float32)
    up_act = jnp.dot(first_bf, up_full, preferred_element_type=jnp.float32)
    hidden_bf = (jax.nn.silu(gate_act) * up_act).astype(jnp.bfloat16)
    down_act = jnp.dot(hidden_bf, down_full, preferred_element_type=jnp.float32)
    result, second_normed, second_scale = norm_forward(
        first_out + down_act, gain_two.astype(jnp.float32), bias_two.astype(jnp.float32)
    )
    gate_full, up_full, down_full, gain_two, bias_two = fetch_feedforward(
        w_gate, w_up, w_down, ln2_gain, ln2_bias
    )
    upstream = out_cotangent.reshape(-1, D).astype(jnp.float32)
    grad_gain_two = jnp.sum(upstream * second_normed, axis=0)
    grad_bias_two = jnp.sum(upstream, axis=0)
    grad_second = norm_backward(upstream, second_normed, second_scale, gain_two.astype(jnp.float32))
    grad_down_bf = grad_second.astype(jnp.bfloat16)
    grad_down_w = jnp.einsum(
        "tf,td->fd", hidden_bf, grad_down_bf, preferred_element_type=jnp.float32
    )
    grad_hidden = jnp.einsum(
        "td,fd->tf", grad_down_bf, down_full, preferred_element_type=jnp.float32
    )
    sigmoid_gate = jax.nn.sigmoid(gate_act)
    grad_gate_bf = (
        grad_hidden * up_act * sigmoid_gate * (1.0 + gate_act * (1.0 - sigmoid_gate))
    ).astype(jnp.bfloat16)
    grad_up_bf = (grad_hidden * jax.nn.silu(gate_act)).astype(jnp.bfloat16)
    grad_gate_w = jnp.einsum(
        "td,tf->df", first_bf, grad_gate_bf, preferred_element_type=jnp.float32
    )
    grad_up_w = jnp.einsum("td,tf->df", first_bf, grad_up_bf, preferred_element_type=jnp.float32)
    grad_first = grad_second + jnp.einsum(
        "tf,df->td", grad_gate_bf, gate_full, preferred_element_type=jnp.float32
    )
    grad_first = grad_first + jnp.einsum(
        "tf,df->td", grad_up_bf, up_full, preferred_element_type=jnp.float32
    )
    qkv_full, out_full, gain_one, bias_one = fetch_attention(w_qkv, w_out, ln1_gain, ln1_bias)
    grad_gain_one = jnp.sum(grad_first * first_normed, axis=0)
    grad_bias_one = jnp.sum(grad_first, axis=0)
    grad_res = norm_backward(grad_first, first_normed, first_scale, gain_one.astype(jnp.float32))
    grad_branch_bf = grad_res.astype(jnp.bfloat16)
    grad_out_w = jnp.einsum(
        "tc,td->cd", attended_bf, grad_branch_bf, preferred_element_type=jnp.float32
    )
    grad_attended_bf = jnp.einsum(
        "td,cd->tc", grad_branch_bf, out_full, preferred_element_type=jnp.float32
    ).astype(jnp.bfloat16)
    grad_queries, grad_keys_all, grad_values_all = attention_backward(
        queries, key_rows, value_rows, grad_attended_bf, log_totals, same_doc
    )
    grad_keys, grad_values = (
        lax.psum_scatter(
            grad_keys_all.astype(jnp.bfloat16), "shard", scatter_dimension=0, tiled=True
        ).astype(jnp.float32),
        lax.psum_scatter(
            grad_values_all.astype(jnp.bfloat16), "shard", scatter_dimension=0, tiled=True
        ).astype(jnp.float32),
    )
    grad_projected = jnp.concatenate(
        [
            rotate_back(grad_queries.reshape(heads_shape), cosine, sine).reshape(token_count, D),
            rotate_back(grad_keys.reshape(heads_shape), cosine, sine).reshape(token_count, D),
            grad_values,
        ],
        axis=1,
    ).astype(jnp.bfloat16)
    grad_qkv_w = jnp.einsum(
        "td,tn->dn", inputs_bf, grad_projected, preferred_element_type=jnp.float32
    )
    grad_inputs = grad_res + jnp.einsum(
        "tn,dn->td", grad_projected, qkv_full, preferred_element_type=jnp.float32
    )
    (
        sum_qkv,
        sum_out,
        sum_gain_one,
        sum_bias_one,
        sum_gate,
        sum_up,
        sum_down,
        sum_gain_two,
        sum_bias_two,
    ) = (
        lax.psum_scatter(
            grad_qkv_w.astype(jnp.bfloat16), "shard", scatter_dimension=0, tiled=True
        ).astype(jnp.float32),
        lax.psum_scatter(
            grad_out_w.astype(jnp.bfloat16), "shard", scatter_dimension=0, tiled=True
        ).astype(jnp.float32),
        lax.psum_scatter(
            grad_gain_one.astype(jnp.bfloat16), "shard", scatter_dimension=0, tiled=True
        ).astype(jnp.float32),
        lax.psum_scatter(
            grad_bias_one.astype(jnp.bfloat16), "shard", scatter_dimension=0, tiled=True
        ).astype(jnp.float32),
        lax.psum_scatter(
            grad_gate_w.astype(jnp.bfloat16), "shard", scatter_dimension=0, tiled=True
        ).astype(jnp.float32),
        lax.psum_scatter(
            grad_up_w.astype(jnp.bfloat16), "shard", scatter_dimension=0, tiled=True
        ).astype(jnp.float32),
        lax.psum_scatter(
            grad_down_w.astype(jnp.bfloat16), "shard", scatter_dimension=0, tiled=True
        ).astype(jnp.float32),
        lax.psum_scatter(
            grad_gain_two.astype(jnp.bfloat16), "shard", scatter_dimension=0, tiled=True
        ).astype(jnp.float32),
        lax.psum_scatter(
            grad_bias_two.astype(jnp.bfloat16), "shard", scatter_dimension=0, tiled=True
        ).astype(jnp.float32),
    )
    totals = (
        lax.psum(sum_qkv.astype(jnp.bfloat16), "rep").astype(jnp.float32),
        lax.psum(sum_out.astype(jnp.bfloat16), "rep").astype(jnp.float32),
        lax.psum(sum_gain_one.astype(jnp.bfloat16), "rep").astype(jnp.float32),
        lax.psum(sum_bias_one.astype(jnp.bfloat16), "rep").astype(jnp.float32),
        lax.psum(sum_gate.astype(jnp.bfloat16), "rep").astype(jnp.float32),
        lax.psum(sum_up.astype(jnp.bfloat16), "rep").astype(jnp.float32),
        lax.psum(sum_down.astype(jnp.bfloat16), "rep").astype(jnp.float32),
        lax.psum(sum_gain_two.astype(jnp.bfloat16), "rep").astype(jnp.float32),
        lax.psum(sum_bias_two.astype(jnp.bfloat16), "rep").astype(jnp.float32),
    )
    return (
        result.astype(jnp.bfloat16).reshape(tokens_in.shape),
        grad_inputs.reshape(tokens_in.shape),
        totals[0],
        totals[1],
        totals[2],
        totals[3],
        totals[4],
        totals[5],
        totals[6],
        totals[7],
        totals[8],
    )


BF = jnp.bfloat16
F32 = jnp.float32
AXES = ("rep", "shard")
TILE = 256
GROUP = 4
OWN_HEADS = 3
NARROW = OWN_HEADS * HEAD_DIM
WIDE = 256
LANES = 128
LOG2E = 1.4426950408889634
SCORE_FACTOR = HEAD_DIM ** (-0.5) * LOG2E
MASKED = -1e30


def cost(flops, *arrays):
    moved = sum(math.prod(array.shape) * array.dtype.itemsize for array in arrays)
    return pl.CostEstimate(flops=flops, transcendentals=0, bytes_accessed=moved)


def moves(target):
    pairs = []
    for rep in range(4):
        for shard in range(8):
            goal = target(rep // 2, rep % 2, shard // 4, shard % 4)
            if goal is not None:
                x, c, h, j = goal
                pairs.append((rep * 8 + shard, (2 * x + c) * 8 + 4 * h + j))
    return pairs


SPREAD = moves(lambda x, c, h, j: (x, h, c, j))
OTHER_CORE = moves(lambda x, c, h, j: (x, 1 - c, h, j))
OTHER_X = moves(lambda x, c, h, j: (1 - x, c, h, j))
OTHER_HALF = moves(lambda x, c, h, j: (x, c, 1 - h, j))
SQUARE = [moves(lambda x, c, h, j, k=k: (x, c, h, j ^ k)) for k in range(GROUP)]
ROUND = [moves(lambda x, c, h, j, i=i: (x, c, h ^ c, j ^ (2 * x + i))) for i in range(2)]
OUT_FETCH = moves(lambda x, c, h, j: (x, j % 2, c, (4 * h + j) // 2))
OUT_RETURN = moves(lambda x, c, h, j: (x, h, (2 * j + c) // 4, (2 * j + c) % 4))
HOME_HALF = moves(lambda x, c, h, j: (x, c, 1 - h, j) if c != h else None)
HOME_SQUARE = [
    moves(lambda x, c, h, j, k=k: (x, c, h, j ^ k) if c == h else None) for k in range(GROUP)
]
HOME_X = moves(lambda x, c, h, j: (1 - x, c, h, j) if c == h else None)


def send(value, pairs):
    return lax.ppermute(value, AXES, pairs)


def pick(flag, first, second):
    return jnp.where(flag, second, first)


def unmix(blocks, j):
    bit0 = (j % 2) == 1
    bit1 = (j // 2) == 1
    b = blocks
    b = [pick(bit0, b[0], b[1]), pick(bit0, b[1], b[0]), pick(bit0, b[2], b[3]), pick(bit0, b[3], b[2])]
    return [pick(bit1, b[0], b[2]), pick(bit1, b[1], b[3]), pick(bit1, b[2], b[0]), pick(bit1, b[3], b[1])]


def turned(values):
    lane = lax.broadcasted_iota(jnp.int32, values.shape, 1) % HEAD_DIM
    middle = HEAD_DIM // 2
    return jnp.where(
        lane < middle,
        -pltpu.roll(values, WIDE - middle, 1),
        pltpu.roll(values, middle, 1),
    )


def doubled(table):
    return jnp.concatenate([table, table], axis=1)


def project_kernel(x_ref, w_ref, cos_ref, sin_ref, q_ref, kv_ref):
    projected = jnp.dot(x_ref[...], w_ref[...], preferred_element_type=F32)
    cosine = doubled(cos_ref[...])
    sine = doubled(sin_ref[...])
    for index, ref in ((0, q_ref), (1, kv_ref)):
        part = projected[:, index * WIDE : (index + 1) * WIDE]
        ref[:, :WIDE] = (part * cosine + turned(part) * sine).astype(BF)
    kv_ref[:, WIDE:] = projected[:, 2 * WIDE :].astype(BF)


def project(x_rows, w_qkv, cosine, sine):
    rows = x_rows.shape[0]
    return pl.pallas_call(
        project_kernel,
        grid=(rows // TILE,),
        in_specs=[
            pl.BlockSpec((TILE, D), lambda i: (i, 0)),
            pl.BlockSpec((D, 3 * WIDE), lambda i: (0, 0)),
            pl.BlockSpec((TILE, 128), lambda i: (i, 0)),
            pl.BlockSpec((TILE, 128), lambda i: (i, 0)),
        ],
        out_specs=[
            pl.BlockSpec((TILE, WIDE), lambda i: (i, 0)),
            pl.BlockSpec((TILE, 2 * WIDE), lambda i: (i, 0)),
        ],
        out_shape=[
            jax.ShapeDtypeStruct((rows, WIDE), BF),
            jax.ShapeDtypeStruct((rows, 2 * WIDE), BF),
        ],
        cost_estimate=cost(2 * rows * w_qkv.size, x_rows, w_qkv, x_rows, cosine, sine),
        name="project",
    )(x_rows, w_qkv, cosine, sine)


def head_only(values, head):
    lane = lax.broadcasted_iota(jnp.int32, values.shape, 1) // HEAD_DIM
    return jnp.where(lane == head, values, jnp.zeros_like(values))


def share_document(ids_ref, q_tile, kv_tile):
    q_first = ids_ref[q_tile * TILE]
    q_last = ids_ref[q_tile * TILE + TILE - 1]
    k_first = ids_ref[kv_tile * TILE]
    k_last = ids_ref[kv_tile * TILE + TILE - 1]
    return jnp.logical_and(k_first <= q_last, q_first <= k_last)


def contract(left, right, left_dim, right_dim):
    return lax.dot_general(
        left, right, (((left_dim,), (right_dim,)), ((), ())), preferred_element_type=F32
    )


def attend_kernel(
    ids_ref, row_ids_ref, col_ids_ref, q_ref, own_ref, other_ref, out_ref, log_ref,
    v_turned, max_ref, total_ref, acc_ref,
):
    q_tile = pl.program_id(0)
    own_tiles = own_ref.shape[0] // TILE

    @pl.when(q_tile == 0)
    def _():
        for base, ref in ((0, own_ref), (own_tiles, other_ref)):
            for tile in range(own_tiles):
                v_turned[base + tile] = jnp.transpose(
                    ref[pl.ds(tile * TILE, TILE), WIDE:]
                )[:NARROW]

    queries = q_ref[...]
    per_head = [head_only(queries, head) for head in range(OWN_HEADS)]
    q_ids = row_ids_ref[0]
    max_ref[...] = jnp.full(max_ref.shape, MASKED, F32)
    total_ref[...] = jnp.zeros(total_ref.shape, F32)
    acc_ref[...] = jnp.zeros(acc_ref.shape, F32)

    for base, ref in ((0, own_ref), (own_tiles, other_ref)):

        def one_tile(tile, carry, base=base, ref=ref):
            @pl.when(share_document(ids_ref, q_tile, base + tile))
            def _():
                start = pl.multiple_of(tile * TILE, TILE)
                keys = ref[pl.ds(start, TILE), :WIDE]
                same = (
                    col_ids_ref[pl.ds(pl.multiple_of((base + tile) * TILE, TILE), TILE), :] == q_ids
                )
                for head in range(OWN_HEADS):
                    scores = contract(keys, per_head[head], 1, 1) * SCORE_FACTOR
                    scores = jnp.where(same, scores, MASKED)
                    old_max = max_ref[head : head + 1, :]
                    new_max = jnp.maximum(old_max, jnp.max(scores, axis=0, keepdims=True))
                    shrink = jnp.exp2(old_max - new_max)
                    expons = jnp.exp2(scores - new_max)
                    max_ref[head : head + 1, :] = new_max
                    total_ref[head : head + 1, :] = total_ref[
                        head : head + 1, :
                    ] * shrink + jnp.sum(expons, axis=0, keepdims=True)
                    rows = slice(head * HEAD_DIM, (head + 1) * HEAD_DIM)
                    acc_ref[rows, :] = acc_ref[rows, :] * shrink + jnp.dot(
                        v_turned[base + tile, rows, :],
                        expons.astype(BF),
                        preferred_element_type=F32,
                    )

            return carry

        lax.fori_loop(0, own_tiles, one_tile, 0)

    parts = []
    for head in range(OWN_HEADS):
        rows = slice(head * HEAD_DIM, (head + 1) * HEAD_DIM)
        parts.append(acc_ref[rows, :] / total_ref[head : head + 1, :])
    parts.append(jnp.zeros((WIDE - NARROW, TILE), F32))
    out_ref[...] = jnp.transpose(jnp.concatenate(parts, axis=0)).astype(BF)
    row = lax.broadcasted_iota(jnp.int32, log_ref.shape, 0)
    log_ref[...] = jnp.where(
        row < OWN_HEADS,
        max_ref[...] + jnp.log2(jnp.where(row < OWN_HEADS, total_ref[...], 1.0)),
        0.0,
    )


def attend(ids, row_ids, col_ids, queries, kv_own, kv_other):
    rows = queries.shape[0]
    whole = lambda array: pl.BlockSpec(array.shape, lambda i, ids: (0,) * array.ndim)
    return pl.pallas_call(
        attend_kernel,
        grid_spec=pltpu.PrefetchScalarGridSpec(
            num_scalar_prefetch=1,
            grid=(rows // TILE,),
            in_specs=[
                pl.BlockSpec((1, 1, TILE), lambda i, ids: (i, 0, 0)),
                whole(col_ids),
                pl.BlockSpec((TILE, WIDE), lambda i, ids: (i, 0)),
                whole(kv_own),
                whole(kv_other),
            ],
            out_specs=[
                pl.BlockSpec((TILE, WIDE), lambda i, ids: (i, 0)),
                pl.BlockSpec((8, TILE), lambda i, ids: (0, i)),
            ],
            scratch_shapes=[
                pltpu.VMEM((2 * rows // TILE, NARROW, TILE), BF),
                pltpu.VMEM((8, TILE), F32),
                pltpu.VMEM((8, TILE), F32),
                pltpu.VMEM((NARROW, TILE), F32),
            ],
        ),
        out_shape=[
            jax.ShapeDtypeStruct((rows, WIDE), BF),
            jax.ShapeDtypeStruct((8, rows), F32),
        ],
        cost_estimate=cost(
            4 * OWN_HEADS * WIDE * rows * 2 * rows, queries, kv_own, kv_other, queries
        ),
        name="attend",
    )(ids, row_ids, col_ids, queries, kv_own, kv_other)


def attend_back_kernel(
    ids_ref, row_ids_ref, col_ids_ref, q_ref, up_ref, out_ref, log_ref, own_ref, other_ref,
    cos_ref, sin_ref, dq_ref, own_grad_ref, other_grad_ref,
    k_turned, acc_ref, key_acc, value_acc,
):
    q_tile = pl.program_id(0)
    own_tiles = own_ref.shape[0] // TILE

    @pl.when(q_tile == 0)
    def _():
        for base, ref in ((0, own_ref), (own_tiles, other_ref)):
            for tile in range(own_tiles):
                k_turned[base + tile] = jnp.transpose(
                    ref[pl.ds(tile * TILE, TILE), :WIDE]
                )[:NARROW]
        key_acc[...] = jnp.zeros(key_acc.shape, F32)
        value_acc[...] = jnp.zeros(value_acc.shape, F32)

    queries = q_ref[...]
    upstream = up_ref[...]
    sides = (slice(0, LANES), slice(LANES, WIDE))
    members = ((0, 1), (2,))
    split = lambda values: [
        [head_only(values[:, side], head % 2) for head in inside]
        for side, inside in zip(sides, members)
    ]
    q_heads, up_heads = split(queries), split(upstream)
    q_stacks = [jnp.concatenate(parts, axis=0) for parts in q_heads]
    up_stacks = [jnp.concatenate(parts, axis=0) for parts in up_heads]
    products = upstream.astype(F32) * out_ref[...].astype(F32)
    lane_head = lax.broadcasted_iota(jnp.int32, (8, WIDE), 1) // HEAD_DIM
    selector = (lane_head == lax.broadcasted_iota(jnp.int32, (8, WIDE), 0)).astype(F32)
    deltas = lax.dot_general(
        selector, products, (((1,), (1,)), ((), ())),
        precision=lax.Precision.HIGHEST, preferred_element_type=F32,
    )
    q_ids = row_ids_ref[0]
    acc_ref[...] = jnp.zeros(acc_ref.shape, F32)

    for base, ref in ((0, own_ref), (own_tiles, other_ref)):

        def one_tile(tile, carry, base=base, ref=ref):
            @pl.when(share_document(ids_ref, q_tile, base + tile))
            def _():
                start = pl.multiple_of(tile * TILE, TILE)
                place = pl.ds(pl.multiple_of((base + tile) * TILE, TILE), TILE)
                keys = ref[pl.ds(start, TILE), :WIDE]
                values = ref[pl.ds(start, TILE), WIDE:]
                same = col_ids_ref[place, :] == q_ids
                for side, inside, q_side, up_side, q_stack, up_stack in zip(
                    sides, members, q_heads, up_heads, q_stacks, up_stacks
                ):
                    all_weights, all_grads = [], []
                    for head, query, grad in zip(inside, q_side, up_side):
                        scores = contract(keys[:, side], query, 1, 1) * SCORE_FACTOR
                        weights = jnp.where(
                            same, jnp.exp2(scores - log_ref[head : head + 1, :]), 0.0
                        )
                        grad_weights = contract(values[:, side], grad, 1, 1)
                        grad_scores = (
                            weights * (grad_weights - deltas[head : head + 1, :])
                        ).astype(BF)
                        all_weights.append(weights.astype(BF))
                        all_grads.append(grad_scores)
                        rows = slice(head * HEAD_DIM, (head + 1) * HEAD_DIM)
                        acc_ref[rows, :] += jnp.dot(
                            k_turned[base + tile, rows, :], grad_scores,
                            preferred_element_type=F32,
                        )
                    value_acc[place, side] += jnp.dot(
                        jnp.concatenate(all_weights, axis=1), up_stack, preferred_element_type=F32
                    )
                    key_acc[place, side] += jnp.dot(
                        jnp.concatenate(all_grads, axis=1), q_stack, preferred_element_type=F32
                    )

            return carry

        lax.fori_loop(0, own_tiles, one_tile, 0)

    factor = HEAD_DIM ** (-0.5)
    grad_query = jnp.transpose(
        jnp.concatenate([acc_ref[...], jnp.zeros((WIDE - NARROW, TILE), F32)], axis=0)
    )
    grad_query = grad_query * factor
    dq_ref[...] = (
        grad_query * doubled(cos_ref[...]) - turned(grad_query) * doubled(sin_ref[...])
    ).astype(BF)

    @pl.when(q_tile == pl.num_programs(0) - 1)
    def _():
        rows = own_grad_ref.shape[0]
        own_grad_ref[:, :WIDE] = key_acc[:rows, :] * factor
        own_grad_ref[:, WIDE:] = value_acc[:rows, :]
        other_grad_ref[:, :WIDE] = (key_acc[rows:, :] * factor).astype(BF)
        other_grad_ref[:, WIDE:] = value_acc[rows:, :].astype(BF)


def attend_back(
    ids, row_ids, col_ids, queries, upstream, attended, logs, kv_own, kv_other, cosine, sine
):
    rows = queries.shape[0]
    whole = lambda array: pl.BlockSpec(array.shape, lambda i, ids: (0,) * array.ndim)
    tiled = lambda width: pl.BlockSpec((TILE, width), lambda i, ids: (i, 0))
    return pl.pallas_call(
        attend_back_kernel,
        grid_spec=pltpu.PrefetchScalarGridSpec(
            num_scalar_prefetch=1,
            grid=(rows // TILE,),
            in_specs=[
                pl.BlockSpec((1, 1, TILE), lambda i, ids: (i, 0, 0)),
                whole(col_ids),
                tiled(WIDE),
                tiled(WIDE),
                tiled(WIDE),
                pl.BlockSpec((8, TILE), lambda i, ids: (0, i)),
                whole(kv_own),
                whole(kv_other),
                tiled(128),
                tiled(128),
            ],
            out_specs=[
                tiled(WIDE),
                pl.BlockSpec((rows, 2 * WIDE), lambda i, ids: (0, 0)),
                pl.BlockSpec((rows, 2 * WIDE), lambda i, ids: (0, 0)),
            ],
            scratch_shapes=[
                pltpu.VMEM((2 * rows // TILE, NARROW, TILE), BF),
                pltpu.VMEM((NARROW, TILE), F32),
                pltpu.VMEM((2 * rows, WIDE), F32),
                pltpu.VMEM((2 * rows, WIDE), F32),
            ],
        ),
        out_shape=[
            jax.ShapeDtypeStruct((rows, WIDE), BF),
            jax.ShapeDtypeStruct((rows, 2 * WIDE), F32),
            jax.ShapeDtypeStruct((rows, 2 * WIDE), BF),
        ],
        cost_estimate=cost(
            10 * OWN_HEADS * WIDE * rows * 2 * rows, queries, kv_own, kv_other, queries
        ),
        name="attend_back",
    )(ids, row_ids, col_ids, queries, upstream, attended, logs, kv_own, kv_other, cosine, sine)


def grad_qkv_kernel(
    c_ref, x_ref, dq_ref, own_ref, got_ref, cos_ref, sin_ref, vectors_ref,
    out_ref, keep_ref, away_ref, acc_ref,
):
    tile = pl.program_id(0)
    total = own_ref[...] + got_ref[...].astype(F32)
    keys = total[:, :WIDE]
    keys = keys * doubled(cos_ref[...]) - turned(keys) * doubled(sin_ref[...])
    grads = jnp.concatenate(
        [dq_ref[...], keys.astype(BF), total[:, WIDE:].astype(BF)], axis=1
    )
    out_ref[...] = grads
    part = contract(x_ref[...], grads, 0, 0)

    @pl.when(tile == 0)
    def _():
        acc_ref[...] = part

    @pl.when(tile > 0)
    def _():
        acc_ref[...] += part

    @pl.when(tile == pl.num_programs(0) - 1)
    def _():
        rows = keep_ref.shape[0]
        core = c_ref[0]
        keep_ref[...] = acc_ref[pl.ds(pl.multiple_of(core * rows, 8), rows), :]
        away_ref[:rows] = acc_ref[pl.ds(pl.multiple_of((1 - core) * rows, 8), rows), :].astype(BF)
        away_ref[rows:] = jnp.zeros((16, away_ref.shape[1]), BF)
        away_ref[rows : rows + 8] = vectors_ref[...].astype(BF)


def grad_qkv(core, x_rows, grad_queries, own, got, cosine, sine, vectors):
    rows = grad_queries.shape[0]
    tiled = lambda width: pl.BlockSpec((TILE, width), lambda i, c: (i, 0))
    whole = lambda *shape: pl.BlockSpec(shape, lambda i, c: (0, 0))
    return pl.pallas_call(
        grad_qkv_kernel,
        grid_spec=pltpu.PrefetchScalarGridSpec(
            num_scalar_prefetch=1,
            grid=(rows // TILE,),
            in_specs=[
                tiled(D), tiled(WIDE), tiled(2 * WIDE), tiled(2 * WIDE), tiled(LANES),
                tiled(LANES), whole(*vectors.shape),
            ],
            out_specs=[tiled(3 * WIDE), whole(D // 2, 3 * WIDE), whole(D // 2 + 16, 3 * WIDE)],
            scratch_shapes=[pltpu.VMEM((D, 3 * WIDE), F32)],
        ),
        out_shape=[
            jax.ShapeDtypeStruct((rows, 3 * WIDE), BF),
            jax.ShapeDtypeStruct((D // 2, 3 * WIDE), F32),
            jax.ShapeDtypeStruct((D // 2 + 16, 3 * WIDE), BF),
        ],
        cost_estimate=cost(2 * rows * D * 3 * WIDE, own, own, got, grad_queries),
        name="grad_qkv",
    )(core, x_rows, grad_queries, own, got, cosine, sine, vectors)


def after(value, *others):
    return lax.optimization_barrier((value,) + others)[0]


def join(*values):
    return lax.optimization_barrier(values)


def pack_qkv_kernel(target_ref, w_ref, vectors_ref, *refs):
    packed = refs[-1]
    for target in range(GROUP):
        for part in range(3):
            start = part * D + target * NARROW
            packed[target, :, part * NARROW : (part + 1) * NARROW] = w_ref[
                :, start : start + NARROW
            ]
        packed[target, :, 3 * NARROW :] = vectors_ref[...]
    for index, ref in enumerate(refs[:-1]):
        ref[...] = packed[target_ref[index]]


def pack_qkv(targets, w_qkv, vectors):
    rows = w_qkv.shape[0]
    width = 3 * NARROW + vectors.shape[1]
    return pl.pallas_call(
        pack_qkv_kernel,
        in_specs=[
            pl.BlockSpec(memory_space=pltpu.SMEM),
            pl.BlockSpec(memory_space=pltpu.VMEM),
            pl.BlockSpec(memory_space=pltpu.VMEM),
        ],
        out_specs=[pl.BlockSpec(memory_space=pltpu.VMEM)] * 2,
        out_shape=[jax.ShapeDtypeStruct((rows, width), BF)] * 2,
        scratch_shapes=[pltpu.VMEM((GROUP, rows, width), BF)],
        name="pack_qkv",
    )(targets, w_qkv, vectors)


def pack_gate_up_kernel(target_ref, gate_ref, up_ref, *refs):
    packed = refs[-1]
    width = packed.shape[2] // 4
    for target in range(GROUP):
        for index in range(4):
            source = (gate_ref, up_ref)[index // 2]
            start = (index % 2 * GROUP + target) * width
            packed[target, :, index * width : (index + 1) * width] = source[
                :, start : start + width
            ]
    for index, ref in enumerate(refs[:-1]):
        ref[...] = packed[target_ref[index]]


def pack_gate_up(targets, w_gate, w_up):
    rows = w_gate.shape[0]
    width = 2 * w_gate.shape[1] // GROUP
    return pl.pallas_call(
        pack_gate_up_kernel,
        in_specs=[
            pl.BlockSpec(memory_space=pltpu.SMEM),
            pl.BlockSpec(memory_space=pltpu.VMEM),
            pl.BlockSpec(memory_space=pltpu.VMEM),
        ],
        out_specs=[pl.BlockSpec(memory_space=pltpu.VMEM)] * 2,
        out_shape=[jax.ShapeDtypeStruct((rows, width), BF)] * 2,
        scratch_shapes=[pltpu.VMEM((GROUP, rows, width), BF)],
        name="pack_gate_up",
    )(targets, w_gate, w_up)


def unpack_qkv_kernel(place_ref, near_ref, far_ref, out_ref, vectors_ref):
    zeros = jnp.zeros((near_ref.shape[1], WIDE - NARROW), BF)
    for index in range(2 * GROUP):
        source = (near_ref, far_ref)[index // GROUP]
        place = place_ref[index]
        for part in range(3):
            out_ref[place, :, part * WIDE : part * WIDE + NARROW] = source[
                index % GROUP, :, part * NARROW : (part + 1) * NARROW
            ]
            out_ref[place, :, part * WIDE + NARROW : (part + 1) * WIDE] = zeros
        vectors_ref[place] = source[index % GROUP, :, 3 * NARROW :]


def unpack_qkv(places, near, far):
    _, rows, width = near.shape
    return pl.pallas_call(
        unpack_qkv_kernel,
        in_specs=[
            pl.BlockSpec(memory_space=pltpu.SMEM),
            pl.BlockSpec(memory_space=pltpu.VMEM),
            pl.BlockSpec(memory_space=pltpu.VMEM),
        ],
        out_specs=[pl.BlockSpec(memory_space=pltpu.VMEM)] * 2,
        out_shape=[
            jax.ShapeDtypeStruct((2 * GROUP, rows, 3 * WIDE), BF),
            jax.ShapeDtypeStruct((2 * GROUP, rows, width - 3 * NARROW), BF),
        ],
        name="unpack_qkv",
    )(places, near, far)


def unpack_kernel(place_ref, near_ref, far_ref, out_ref):
    for index in range(2 * GROUP):
        out_ref[place_ref[index]] = (near_ref, far_ref)[index // GROUP][index % GROUP]


def unpack(places, near, far):
    count, rows, width = near.shape
    return pl.pallas_call(
        unpack_kernel,
        in_specs=[
            pl.BlockSpec(memory_space=pltpu.SMEM),
            pl.BlockSpec(memory_space=pltpu.VMEM),
            pl.BlockSpec(memory_space=pltpu.VMEM),
        ],
        out_specs=pl.BlockSpec(memory_space=pltpu.VMEM),
        out_shape=jax.ShapeDtypeStruct((2 * count, rows, width), BF),
        name="unpack",
    )(places, near, far)


def split_feed_kernel(x_ref, down_ref, down_got_ref, gate_up_ref, gate_up_got_ref, keep_ref, away_ref):
    mine = x_ref[0]
    width = down_ref.shape[-1]
    for block in range(GROUP):
        for side, ref in ((mine, keep_ref), (1 - mine, away_ref)):
            ref[block] = (
                down_ref[block, side] + down_got_ref[block, side].astype(F32)
            ).astype(BF)
            total = gate_up_ref[block, side] + gate_up_got_ref[block, side].astype(F32)
            ref[GROUP + block] = total[:, :width].astype(BF)
            ref[2 * GROUP + block] = total[:, width:].astype(BF)


def whole_call(kernel, name, shapes, scalars, *arrays):
    return pl.pallas_call(
        kernel,
        in_specs=[pl.BlockSpec(memory_space=pltpu.SMEM)]
        + [pl.BlockSpec(memory_space=pltpu.VMEM)] * len(arrays),
        out_specs=[pl.BlockSpec(memory_space=pltpu.VMEM)] * len(shapes),
        out_shape=[jax.ShapeDtypeStruct(shape, dtype) for shape, dtype in shapes],
        cost_estimate=cost(sum(a.size for a in arrays), *arrays, *arrays),
        name=name,
    )(scalars, *arrays)


def square_feed_kernel(index_ref, mine_ref, got_ref, kept_ref, *send_refs):
    for k in range(GROUP):
        target = index_ref[k]
        for part in range(2):
            slot = (part + 1) * GROUP + target
            block = mine_ref[slot] + got_ref[slot]
            if k == 0:
                kept_ref[GROUP + part] = block
            else:
                send_refs[k - 1][part] = block
        kept_ref[k] = mine_ref[k] + got_ref[k]


def join_feed_kernel(index_ref, kept_ref, *refs):
    out_ref = refs[-1]
    for k in range(GROUP):
        out_ref[k] = kept_ref[k]
        for part in range(2):
            slot = (part + 1) * GROUP + index_ref[k]
            out_ref[slot] = kept_ref[GROUP + part] if k == 0 else refs[k - 1][part]


def finish_feed_kernel(flag_ref, own_ref, other_ref, far_own_ref, far_other_ref, down_ref, gate_ref, up_ref):
    mine, at_home = flag_ref[0], flag_ref[1] == 1
    rows = own_ref.shape[1]
    half = own_ref.shape[2] // 2
    for slot in range(3 * GROUP):
        for near, far, side in ((own_ref, far_own_ref, mine), (other_ref, far_other_ref, 1 - mine)):
            block = jnp.where(at_home, near[slot], far[slot]).astype(F32)
            if slot < GROUP:
                down_ref[slot, side] = block
            else:
                ref = gate_ref if slot < 2 * GROUP else up_ref
                start = slot % GROUP * half
                width = GROUP * half
                ref[side, :, start : start + half] = block[:, :half]
                ref[side, :, width + start : width + start + half] = block[:, half:]


def split_x_kernel(flag_ref, part_ref, vectors_ref, got_ref, keep_ref, away_ref):
    mine = flag_ref[0]
    rows = part_ref.shape[0]
    step = rows // (2 * GROUP)
    for block in range(GROUP):
        for side, ref in ((mine, keep_ref), (1 - mine, away_ref)):
            place = pl.ds(pl.multiple_of((2 * block + side) * step, step), step)
            ref[block * step : (block + 1) * step] = (
                part_ref[place] + got_ref[place].astype(F32)
            ).astype(BF)
    for ref in (keep_ref, away_ref):
        ref[GROUP * step :] = got_ref[rows:]
        ref[GROUP * step : GROUP * step + 8] = (
            vectors_ref[...] + got_ref[rows : rows + 8].astype(F32)
        ).astype(BF)


def square_qkv_kernel(index_ref, mine_ref, got_ref, *refs):
    step = (mine_ref.shape[0] - 16) // GROUP
    vectors = mine_ref[GROUP * step :] + got_ref[GROUP * step :]
    for k in range(GROUP):
        place = pl.ds(pl.multiple_of(index_ref[k] * step, step), step)
        refs[k][:step] = mine_ref[place] + got_ref[place]
        refs[k][step:] = vectors


def join_qkv_kernel(index_ref, *refs):
    out_ref = refs[-1]
    step = refs[0].shape[0] - 16
    vectors = refs[0][step:].astype(F32)
    for k in range(GROUP):
        place = pl.ds(pl.multiple_of(index_ref[k] * step, step), step)
        out_ref[place] = refs[k][:step]
        if k:
            vectors += refs[k][step:].astype(F32)
    out_ref[GROUP * step :] = vectors.astype(BF)


def finish_qkv_kernel(flag_ref, own_ref, other_ref, far_own_ref, far_other_ref, out_ref, vectors_ref):
    mine, at_home = flag_ref[0], flag_ref[1] == 1
    step = (own_ref.shape[0] - 16) // GROUP
    for block in range(GROUP):
        rows = slice(block * step, (block + 1) * step)
        for near, far, side in ((own_ref, far_own_ref, mine), (other_ref, far_other_ref, 1 - mine)):
            values = jnp.where(at_home, near[rows], far[rows]).astype(F32)
            for part in range(3):
                start = part * D + block * NARROW
                out_ref[side, :, start : start + NARROW] = values[
                    :, part * WIDE : part * WIDE + NARROW
                ]
    rows = slice(GROUP * step, GROUP * step + 8)
    vectors_ref[...] = jnp.where(at_home, own_ref[rows], far_own_ref[rows]).astype(F32)


def gather_square(block):
    return [block] + [send(block, SQUARE[k]) for k in range(1, GROUP)]


def square_parts(left, weight, weight_dim):
    return [
        contract(left[k * TILE : (k + 1) * TILE], weight, 1, weight_dim).astype(BF)
        for k in range(1, GROUP)
    ]


def reduce_square(left, weight, weight_dim, parts=None):
    if parts is None:
        parts = square_parts(left, weight, weight_dim)
    got = [send(part, SQUARE[k + 1]) for k, part in enumerate(parts)]
    (total,) = join(contract(left[:TILE], weight, 1, weight_dim))
    for part in got:
        total = total + part.astype(F32)
    return total


def per_device_clustered(
    tokens_in,
    segment_ids,
    w_qkv,
    w_out,
    ln1_gain,
    ln1_bias,
    w_gate,
    w_up,
    w_down,
    ln2_gain,
    ln2_bias,
    out_cotangent,
):
    rep = lax.axis_index("rep")
    shard = lax.axis_index("shard")
    x, c = rep // 2, rep % 2
    h, j = shard // 4, shard % 4
    core_is_one = c == 1
    half_is_one = h == 1
    x_is_one = x == 1
    at_home = c == h
    token_count = tokens_in.shape[1]
    length = segment_ids.shape[1]
    rows_d = w_qkv.shape[0]
    rows_f = w_down.shape[0]
    slice_f = 2 * rows_f
    group_rows = GROUP * token_count

    inputs_bf = send(tokens_in.reshape(token_count, D), SPREAD)
    doc_ids = send(segment_ids, SPREAD).reshape(2, GROUP, token_count)

    by_x = jnp.stack([2 * x, 2 * x + 1, 2 - 2 * x, 3 - 2 * x]) ^ j
    targets = by_x[:2]
    places = jnp.concatenate([GROUP * (h ^ c) + by_x, GROUP * (1 - (h ^ c)) + by_x])

    out_got = send(w_out, OUT_FETCH)
    vectors = jnp.stack([ln1_gain, ln1_bias, ln2_gain, ln2_bias], axis=1)
    qkv_packed = pack_qkv(targets, w_qkv, vectors)
    qkv_mine = after(
        jnp.stack([send(part, ROUND[i]) for i, part in enumerate(qkv_packed)]), inputs_bf
    )
    x_tiles = gather_square(inputs_bf)
    qkv_second = send(qkv_mine, OTHER_X)
    qkv_near = jnp.concatenate([qkv_mine, qkv_second], axis=0)
    qkv_second, w_gate, w_up, down_whole, doc_ids, j = join(
        qkv_second, w_gate, w_up, w_down, doc_ids, j
    )
    qkv_far = send(qkv_near, OTHER_CORE)
    qkv_own, vectors_got = unpack_qkv(places, qkv_near, qkv_far)
    qkv_own = qkv_own.reshape(D, 3 * WIDE)
    qkv_own, *x_tiles = join(qkv_own, *x_tiles)
    x_rows = jnp.concatenate(x_tiles, axis=0)

    tile_index = j ^ jnp.arange(GROUP, dtype=jnp.int32)
    first_row = (c * GROUP + tile_index) * token_count
    positions = (
        first_row[:, None] + jnp.arange(token_count, dtype=jnp.int32)[None, :]
    ).reshape(group_rows).astype(F32)
    middle = HEAD_DIM // 2
    exponents = jnp.arange(128, dtype=jnp.int32) % middle
    inverse = rope_base ** (-(2.0 * exponents.astype(F32)) / HEAD_DIM)
    angles = positions[:, None] * inverse[None, :]
    cosine, sine = jnp.cos(angles), jnp.sin(angles)
    mixed = jnp.stack(unmix([doc_ids[:, k] for k in range(GROUP)], j), axis=1)
    ids = jnp.concatenate(
        [pick(core_is_one, mixed[0], mixed[1]), pick(core_is_one, mixed[1], mixed[0])], axis=0
    )
    flat_ids = ids.reshape(length)
    row_ids = ids.reshape(length // TILE, 1, TILE)
    col_ids = flat_ids[:, None]

    part_f = rows_f // 4
    gate_up_packed = pack_gate_up(targets, w_gate, w_up)
    down_sent = lax.dynamic_slice_in_dim(down_whole, (2 * c + x) * part_f, part_f, 0)
    down_mine = send(down_sent, OTHER_HALF)
    (
        x_rows, qkv_own, vectors_got, out_got, flat_ids, row_ids, col_ids, cosine, sine, down_mine,
        *gate_up_packed,
    ) = join(
        x_rows, qkv_own, vectors_got, out_got, flat_ids, row_ids, col_ids, cosine, sine, down_mine,
        *gate_up_packed,
    )

    queries, kv_own = project(x_rows, qkv_own, cosine, sine)
    kv_other = send(kv_own, OTHER_CORE)
    out_other = send(out_got, OTHER_CORE)
    kv_other, out_other, *gate_up_packed = join(kv_other, out_other, *gate_up_packed)
    attended, logs = attend(flat_ids, row_ids, col_ids, queries, kv_own, kv_other)
    gate_up_first = [send(part, ROUND[i]) for i, part in enumerate(gate_up_packed)]
    attended, logs, *gate_up_first = join(attended, logs, *gate_up_first)
    out_own = jnp.concatenate(
        [
            pick(core_is_one, out_got, out_other),
            pick(core_is_one, out_other, out_got),
            jnp.zeros((WIDE - NARROW, D), BF),
        ],
        axis=0,
    )

    branch_parts = square_parts(attended, out_own, 0)
    gate_up_mine, down_mine, *branch_parts = join(
        jnp.stack(gate_up_first), down_mine, *branch_parts
    )
    gate_up_second = send(gate_up_mine, OTHER_X)
    down_got = send(down_mine, OTHER_X)
    branch = reduce_square(attended, out_own, 0, branch_parts)
    vectors_full = jnp.transpose(vectors_got.reshape(D, 4)).astype(F32)
    gain_one, bias_one, gain_two, bias_two = (vectors_full[i] for i in range(4))
    first_out, first_normed, first_scale = norm_forward(
        inputs_bf.astype(F32) + branch, gain_one, bias_one
    )
    first_bf, gate_up_second, down_got, out_cotangent = join(
        first_out.astype(BF), gate_up_second, down_got, out_cotangent
    )

    first_tiles = gather_square(first_bf)
    gate_up_near = jnp.concatenate([gate_up_mine, gate_up_second], axis=0)
    gate_up_far = send(gate_up_near, OTHER_CORE)
    gate_up_own = unpack(places, gate_up_near, gate_up_far).reshape(D, 2 * slice_f)
    down_got = after(down_got, first_tiles[1])
    down_pair = jnp.concatenate(
        [pick(x_is_one, down_mine, down_got), pick(x_is_one, down_got, down_mine)], axis=0
    )
    down_other = send(down_pair, OTHER_CORE)
    down_far = jnp.concatenate(
        [pick(core_is_one, down_pair, down_other), pick(core_is_one, down_other, down_pair)], axis=0
    )
    down_own = jnp.concatenate(
        [pick(half_is_one, w_down, down_far), pick(half_is_one, down_far, w_down)], axis=0
    )
    first_rows = jnp.concatenate(first_tiles, axis=0)
    acts = contract(first_rows, gate_up_own, 1, 0)
    gate_act, up_act = acts[:, :slice_f], acts[:, slice_f:]
    hidden_bf = (jax.nn.silu(gate_act) * up_act).astype(BF)
    cotangent = send(after(out_cotangent, hidden_bf).reshape(token_count, D), SPREAD)
    down_act = reduce_square(hidden_bf, down_own, 0)
    result, second_normed, second_scale = norm_forward(first_out + down_act, gain_two, bias_two)

    upstream = cotangent.astype(F32)
    grad_gain_two = jnp.sum(upstream * second_normed, axis=0, keepdims=True)
    grad_bias_two = jnp.sum(upstream, axis=0, keepdims=True)
    grad_second = norm_backward(upstream, second_normed, second_scale, gain_two)
    grad_down_rows = jnp.concatenate(gather_square(grad_second.astype(BF)), axis=0)
    grad_hidden = contract(grad_down_rows, down_own, 1, 1)
    sigmoid_gate = jax.nn.sigmoid(gate_act)
    grad_gate_bf = (
        grad_hidden * up_act * sigmoid_gate * (1.0 + gate_act * (1.0 - sigmoid_gate))
    ).astype(BF)
    grad_up_bf = (grad_hidden * (gate_act * sigmoid_gate)).astype(BF)
    grad_acts = jnp.concatenate([grad_gate_bf, grad_up_bf], axis=1)
    first_parts = square_parts(grad_acts, gate_up_own, 1)

    quarter = rows_d // 2
    step_square = jnp.arange(GROUP, dtype=jnp.int32) ^ j
    x_flag = x.reshape(1)
    home_flags = jnp.stack([x, at_home.astype(jnp.int32)])

    def over_cores(partial):
        keep = pick(core_is_one, partial[0], partial[1])
        away = pick(core_is_one, partial[1], partial[0])
        return keep, send(away.astype(BF), OTHER_CORE)

    by_x_rows = (GROUP, 2, quarter)
    gate_up_keep, gate_up_got = over_cores(
        contract(first_rows, after(grad_acts, *first_parts), 0, 0).reshape(
            2, D // 2, 2 * slice_f
        )
    )
    down_keep, down_got = over_cores(
        contract(hidden_bf, after(grad_down_rows, *first_parts), 0, 0).reshape(2, rows_f, D)
    )
    bundle_shape = ((3 * GROUP, quarter, D), BF)
    grad_first = grad_second + reduce_square(grad_acts, gate_up_own, 1, first_parts)
    grad_gain_one = jnp.sum(grad_first * first_normed, axis=0, keepdims=True)
    grad_bias_one = jnp.sum(grad_first, axis=0, keepdims=True)
    grad_res = norm_backward(grad_first, first_normed, first_scale, gain_one)
    grad_res_bf, down_got, gate_up_got = join(grad_res.astype(BF), down_got, gate_up_got)
    grad_branch_tiles = gather_square(grad_res_bf)
    feed_keep, feed_away = whole_call(
        split_feed_kernel, "split_feed", [bundle_shape] * 2, x_flag,
        down_keep.reshape(by_x_rows + (D,)), down_got.reshape(by_x_rows + (D,)),
        gate_up_keep.reshape(by_x_rows + (2 * slice_f,)),
        gate_up_got.reshape(by_x_rows + (2 * slice_f,)),
    )
    feed_got = send(feed_away, OTHER_X)

    grad_branch_rows = jnp.concatenate(grad_branch_tiles, axis=0)
    grad_attended = contract(grad_branch_rows, out_own, 1, 1).astype(BF)
    out_keep, out_got = over_cores(
        contract(attended, grad_branch_rows, 0, 0)[:NARROW].reshape(2, rows_d, D)
    )
    grad_attended, out_got = join(grad_attended, out_got)
    out_total = (out_keep + out_got.astype(F32)).astype(BF)
    grad_attended, out_total, result_bf = join(grad_attended, out_total, result.astype(BF))
    grad_queries, kv_grad_own, kv_grad_away = attend_back(
        flat_ids, row_ids, col_ids, queries, grad_attended, attended, logs, kv_own, kv_other,
        cosine, sine,
    )
    out_far = send(out_total, OTHER_X)
    result_home = send(result_bf, SPREAD)
    vector_part = jnp.concatenate(
        [grad_gain_one, grad_bias_one, grad_gain_two, grad_bias_two]
        + [jnp.zeros((4, D), F32)], axis=0
    )
    grad_queries, kv_grad_own, kv_grad_away, feed_got, out_far, result_home = join(
        grad_queries, kv_grad_own, kv_grad_away, feed_got, out_far, result_home
    )
    kv_grad_got = send(kv_grad_away, OTHER_CORE)
    feed_mine = feed_keep + feed_got
    out_total = (out_total.astype(F32) + out_far.astype(F32)).astype(BF)
    kv_grad_got, feed_mine, out_total = join(kv_grad_got, feed_mine, out_total)
    feed_home = send(feed_mine, HOME_HALF)
    out_got = send(out_total, OTHER_HALF)

    grad_projected, qkv_keep, qkv_away = grad_qkv(
        c.reshape(1), x_rows, grad_queries, kv_grad_own, kv_grad_got, cosine, sine, vector_part
    )
    moved_rows = D // 4 + 16
    qkv_got = send(qkv_away, OTHER_CORE)
    input_parts = square_parts(grad_projected, qkv_own, 1)
    qkv_got, *input_parts = join(qkv_got, *input_parts)

    input_sum = reduce_square(grad_projected, qkv_own, 1, input_parts)
    qkv_keep, qkv_away = whole_call(
        split_x_kernel, "split_x", [((moved_rows, 3 * WIDE), BF)] * 2, x_flag,
        qkv_keep, vector_part, qkv_got,
    )
    qkv_mine, feed_home = join(qkv_keep + send(qkv_away, OTHER_X), feed_home)
    qkv_home = send(qkv_mine, HOME_HALF)
    feed_kept, *feed_sends = whole_call(
        square_feed_kernel, "square_feed",
        [((GROUP + 2, quarter, D), BF)] + [((2, quarter, D), BF)] * 3,
        step_square, feed_mine, feed_home,
    )
    feed_gots = [send(part, HOME_SQUARE[k + 1]) for k, part in enumerate(feed_sends)]
    inputs_back, qkv_home, out_got, *feed_gots = join(
        (grad_res + input_sum).astype(BF), qkv_home, out_got, *feed_gots
    )
    grad_inputs_home = send(inputs_back, SPREAD)
    grad_w_out = send(out_total + out_got, OUT_RETURN)
    qkv_sends = whole_call(
        square_qkv_kernel, "square_qkv", [((quarter + 16, 3 * WIDE), BF)] * GROUP,
        step_square, qkv_mine, qkv_home,
    )
    feed_kept, *qkv_sends = join(feed_kept, *qkv_sends)
    qkv_gots = [qkv_sends[0]] + [send(qkv_sends[k], HOME_SQUARE[k]) for k in range(1, GROUP)]
    (feed_bundle,) = whole_call(
        join_feed_kernel, "join_feed", [bundle_shape], step_square, feed_kept, *feed_gots
    )
    feed_other = send(feed_bundle, HOME_X)
    feed_far = send(feed_bundle, OTHER_CORE)
    grad_inputs_home, grad_w_out, feed_other, feed_far, *qkv_gots = join(
        grad_inputs_home, grad_w_out, feed_other, feed_far, *qkv_gots
    )
    feed_far_other = send(feed_other, OTHER_CORE)
    grad_w_down, grad_w_gate, grad_w_up = whole_call(
        finish_feed_kernel, "finish_feed",
        [(by_x_rows + (D,), F32)] + [((2, quarter, w_gate.shape[1]), F32)] * 2,
        home_flags, feed_bundle, feed_other, feed_far, feed_far_other,
    )
    (qkv_bundle,) = whole_call(
        join_qkv_kernel, "join_qkv", [((moved_rows, 3 * WIDE), BF)], step_square, *qkv_gots
    )
    qkv_other, grad_w_down, grad_w_gate, grad_w_up = join(
        send(qkv_bundle, HOME_X), grad_w_down, grad_w_gate, grad_w_up
    )
    grad_w_qkv, vector_grads = whole_call(
        finish_qkv_kernel, "finish_qkv", [((2, quarter, 3 * D), F32), ((8, D), F32)],
        home_flags, qkv_bundle, qkv_other, send(qkv_bundle, OTHER_CORE), send(qkv_other, OTHER_CORE),
    )
    vector_grads = lax.dynamic_slice_in_dim(vector_grads, shard * rows_d, rows_d, 1)

    return (
        result_home.reshape(tokens_in.shape),
        grad_inputs_home.astype(F32).reshape(tokens_in.shape),
        grad_w_qkv.reshape(w_qkv.shape),
        grad_w_out.astype(F32),
        vector_grads[0],
        vector_grads[1],
        grad_w_gate.reshape(w_gate.shape),
        grad_w_up.reshape(w_up.shape),
        grad_w_down.reshape(w_down.shape),
        vector_grads[2],
        vector_grads[3],
    )


def solution(mesh):
    sizes = dict(mesh.shape)
    clustered = (sizes["rep"], sizes["shard"]) == (4, 8)
    plan = per_device_clustered if clustered else per_device
    return jax.shard_map(
        plan,
        mesh=mesh,
        in_specs=(
            P("rep", "shard", None),
            P("rep", None),
            P("shard", None),
            P("shard", None),
            P("shard"),
            P("shard"),
            P("shard", None),
            P("shard", None),
            P("shard", None),
            P("shard"),
            P("shard"),
            P("rep", "shard", None),
        ),
        out_specs=(
            P("rep", "shard", None),
            P("rep", "shard", None),
            P("shard", None),
            P("shard", None),
            P("shard"),
            P("shard"),
            P("shard", None),
            P("shard", None),
            P("shard", None),
            P("shard"),
            P("shard"),
        ),
        check_vma=False,
    )
```

```python
import math

import jax
import jax.numpy as jnp
from jax import lax
from jax.experimental import pallas as pl
from jax.experimental.pallas import tpu as pltpu
from jax.sharding import PartitionSpec as P

D = 768
HEAD_DIM = 64
HEADS = 12


epsilon = 1e-05
rope_base = 1000.0


def rope_tables(start, count):
    positions = (start + jnp.arange(count, dtype=jnp.int32)).astype(jnp.float32)
    middle = HEAD_DIM // 2
    inverse = rope_base ** (-(2.0 * jnp.arange(middle).astype(jnp.float32)) / HEAD_DIM)
    angles = positions[:, None] * inverse[None, :]
    return (jnp.cos(angles)[:, None, :], jnp.sin(angles)[:, None, :])


def rotate(values_in, cosine, sine):
    middle = values_in.shape[-1] // 2
    first_half = values_in[..., :middle]
    second_half = values_in[..., middle:]
    return jnp.concatenate(
        [first_half * cosine - second_half * sine, second_half * cosine + first_half * sine],
        axis=-1,
    )


def rotate_back(upstream, cosine, sine):
    middle = upstream.shape[-1] // 2
    first_half = upstream[..., :middle]
    second_half = upstream[..., middle:]
    return jnp.concatenate(
        [first_half * cosine + second_half * sine, second_half * cosine - first_half * sine],
        axis=-1,
    )


def norm_forward(values_in, gain_vec, shift_vec):
    centred = values_in - jnp.mean(values_in, axis=-1, keepdims=True)
    variance = jnp.mean(centred * centred, axis=-1, keepdims=True)
    inverse_scale = lax.rsqrt(variance + epsilon)
    normed = centred * inverse_scale
    return (normed * gain_vec + shift_vec, normed, inverse_scale)


def norm_backward(upstream, normed, inverse_scale, gain_vec):
    scaled = upstream * gain_vec
    return inverse_scale * (
        scaled
        - jnp.mean(scaled, axis=-1, keepdims=True)
        - normed * jnp.mean(scaled * normed, axis=-1, keepdims=True)
    )


def fetch_attention(w_qkv, w_out, ln1_gain, ln1_bias):
    return (
        lax.all_gather(w_qkv, "shard", axis=0, tiled=True),
        lax.all_gather(w_out, "shard", axis=0, tiled=True),
        lax.all_gather(ln1_gain, "shard", axis=0, tiled=True),
        lax.all_gather(ln1_bias, "shard", axis=0, tiled=True),
    )


def fetch_feedforward(w_gate, w_up, w_down, ln2_gain, ln2_bias):
    return (
        lax.all_gather(w_gate, "shard", axis=0, tiled=True),
        lax.all_gather(w_up, "shard", axis=0, tiled=True),
        lax.all_gather(w_down, "shard", axis=0, tiled=True),
        lax.all_gather(ln2_gain, "shard", axis=0, tiled=True),
        lax.all_gather(ln2_bias, "shard", axis=0, tiled=True),
    )


def pair_columns(matrix, pair_index):
    width = 2 * HEAD_DIM
    return lax.dynamic_slice_in_dim(matrix, pair_index * width, width, 1).reshape(
        matrix.shape[0], 2, HEAD_DIM
    )


def pair_scores(pair_index, queries, key_rows, same_doc):
    scores = jnp.einsum(
        "qhd,khd->hqk",
        pair_columns(queries, pair_index),
        pair_columns(key_rows, pair_index),
        preferred_element_type=jnp.float32,
    ) * HEAD_DIM ** (-0.5)
    return jnp.where(same_doc[None], scores, -jnp.inf)


def attention_forward(queries, key_rows, value_rows, same_doc):

    def one_pair(pair_index):
        scores = pair_scores(pair_index, queries, key_rows, same_doc)
        row_max = jnp.max(scores, axis=-1, keepdims=True)
        expons = jnp.exp(scores - row_max)
        row_total = jnp.sum(expons, axis=-1, keepdims=True)
        weights_bf = (expons / row_total).astype(jnp.bfloat16)
        attended = jnp.einsum(
            "hqk,khd->qhd",
            weights_bf,
            pair_columns(value_rows, pair_index),
            preferred_element_type=jnp.float32,
        )
        return (
            attended.reshape(attended.shape[0], 2 * HEAD_DIM),
            (row_max + jnp.log(row_total))[..., 0],
        )

    attended, log_totals = lax.map(one_pair, jnp.arange(HEADS // 2, dtype=jnp.int32))
    return (jnp.transpose(attended, (1, 0, 2)).reshape(queries.shape[0], D), log_totals)


def attention_backward(queries, key_rows, value_rows, grad_attended, log_totals, same_doc):
    scale_factor = HEAD_DIM ** (-0.5)
    width = 2 * HEAD_DIM

    def one_pair(inputs):
        pair_index, pair_logs = inputs
        scores = pair_scores(pair_index, queries, key_rows, same_doc)
        weights = jnp.exp(scores - pair_logs[..., None])
        grad_pair = pair_columns(grad_attended, pair_index)
        grad_weights = jnp.einsum(
            "qhd,khd->hqk",
            grad_pair,
            pair_columns(value_rows, pair_index),
            preferred_element_type=jnp.float32,
        )
        row_delta = jnp.sum(weights * grad_weights, axis=-1, keepdims=True)
        grad_scores = (weights * (grad_weights - row_delta)).astype(jnp.bfloat16)
        grad_query = (
            jnp.einsum(
                "hqk,khd->qhd",
                grad_scores,
                pair_columns(key_rows, pair_index),
                preferred_element_type=jnp.float32,
            )
            * scale_factor
        )
        grad_key = (
            jnp.einsum(
                "hqk,qhd->khd",
                grad_scores,
                pair_columns(queries, pair_index),
                preferred_element_type=jnp.float32,
            )
            * scale_factor
        )
        grad_value = jnp.einsum(
            "hqk,qhd->khd",
            weights.astype(jnp.bfloat16),
            grad_pair,
            preferred_element_type=jnp.float32,
        )
        return (
            grad_query.reshape(-1, width),
            grad_key.reshape(-1, width),
            grad_value.reshape(-1, width),
        )

    pair_grads = lax.map(one_pair, (jnp.arange(HEADS // 2, dtype=jnp.int32), log_totals))
    return tuple(
        (
            jnp.transpose(pair_part, (1, 0, 2)).reshape(pair_part.shape[1], D)
            for pair_part in pair_grads
        )
    )


def per_device(
    tokens_in,
    segment_ids,
    w_qkv,
    w_out,
    ln1_gain,
    ln1_bias,
    w_gate,
    w_up,
    w_down,
    ln2_gain,
    ln2_bias,
    out_cotangent,
):
    inputs_bf = tokens_in.reshape(-1, D)
    token_count = inputs_bf.shape[0]
    doc_ids = segment_ids.reshape(-1)
    start = lax.axis_index("shard") * token_count
    own_docs = lax.dynamic_slice_in_dim(doc_ids, start, token_count)
    same_doc = own_docs[:, None] == doc_ids[None, :]
    cosine, sine = rope_tables(start, token_count)
    heads_shape = (token_count, HEADS, HEAD_DIM)
    qkv_full, out_full, gain_one, bias_one = fetch_attention(w_qkv, w_out, ln1_gain, ln1_bias)
    projected = jnp.dot(inputs_bf, qkv_full, preferred_element_type=jnp.float32)
    queries = (
        rotate(projected[:, :D].reshape(heads_shape), cosine, sine)
        .reshape(token_count, D)
        .astype(jnp.bfloat16)
    )
    own_keys = (
        rotate(projected[:, D : 2 * D].reshape(heads_shape), cosine, sine)
        .reshape(token_count, D)
        .astype(jnp.bfloat16)
    )
    own_values = projected[:, 2 * D :].astype(jnp.bfloat16)
    key_rows, value_rows = (
        lax.all_gather(own_keys, "shard", axis=0, tiled=True),
        lax.all_gather(own_values, "shard", axis=0, tiled=True),
    )
    attended, log_totals = attention_forward(queries, key_rows, value_rows, same_doc)
    attended_bf = attended.astype(jnp.bfloat16)
    branch = jnp.dot(attended_bf, out_full, preferred_element_type=jnp.float32)
    inputs_f = inputs_bf.astype(jnp.float32)
    first_out, first_normed, first_scale = norm_forward(
        inputs_f + branch, gain_one.astype(jnp.float32), bias_one.astype(jnp.float32)
    )
    gate_full, up_full, down_full, gain_two, bias_two = fetch_feedforward(
        w_gate, w_up, w_down, ln2_gain, ln2_bias
    )
    first_bf = first_out.astype(jnp.bfloat16)
    gate_act = jnp.dot(first_bf, gate_full, preferred_element_type=jnp.float32)
    up_act = jnp.dot(first_bf, up_full, preferred_element_type=jnp.float32)
    hidden_bf = (jax.nn.silu(gate_act) * up_act).astype(jnp.bfloat16)
    down_act = jnp.dot(hidden_bf, down_full, preferred_element_type=jnp.float32)
    result, second_normed, second_scale = norm_forward(
        first_out + down_act, gain_two.astype(jnp.float32), bias_two.astype(jnp.float32)
    )
    gate_full, up_full, down_full, gain_two, bias_two = fetch_feedforward(
        w_gate, w_up, w_down, ln2_gain, ln2_bias
    )
    upstream = out_cotangent.reshape(-1, D).astype(jnp.float32)
    grad_gain_two = jnp.sum(upstream * second_normed, axis=0)
    grad_bias_two = jnp.sum(upstream, axis=0)
    grad_second = norm_backward(upstream, second_normed, second_scale, gain_two.astype(jnp.float32))
    grad_down_bf = grad_second.astype(jnp.bfloat16)
    grad_down_w = jnp.einsum(
        "tf,td->fd", hidden_bf, grad_down_bf, preferred_element_type=jnp.float32
    )
    grad_hidden = jnp.einsum(
        "td,fd->tf", grad_down_bf, down_full, preferred_element_type=jnp.float32
    )
    sigmoid_gate = jax.nn.sigmoid(gate_act)
    grad_gate_bf = (
        grad_hidden * up_act * sigmoid_gate * (1.0 + gate_act * (1.0 - sigmoid_gate))
    ).astype(jnp.bfloat16)
    grad_up_bf = (grad_hidden * jax.nn.silu(gate_act)).astype(jnp.bfloat16)
    grad_gate_w = jnp.einsum(
        "td,tf->df", first_bf, grad_gate_bf, preferred_element_type=jnp.float32
    )
    grad_up_w = jnp.einsum("td,tf->df", first_bf, grad_up_bf, preferred_element_type=jnp.float32)
    grad_first = grad_second + jnp.einsum(
        "tf,df->td", grad_gate_bf, gate_full, preferred_element_type=jnp.float32
    )
    grad_first = grad_first + jnp.einsum(
        "tf,df->td", grad_up_bf, up_full, preferred_element_type=jnp.float32
    )
    qkv_full, out_full, gain_one, bias_one = fetch_attention(w_qkv, w_out, ln1_gain, ln1_bias)
    grad_gain_one = jnp.sum(grad_first * first_normed, axis=0)
    grad_bias_one = jnp.sum(grad_first, axis=0)
    grad_res = norm_backward(grad_first, first_normed, first_scale, gain_one.astype(jnp.float32))
    grad_branch_bf = grad_res.astype(jnp.bfloat16)
    grad_out_w = jnp.einsum(
        "tc,td->cd", attended_bf, grad_branch_bf, preferred_element_type=jnp.float32
    )
    grad_attended_bf = jnp.einsum(
        "td,cd->tc", grad_branch_bf, out_full, preferred_element_type=jnp.float32
    ).astype(jnp.bfloat16)
    grad_queries, grad_keys_all, grad_values_all = attention_backward(
        queries, key_rows, value_rows, grad_attended_bf, log_totals, same_doc
    )
    grad_keys, grad_values = (
        lax.psum_scatter(
            grad_keys_all.astype(jnp.bfloat16), "shard", scatter_dimension=0, tiled=True
        ).astype(jnp.float32),
        lax.psum_scatter(
            grad_values_all.astype(jnp.bfloat16), "shard", scatter_dimension=0, tiled=True
        ).astype(jnp.float32),
    )
    grad_projected = jnp.concatenate(
        [
            rotate_back(grad_queries.reshape(heads_shape), cosine, sine).reshape(token_count, D),
            rotate_back(grad_keys.reshape(heads_shape), cosine, sine).reshape(token_count, D),
            grad_values,
        ],
        axis=1,
    ).astype(jnp.bfloat16)
    grad_qkv_w = jnp.einsum(
        "td,tn->dn", inputs_bf, grad_projected, preferred_element_type=jnp.float32
    )
    grad_inputs = grad_res + jnp.einsum(
        "tn,dn->td", grad_projected, qkv_full, preferred_element_type=jnp.float32
    )
    (
        sum_qkv,
        sum_out,
        sum_gain_one,
        sum_bias_one,
        sum_gate,
        sum_up,
        sum_down,
        sum_gain_two,
        sum_bias_two,
    ) = (
        lax.psum_scatter(
            grad_qkv_w.astype(jnp.bfloat16), "shard", scatter_dimension=0, tiled=True
        ).astype(jnp.float32),
        lax.psum_scatter(
            grad_out_w.astype(jnp.bfloat16), "shard", scatter_dimension=0, tiled=True
        ).astype(jnp.float32),
        lax.psum_scatter(
            grad_gain_one.astype(jnp.bfloat16), "shard", scatter_dimension=0, tiled=True
        ).astype(jnp.float32),
        lax.psum_scatter(
            grad_bias_one.astype(jnp.bfloat16), "shard", scatter_dimension=0, tiled=True
        ).astype(jnp.float32),
        lax.psum_scatter(
            grad_gate_w.astype(jnp.bfloat16), "shard", scatter_dimension=0, tiled=True
        ).astype(jnp.float32),
        lax.psum_scatter(
            grad_up_w.astype(jnp.bfloat16), "shard", scatter_dimension=0, tiled=True
        ).astype(jnp.float32),
        lax.psum_scatter(
            grad_down_w.astype(jnp.bfloat16), "shard", scatter_dimension=0, tiled=True
        ).astype(jnp.float32),
        lax.psum_scatter(
            grad_gain_two.astype(jnp.bfloat16), "shard", scatter_dimension=0, tiled=True
        ).astype(jnp.float32),
        lax.psum_scatter(
            grad_bias_two.astype(jnp.bfloat16), "shard", scatter_dimension=0, tiled=True
        ).astype(jnp.float32),
    )
    totals = (
        lax.psum(sum_qkv.astype(jnp.bfloat16), "rep").astype(jnp.float32),
        lax.psum(sum_out.astype(jnp.bfloat16), "rep").astype(jnp.float32),
        lax.psum(sum_gain_one.astype(jnp.bfloat16), "rep").astype(jnp.float32),
        lax.psum(sum_bias_one.astype(jnp.bfloat16), "rep").astype(jnp.float32),
        lax.psum(sum_gate.astype(jnp.bfloat16), "rep").astype(jnp.float32),
        lax.psum(sum_up.astype(jnp.bfloat16), "rep").astype(jnp.float32),
        lax.psum(sum_down.astype(jnp.bfloat16), "rep").astype(jnp.float32),
        lax.psum(sum_gain_two.astype(jnp.bfloat16), "rep").astype(jnp.float32),
        lax.psum(sum_bias_two.astype(jnp.bfloat16), "rep").astype(jnp.float32),
    )
    return (
        result.astype(jnp.bfloat16).reshape(tokens_in.shape),
        grad_inputs.reshape(tokens_in.shape),
        totals[0],
        totals[1],
        totals[2],
        totals[3],
        totals[4],
        totals[5],
        totals[6],
        totals[7],
        totals[8],
    )


BF = jnp.bfloat16
F32 = jnp.float32
AXES = ("rep", "shard")
TILE = 256
GROUP = 4
OWN_HEADS = 3
NARROW = OWN_HEADS * HEAD_DIM
WIDE = 256
LANES = 128
LOG2E = 1.4426950408889634
SCORE_FACTOR = HEAD_DIM ** (-0.5) * LOG2E
MASKED = -1e30


def cost(flops, *arrays):
    moved = sum(math.prod(array.shape) * array.dtype.itemsize for array in arrays)
    return pl.CostEstimate(flops=flops, transcendentals=0, bytes_accessed=moved)


def moves(target):
    pairs = []
    for rep in range(4):
        for shard in range(8):
            goal = target(rep // 2, rep % 2, shard // 4, shard % 4)
            if goal is not None:
                x, c, h, j = goal
                pairs.append((rep * 8 + shard, (2 * x + c) * 8 + 4 * h + j))
    return pairs


SPREAD = moves(lambda x, c, h, j: (x, h, c, j))
OTHER_CORE = moves(lambda x, c, h, j: (x, 1 - c, h, j))
OTHER_X = moves(lambda x, c, h, j: (1 - x, c, h, j))
OTHER_HALF = moves(lambda x, c, h, j: (x, c, 1 - h, j))
SQUARE = [moves(lambda x, c, h, j, k=k: (x, c, h, j ^ k)) for k in range(GROUP)]
ROUND = [moves(lambda x, c, h, j, i=i: (x, c, h ^ c, j ^ (2 * x + i))) for i in range(2)]
OUT_FETCH = moves(lambda x, c, h, j: (x, j % 2, c, (4 * h + j) // 2))
OUT_RETURN = moves(lambda x, c, h, j: (x, h, (2 * j + c) // 4, (2 * j + c) % 4))
HOME_HALF = moves(lambda x, c, h, j: (x, c, 1 - h, j) if c != h else None)
HOME_SQUARE = [
    moves(lambda x, c, h, j, k=k: (x, c, h, j ^ k) if c == h else None) for k in range(GROUP)
]
HOME_X = moves(lambda x, c, h, j: (1 - x, c, h, j) if c == h else None)


def send(value, pairs):
    return lax.ppermute(value, AXES, pairs)


def pick(flag, first, second):
    return jnp.where(flag, second, first)


def unmix(blocks, j):
    bit0 = (j % 2) == 1
    bit1 = (j // 2) == 1
    b = blocks
    b = [pick(bit0, b[0], b[1]), pick(bit0, b[1], b[0]), pick(bit0, b[2], b[3]), pick(bit0, b[3], b[2])]
    return [pick(bit1, b[0], b[2]), pick(bit1, b[1], b[3]), pick(bit1, b[2], b[0]), pick(bit1, b[3], b[1])]


def turned(values):
    lane = lax.broadcasted_iota(jnp.int32, values.shape, 1) % HEAD_DIM
    middle = HEAD_DIM // 2
    return jnp.where(
        lane < middle,
        -pltpu.roll(values, WIDE - middle, 1),
        pltpu.roll(values, middle, 1),
    )


def doubled(table):
    return jnp.concatenate([table, table], axis=1)


def project_kernel(x_ref, w_ref, cos_ref, sin_ref, q_ref, kv_ref):
    projected = jnp.dot(x_ref[...], w_ref[...], preferred_element_type=F32)
    cosine = doubled(cos_ref[...])
    sine = doubled(sin_ref[...])
    for index, ref in ((0, q_ref), (1, kv_ref)):
        part = projected[:, index * WIDE : (index + 1) * WIDE]
        ref[:, :WIDE] = (part * cosine + turned(part) * sine).astype(BF)
    kv_ref[:, WIDE:] = projected[:, 2 * WIDE :].astype(BF)


def project(x_rows, w_qkv, cosine, sine):
    rows = x_rows.shape[0]
    return pl.pallas_call(
        project_kernel,
        grid=(rows // TILE,),
        in_specs=[
            pl.BlockSpec((TILE, D), lambda i: (i, 0)),
            pl.BlockSpec((D, 3 * WIDE), lambda i: (0, 0)),
            pl.BlockSpec((TILE, 128), lambda i: (i, 0)),
            pl.BlockSpec((TILE, 128), lambda i: (i, 0)),
        ],
        out_specs=[
            pl.BlockSpec((TILE, WIDE), lambda i: (i, 0)),
            pl.BlockSpec((TILE, 2 * WIDE), lambda i: (i, 0)),
        ],
        out_shape=[
            jax.ShapeDtypeStruct((rows, WIDE), BF),
            jax.ShapeDtypeStruct((rows, 2 * WIDE), BF),
        ],
        cost_estimate=cost(2 * rows * w_qkv.size, x_rows, w_qkv, x_rows, cosine, sine),
        name="project",
    )(x_rows, w_qkv, cosine, sine)


def head_only(values, head):
    lane = lax.broadcasted_iota(jnp.int32, values.shape, 1) // HEAD_DIM
    return jnp.where(lane == head, values, jnp.zeros_like(values))


def share_document(ids_ref, q_tile, kv_tile):
    q_first = ids_ref[q_tile * TILE]
    q_last = ids_ref[q_tile * TILE + TILE - 1]
    k_first = ids_ref[kv_tile * TILE]
    k_last = ids_ref[kv_tile * TILE + TILE - 1]
    return jnp.logical_and(k_first <= q_last, q_first <= k_last)


def contract(left, right, left_dim, right_dim):
    return lax.dot_general(
        left, right, (((left_dim,), (right_dim,)), ((), ())), preferred_element_type=F32
    )


def attend_kernel(
    ids_ref, row_ids_ref, col_ids_ref, q_ref, own_ref, other_ref, out_ref, log_ref,
    k_all, v_turned, max_ref, total_ref, acc_ref,
):
    q_tile = pl.program_id(0)
    own_tiles = own_ref.shape[0] // TILE

    @pl.when(q_tile == 0)
    def _():
        for base, ref in ((0, own_ref), (own_tiles, other_ref)):

            def gather(tile, carry, base=base, ref=ref):
                place = pl.ds(pl.multiple_of(tile * TILE, TILE), TILE)
                k_all[base + tile] = ref[place, :WIDE]
                v_turned[base + tile] = jnp.transpose(ref[place, WIDE:])[:NARROW]
                return carry

            lax.fori_loop(0, own_tiles, gather, 0)

    queries = q_ref[...]
    per_head = [head_only(queries, head) for head in range(OWN_HEADS)]
    q_ids = row_ids_ref[0]
    max_ref[...] = jnp.full(max_ref.shape, MASKED, F32)
    total_ref[...] = jnp.zeros(total_ref.shape, F32)
    acc_ref[...] = jnp.zeros(acc_ref.shape, F32)

    def one_tile(tile, carry):
        @pl.when(share_document(ids_ref, q_tile, tile))
        def _():
            keys = k_all[tile]
            same = (
                col_ids_ref[pl.ds(pl.multiple_of(tile * TILE, TILE), TILE), :] == q_ids
            )
            for head in range(OWN_HEADS):
                scores = contract(keys, per_head[head], 1, 1) * SCORE_FACTOR
                scores = jnp.where(same, scores, MASKED)
                old_max = max_ref[head : head + 1, :]
                new_max = jnp.maximum(old_max, jnp.max(scores, axis=0, keepdims=True))
                shrink = jnp.exp2(old_max - new_max)
                expons = jnp.exp2(scores - new_max)
                max_ref[head : head + 1, :] = new_max
                total_ref[head : head + 1, :] = total_ref[
                    head : head + 1, :
                ] * shrink + jnp.sum(expons, axis=0, keepdims=True)
                rows = slice(head * HEAD_DIM, (head + 1) * HEAD_DIM)
                acc_ref[rows, :] = acc_ref[rows, :] * shrink + jnp.dot(
                    v_turned[tile, rows, :],
                    expons.astype(BF),
                    preferred_element_type=F32,
                )

        return carry

    lax.fori_loop(0, 2 * own_tiles, one_tile, 0)

    parts = []
    for head in range(OWN_HEADS):
        rows = slice(head * HEAD_DIM, (head + 1) * HEAD_DIM)
        parts.append(acc_ref[rows, :] / total_ref[head : head + 1, :])
    parts.append(jnp.zeros((WIDE - NARROW, TILE), F32))
    out_ref[...] = jnp.transpose(jnp.concatenate(parts, axis=0)).astype(BF)
    row = lax.broadcasted_iota(jnp.int32, log_ref.shape, 0)
    log_ref[...] = jnp.where(
        row < OWN_HEADS,
        max_ref[...] + jnp.log2(jnp.where(row < OWN_HEADS, total_ref[...], 1.0)),
        0.0,
    )


def attend(ids, row_ids, col_ids, queries, kv_own, kv_other):
    rows = queries.shape[0]
    whole = lambda array: pl.BlockSpec(array.shape, lambda i, ids: (0,) * array.ndim)
    return pl.pallas_call(
        attend_kernel,
        grid_spec=pltpu.PrefetchScalarGridSpec(
            num_scalar_prefetch=1,
            grid=(rows // TILE,),
            in_specs=[
                pl.BlockSpec((1, 1, TILE), lambda i, ids: (i, 0, 0)),
                whole(col_ids),
                pl.BlockSpec((TILE, WIDE), lambda i, ids: (i, 0)),
                whole(kv_own),
                whole(kv_other),
            ],
            out_specs=[
                pl.BlockSpec((TILE, WIDE), lambda i, ids: (i, 0)),
                pl.BlockSpec((8, TILE), lambda i, ids: (0, i)),
            ],
            scratch_shapes=[
                pltpu.VMEM((2 * rows // TILE, TILE, WIDE), BF),
                pltpu.VMEM((2 * rows // TILE, NARROW, TILE), BF),
                pltpu.VMEM((8, TILE), F32),
                pltpu.VMEM((8, TILE), F32),
                pltpu.VMEM((NARROW, TILE), F32),
            ],
        ),
        out_shape=[
            jax.ShapeDtypeStruct((rows, WIDE), BF),
            jax.ShapeDtypeStruct((8, rows), F32),
        ],
        cost_estimate=cost(
            4 * OWN_HEADS * WIDE * rows * 2 * rows, queries, kv_own, kv_other, queries
        ),
        name="attend",
    )(ids, row_ids, col_ids, queries, kv_own, kv_other)


def attend_back_kernel(
    ids_ref, row_ids_ref, col_ids_ref, q_ref, up_ref, out_ref, log_ref, own_ref, other_ref,
    cos_ref, sin_ref, dq_ref, own_grad_ref, other_grad_ref,
    kv_all, k_turned, acc_ref, key_acc, value_acc,
):
    q_tile = pl.program_id(0)
    own_tiles = own_ref.shape[0] // TILE

    @pl.when(q_tile == 0)
    def _():
        for base, ref in ((0, own_ref), (own_tiles, other_ref)):

            def gather(tile, carry, base=base, ref=ref):
                place = pl.ds(pl.multiple_of(tile * TILE, TILE), TILE)
                kv_all[base + tile] = ref[place, :]
                k_turned[base + tile] = jnp.transpose(ref[place, :WIDE])[:NARROW]
                rows = pl.ds(pl.multiple_of((base + tile) * TILE, TILE), TILE)
                key_acc[rows, :] = jnp.zeros((TILE, WIDE), F32)
                value_acc[rows, :] = jnp.zeros((TILE, WIDE), F32)
                return carry

            lax.fori_loop(0, own_tiles, gather, 0)

    queries = q_ref[...]
    upstream = up_ref[...]
    sides = (slice(0, LANES), slice(LANES, WIDE))
    members = ((0, 1), (2,))
    split = lambda values: [
        [head_only(values[:, side], head % 2) for head in inside]
        for side, inside in zip(sides, members)
    ]
    q_heads, up_heads = split(queries), split(upstream)
    q_stacks = [jnp.concatenate(parts, axis=0) for parts in q_heads]
    up_stacks = [jnp.concatenate(parts, axis=0) for parts in up_heads]
    products = upstream.astype(F32) * out_ref[...].astype(F32)
    lane_head = lax.broadcasted_iota(jnp.int32, (8, WIDE), 1) // HEAD_DIM
    selector = (lane_head == lax.broadcasted_iota(jnp.int32, (8, WIDE), 0)).astype(F32)
    deltas = lax.dot_general(
        selector, products, (((1,), (1,)), ((), ())),
        precision=lax.Precision.HIGHEST, preferred_element_type=F32,
    )
    q_ids = row_ids_ref[0]
    acc_ref[...] = jnp.zeros(acc_ref.shape, F32)

    def one_tile(tile, carry):
        @pl.when(share_document(ids_ref, q_tile, tile))
        def _():
            place = pl.ds(pl.multiple_of(tile * TILE, TILE), TILE)
            keys = kv_all[tile, :, :WIDE]
            values = kv_all[tile, :, WIDE:]
            same = col_ids_ref[place, :] == q_ids
            for side, inside, q_side, up_side, q_stack, up_stack in zip(
                sides, members, q_heads, up_heads, q_stacks, up_stacks
            ):
                all_weights, all_grads = [], []
                for head, query, grad in zip(inside, q_side, up_side):
                    scores = contract(keys[:, side], query, 1, 1) * SCORE_FACTOR
                    weights = jnp.where(
                        same, jnp.exp2(scores - log_ref[head : head + 1, :]), 0.0
                    )
                    grad_weights = contract(values[:, side], grad, 1, 1)
                    grad_scores = (
                        weights * (grad_weights - deltas[head : head + 1, :])
                    ).astype(BF)
                    all_weights.append(weights.astype(BF))
                    all_grads.append(grad_scores)
                    rows = slice(head * HEAD_DIM, (head + 1) * HEAD_DIM)
                    acc_ref[rows, :] += jnp.dot(
                        k_turned[tile, rows, :], grad_scores,
                        preferred_element_type=F32,
                    )
                value_acc[place, side] += jnp.dot(
                    jnp.concatenate(all_weights, axis=1), up_stack, preferred_element_type=F32
                )
                key_acc[place, side] += jnp.dot(
                    jnp.concatenate(all_grads, axis=1), q_stack, preferred_element_type=F32
                )

        return carry

    lax.fori_loop(0, 2 * own_tiles, one_tile, 0)

    factor = HEAD_DIM ** (-0.5)
    grad_query = jnp.transpose(
        jnp.concatenate([acc_ref[...], jnp.zeros((WIDE - NARROW, TILE), F32)], axis=0)
    )
    grad_query = grad_query * factor
    dq_ref[...] = (
        grad_query * doubled(cos_ref[...]) - turned(grad_query) * doubled(sin_ref[...])
    ).astype(BF)

    @pl.when(q_tile == pl.num_programs(0) - 1)
    def _():

        def write(tile, carry):
            own = pl.ds(pl.multiple_of(tile * TILE, TILE), TILE)
            other = pl.ds(pl.multiple_of((own_tiles + tile) * TILE, TILE), TILE)
            own_grad_ref[own, :WIDE] = key_acc[own, :] * factor
            own_grad_ref[own, WIDE:] = value_acc[own, :]
            other_grad_ref[own, :WIDE] = (key_acc[other, :] * factor).astype(BF)
            other_grad_ref[own, WIDE:] = value_acc[other, :].astype(BF)
            return carry

        lax.fori_loop(0, own_tiles, write, 0)


def attend_back(
    ids, row_ids, col_ids, queries, upstream, attended, logs, kv_own, kv_other, cosine, sine
):
    rows = queries.shape[0]
    whole = lambda array: pl.BlockSpec(array.shape, lambda i, ids: (0,) * array.ndim)
    tiled = lambda width: pl.BlockSpec((TILE, width), lambda i, ids: (i, 0))
    return pl.pallas_call(
        attend_back_kernel,
        grid_spec=pltpu.PrefetchScalarGridSpec(
            num_scalar_prefetch=1,
            grid=(rows // TILE,),
            in_specs=[
                pl.BlockSpec((1, 1, TILE), lambda i, ids: (i, 0, 0)),
                whole(col_ids),
                tiled(WIDE),
                tiled(WIDE),
                tiled(WIDE),
                pl.BlockSpec((8, TILE), lambda i, ids: (0, i)),
                whole(kv_own),
                whole(kv_other),
                tiled(128),
                tiled(128),
            ],
            out_specs=[
                tiled(WIDE),
                pl.BlockSpec((rows, 2 * WIDE), lambda i, ids: (0, 0)),
                pl.BlockSpec((rows, 2 * WIDE), lambda i, ids: (0, 0)),
            ],
            scratch_shapes=[
                pltpu.VMEM((2 * rows // TILE, TILE, 2 * WIDE), BF),
                pltpu.VMEM((2 * rows // TILE, NARROW, TILE), BF),
                pltpu.VMEM((NARROW, TILE), F32),
                pltpu.VMEM((2 * rows, WIDE), F32),
                pltpu.VMEM((2 * rows, WIDE), F32),
            ],
        ),
        out_shape=[
            jax.ShapeDtypeStruct((rows, WIDE), BF),
            jax.ShapeDtypeStruct((rows, 2 * WIDE), F32),
            jax.ShapeDtypeStruct((rows, 2 * WIDE), BF),
        ],
        cost_estimate=cost(
            10 * OWN_HEADS * WIDE * rows * 2 * rows, queries, kv_own, kv_other, queries
        ),
        name="attend_back",
    )(ids, row_ids, col_ids, queries, upstream, attended, logs, kv_own, kv_other, cosine, sine)


def grad_qkv_kernel(
    c_ref, x_ref, dq_ref, own_ref, got_ref, cos_ref, sin_ref, vectors_ref,
    out_ref, keep_ref, away_ref, acc_ref,
):
    tile = pl.program_id(0)
    total = own_ref[...] + got_ref[...].astype(F32)
    keys = total[:, :WIDE]
    keys = keys * doubled(cos_ref[...]) - turned(keys) * doubled(sin_ref[...])
    grads = jnp.concatenate(
        [dq_ref[...], keys.astype(BF), total[:, WIDE:].astype(BF)], axis=1
    )
    out_ref[...] = grads
    part = contract(x_ref[...], grads, 0, 0)

    @pl.when(tile == 0)
    def _():
        acc_ref[...] = part

    @pl.when(tile > 0)
    def _():
        acc_ref[...] += part

    @pl.when(tile == pl.num_programs(0) - 1)
    def _():
        rows = keep_ref.shape[0]
        core = c_ref[0]
        step = rows // 8

        def write(index, carry):
            place = pl.ds(pl.multiple_of(index * step, 16), step)
            keep_ref[place, :] = acc_ref[pl.ds(pl.multiple_of(core * rows + index * step, 8), step), :]
            away_ref[place, :] = acc_ref[
                pl.ds(pl.multiple_of((1 - core) * rows + index * step, 8), step), :
            ].astype(BF)
            return carry

        lax.fori_loop(0, 8, write, 0)
        away_ref[rows:] = jnp.zeros((16, away_ref.shape[1]), BF)
        away_ref[rows : rows + 8] = vectors_ref[...].astype(BF)


def grad_qkv(core, x_rows, grad_queries, own, got, cosine, sine, vectors):
    rows = grad_queries.shape[0]
    tiled = lambda width: pl.BlockSpec((TILE, width), lambda i, c: (i, 0))
    whole = lambda *shape: pl.BlockSpec(shape, lambda i, c: (0, 0))
    return pl.pallas_call(
        grad_qkv_kernel,
        grid_spec=pltpu.PrefetchScalarGridSpec(
            num_scalar_prefetch=1,
            grid=(rows // TILE,),
            in_specs=[
                tiled(D), tiled(WIDE), tiled(2 * WIDE), tiled(2 * WIDE), tiled(LANES),
                tiled(LANES), whole(*vectors.shape),
            ],
            out_specs=[tiled(3 * WIDE), whole(D // 2, 3 * WIDE), whole(D // 2 + 16, 3 * WIDE)],
            scratch_shapes=[pltpu.VMEM((D, 3 * WIDE), F32)],
        ),
        out_shape=[
            jax.ShapeDtypeStruct((rows, 3 * WIDE), BF),
            jax.ShapeDtypeStruct((D // 2, 3 * WIDE), F32),
            jax.ShapeDtypeStruct((D // 2 + 16, 3 * WIDE), BF),
        ],
        cost_estimate=cost(2 * rows * D * 3 * WIDE, own, own, got, grad_queries),
        name="grad_qkv",
    )(core, x_rows, grad_queries, own, got, cosine, sine, vectors)


def after(value, *others):
    return lax.optimization_barrier((value,) + others)[0]


def join(*values):
    return lax.optimization_barrier(values)


def pack_qkv_kernel(target_ref, w_ref, vectors_ref, *refs):
    packed = refs[-1]
    for target in range(GROUP):
        for part in range(3):
            start = part * D + target * NARROW
            packed[target, :, part * NARROW : (part + 1) * NARROW] = w_ref[
                :, start : start + NARROW
            ]
        packed[target, :, 3 * NARROW :] = vectors_ref[...]
    for index, ref in enumerate(refs[:-1]):
        ref[...] = packed[target_ref[index]]


def pack_qkv(targets, w_qkv, vectors):
    rows = w_qkv.shape[0]
    width = 3 * NARROW + vectors.shape[1]
    return pl.pallas_call(
        pack_qkv_kernel,
        in_specs=[
            pl.BlockSpec(memory_space=pltpu.SMEM),
            pl.BlockSpec(memory_space=pltpu.VMEM),
            pl.BlockSpec(memory_space=pltpu.VMEM),
        ],
        out_specs=[pl.BlockSpec(memory_space=pltpu.VMEM)] * 2,
        out_shape=[jax.ShapeDtypeStruct((rows, width), BF)] * 2,
        scratch_shapes=[pltpu.VMEM((GROUP, rows, width), BF)],
        name="pack_qkv",
    )(targets, w_qkv, vectors)


def pack_gate_up_kernel(target_ref, gate_ref, up_ref, *refs):
    packed = refs[-1]
    width = packed.shape[2] // 4
    for target in range(GROUP):
        for index in range(4):
            source = (gate_ref, up_ref)[index // 2]
            start = (index % 2 * GROUP + target) * width
            packed[target, :, index * width : (index + 1) * width] = source[
                :, start : start + width
            ]
    for index, ref in enumerate(refs[:-1]):
        ref[...] = packed[target_ref[index]]


def pack_gate_up(targets, w_gate, w_up):
    rows = w_gate.shape[0]
    width = 2 * w_gate.shape[1] // GROUP
    return pl.pallas_call(
        pack_gate_up_kernel,
        in_specs=[
            pl.BlockSpec(memory_space=pltpu.SMEM),
            pl.BlockSpec(memory_space=pltpu.VMEM),
            pl.BlockSpec(memory_space=pltpu.VMEM),
        ],
        out_specs=[pl.BlockSpec(memory_space=pltpu.VMEM)] * 2,
        out_shape=[jax.ShapeDtypeStruct((rows, width), BF)] * 2,
        scratch_shapes=[pltpu.VMEM((GROUP, rows, width), BF)],
        name="pack_gate_up",
    )(targets, w_gate, w_up)


def unpack_qkv_kernel(place_ref, near_ref, far_ref, out_ref, vectors_ref):
    zeros = jnp.zeros((near_ref.shape[1], WIDE - NARROW), BF)
    for base, source in ((0, near_ref), (GROUP, far_ref)):

        def one_block(index, carry, base=base, source=source):
            place = place_ref[base + index]
            for part in range(3):
                out_ref[place, :, part * WIDE : part * WIDE + NARROW] = source[
                    index, :, part * NARROW : (part + 1) * NARROW
                ]
                out_ref[place, :, part * WIDE + NARROW : (part + 1) * WIDE] = zeros
            vectors_ref[place] = source[index, :, 3 * NARROW :]
            return carry

        lax.fori_loop(0, GROUP, one_block, 0)


def unpack_qkv(places, near, far):
    _, rows, width = near.shape
    return pl.pallas_call(
        unpack_qkv_kernel,
        in_specs=[
            pl.BlockSpec(memory_space=pltpu.SMEM),
            pl.BlockSpec(memory_space=pltpu.VMEM),
            pl.BlockSpec(memory_space=pltpu.VMEM),
        ],
        out_specs=[pl.BlockSpec(memory_space=pltpu.VMEM)] * 2,
        out_shape=[
            jax.ShapeDtypeStruct((2 * GROUP, rows, 3 * WIDE), BF),
            jax.ShapeDtypeStruct((2 * GROUP, rows, width - 3 * NARROW), BF),
        ],
        name="unpack_qkv",
    )(places, near, far)


def unpack_kernel(place_ref, near_ref, far_ref, out_ref):
    for base, ref in ((0, near_ref), (GROUP, far_ref)):

        def one_block(index, carry, base=base, ref=ref):
            out_ref[place_ref[base + index]] = ref[index]
            return carry

        lax.fori_loop(0, GROUP, one_block, 0)


def unpack(places, near, far):
    count, rows, width = near.shape
    return pl.pallas_call(
        unpack_kernel,
        in_specs=[
            pl.BlockSpec(memory_space=pltpu.SMEM),
            pl.BlockSpec(memory_space=pltpu.VMEM),
            pl.BlockSpec(memory_space=pltpu.VMEM),
        ],
        out_specs=pl.BlockSpec(memory_space=pltpu.VMEM),
        out_shape=jax.ShapeDtypeStruct((2 * count, rows, width), BF),
        name="unpack",
    )(places, near, far)


def split_feed_kernel(x_ref, down_ref, down_got_ref, gate_up_ref, gate_up_got_ref, keep_ref, away_ref):
    mine = x_ref[0]
    width = down_ref.shape[-1]

    def one_block(block, carry):
        for side, ref in ((mine, keep_ref), (1 - mine, away_ref)):
            ref[block] = (
                down_ref[block, side] + down_got_ref[block, side].astype(F32)
            ).astype(BF)
            total = gate_up_ref[block, side] + gate_up_got_ref[block, side].astype(F32)
            ref[GROUP + block] = total[:, :width].astype(BF)
            ref[2 * GROUP + block] = total[:, width:].astype(BF)
        return carry

    lax.fori_loop(0, GROUP, one_block, 0)


def whole_call(kernel, name, shapes, scalars, *arrays):
    return pl.pallas_call(
        kernel,
        in_specs=[pl.BlockSpec(memory_space=pltpu.SMEM)]
        + [pl.BlockSpec(memory_space=pltpu.VMEM)] * len(arrays),
        out_specs=[pl.BlockSpec(memory_space=pltpu.VMEM)] * len(shapes),
        out_shape=[jax.ShapeDtypeStruct(shape, dtype) for shape, dtype in shapes],
        cost_estimate=cost(sum(a.size for a in arrays), *arrays, *arrays),
        name=name,
    )(scalars, *arrays)


def square_feed_kernel(index_ref, mine_ref, got_ref, kept_ref, *send_refs):
    for k in range(GROUP):
        target = index_ref[k]
        for part in range(2):
            slot = (part + 1) * GROUP + target
            block = mine_ref[slot] + got_ref[slot]
            if k == 0:
                kept_ref[GROUP + part] = block
            else:
                send_refs[k - 1][part] = block
        kept_ref[k] = mine_ref[k] + got_ref[k]


def join_feed_kernel(index_ref, kept_ref, *refs):
    out_ref = refs[-1]
    for k in range(GROUP):
        out_ref[k] = kept_ref[k]
        for part in range(2):
            slot = (part + 1) * GROUP + index_ref[k]
            out_ref[slot] = kept_ref[GROUP + part] if k == 0 else refs[k - 1][part]


def finish_feed_kernel(flag_ref, own_ref, other_ref, far_own_ref, far_other_ref, down_ref, gate_ref, up_ref):
    mine, at_home = flag_ref[0], flag_ref[1] == 1
    rows = own_ref.shape[1]
    half = own_ref.shape[2] // 2
    pairs = ((own_ref, far_own_ref, mine), (other_ref, far_other_ref, 1 - mine))

    def down_slot(slot, carry):
        for near, far, side in pairs:
            down_ref[slot, side] = jnp.where(at_home, near[slot], far[slot]).astype(F32)
        return carry

    lax.fori_loop(0, GROUP, down_slot, 0)
    for slot in range(GROUP):
        for near, far, side in pairs:
            for part, ref in ((1, gate_ref), (2, up_ref)):
                place = part * GROUP + slot
                block = jnp.where(at_home, near[place], far[place]).astype(F32)
                start = slot % GROUP * half
                width = GROUP * half
                ref[side, :, start : start + half] = block[:, :half]
                ref[side, :, width + start : width + start + half] = block[:, half:]


def split_x_kernel(flag_ref, part_ref, vectors_ref, got_ref, keep_ref, away_ref):
    mine = flag_ref[0]
    rows = part_ref.shape[0]
    step = rows // (2 * GROUP)

    def one_block(block, carry):
        for side, ref in ((mine, keep_ref), (1 - mine, away_ref)):
            place = pl.ds(pl.multiple_of((2 * block + side) * step, step), step)
            ref[pl.ds(pl.multiple_of(block * step, step), step)] = (
                part_ref[place] + got_ref[place].astype(F32)
            ).astype(BF)
        return carry

    lax.fori_loop(0, GROUP, one_block, 0)
    for ref in (keep_ref, away_ref):
        ref[GROUP * step :] = got_ref[rows:]
        ref[GROUP * step : GROUP * step + 8] = (
            vectors_ref[...] + got_ref[rows : rows + 8].astype(F32)
        ).astype(BF)


def square_qkv_kernel(index_ref, mine_ref, got_ref, *refs):
    step = (mine_ref.shape[0] - 16) // GROUP
    vectors = mine_ref[GROUP * step :] + got_ref[GROUP * step :]
    for k in range(GROUP):
        place = pl.ds(pl.multiple_of(index_ref[k] * step, step), step)
        refs[k][:step] = mine_ref[place] + got_ref[place]
        refs[k][step:] = vectors


def join_qkv_kernel(index_ref, *refs):
    out_ref = refs[-1]
    step = refs[0].shape[0] - 16
    vectors = refs[0][step:].astype(F32)
    for k in range(GROUP):
        place = pl.ds(pl.multiple_of(index_ref[k] * step, step), step)
        out_ref[place] = refs[k][:step]
        if k:
            vectors += refs[k][step:].astype(F32)
    out_ref[GROUP * step :] = vectors.astype(BF)


def finish_qkv_kernel(flag_ref, own_ref, other_ref, far_own_ref, far_other_ref, out_ref, vectors_ref):
    mine, at_home = flag_ref[0], flag_ref[1] == 1
    step = (own_ref.shape[0] - 16) // GROUP
    for block in range(GROUP):
        rows = slice(block * step, (block + 1) * step)
        for near, far, side in ((own_ref, far_own_ref, mine), (other_ref, far_other_ref, 1 - mine)):
            values = jnp.where(at_home, near[rows], far[rows]).astype(F32)
            for part in range(3):
                start = part * D + block * NARROW
                out_ref[side, :, start : start + NARROW] = values[
                    :, part * WIDE : part * WIDE + NARROW
                ]
    rows = slice(GROUP * step, GROUP * step + 8)
    vectors_ref[...] = jnp.where(at_home, own_ref[rows], far_own_ref[rows]).astype(F32)


def gather_square(block):
    return [block] + [send(block, SQUARE[k]) for k in range(1, GROUP)]


def square_parts(left, weight, weight_dim):
    return [
        contract(left[k * TILE : (k + 1) * TILE], weight, 1, weight_dim).astype(BF)
        for k in range(1, GROUP)
    ]


def reduce_square(left, weight, weight_dim, parts=None):
    if parts is None:
        parts = square_parts(left, weight, weight_dim)
    got = [send(part, SQUARE[k + 1]) for k, part in enumerate(parts)]
    (total,) = join(contract(left[:TILE], weight, 1, weight_dim))
    for part in got:
        total = total + part.astype(F32)
    return total


def per_device_clustered(
    tokens_in,
    segment_ids,
    w_qkv,
    w_out,
    ln1_gain,
    ln1_bias,
    w_gate,
    w_up,
    w_down,
    ln2_gain,
    ln2_bias,
    out_cotangent,
):
    rep = lax.axis_index("rep")
    shard = lax.axis_index("shard")
    x, c = rep // 2, rep % 2
    h, j = shard // 4, shard % 4
    core_is_one = c == 1
    half_is_one = h == 1
    x_is_one = x == 1
    at_home = c == h
    token_count = tokens_in.shape[1]
    length = segment_ids.shape[1]
    rows_d = w_qkv.shape[0]
    rows_f = w_down.shape[0]
    slice_f = 2 * rows_f
    group_rows = GROUP * token_count

    inputs_bf = send(tokens_in.reshape(token_count, D), SPREAD)
    doc_ids = send(segment_ids, SPREAD).reshape(2, GROUP, token_count)

    by_x = jnp.stack([2 * x, 2 * x + 1, 2 - 2 * x, 3 - 2 * x]) ^ j
    targets = by_x[:2]
    places = jnp.concatenate([GROUP * (h ^ c) + by_x, GROUP * (1 - (h ^ c)) + by_x])

    out_got = send(w_out, OUT_FETCH)
    vectors = jnp.stack([ln1_gain, ln1_bias, ln2_gain, ln2_bias], axis=1)
    qkv_packed = pack_qkv(targets, w_qkv, vectors)
    qkv_mine = after(
        jnp.stack([send(part, ROUND[i]) for i, part in enumerate(qkv_packed)]), inputs_bf
    )
    x_tiles = gather_square(inputs_bf)
    qkv_second = send(qkv_mine, OTHER_X)
    qkv_near = jnp.concatenate([qkv_mine, qkv_second], axis=0)
    qkv_second, w_gate, w_up, down_whole, doc_ids, j = join(
        qkv_second, w_gate, w_up, w_down, doc_ids, j
    )
    qkv_far = send(qkv_near, OTHER_CORE)
    qkv_own, vectors_got = unpack_qkv(places, qkv_near, qkv_far)
    qkv_own = qkv_own.reshape(D, 3 * WIDE)
    qkv_own, *x_tiles = join(qkv_own, *x_tiles)
    x_rows = jnp.concatenate(x_tiles, axis=0)

    tile_index = j ^ jnp.arange(GROUP, dtype=jnp.int32)
    first_row = (c * GROUP + tile_index) * token_count
    positions = (
        first_row[:, None] + jnp.arange(token_count, dtype=jnp.int32)[None, :]
    ).reshape(group_rows).astype(F32)
    middle = HEAD_DIM // 2
    exponents = jnp.arange(128, dtype=jnp.int32) % middle
    inverse = rope_base ** (-(2.0 * exponents.astype(F32)) / HEAD_DIM)
    angles = positions[:, None] * inverse[None, :]
    cosine, sine = jnp.cos(angles), jnp.sin(angles)
    mixed = jnp.stack(unmix([doc_ids[:, k] for k in range(GROUP)], j), axis=1)
    ids = jnp.concatenate(
        [pick(core_is_one, mixed[0], mixed[1]), pick(core_is_one, mixed[1], mixed[0])], axis=0
    )
    flat_ids = ids.reshape(length)
    row_ids = ids.reshape(length // TILE, 1, TILE)
    col_ids = flat_ids[:, None]

    part_f = rows_f // 4
    gate_up_packed = pack_gate_up(targets, w_gate, w_up)
    down_sent = lax.dynamic_slice_in_dim(down_whole, (2 * c + x) * part_f, part_f, 0)
    down_mine = send(down_sent, OTHER_HALF)
    (
        x_rows, qkv_own, vectors_got, out_got, flat_ids, row_ids, col_ids, cosine, sine, down_mine,
        *gate_up_packed,
    ) = join(
        x_rows, qkv_own, vectors_got, out_got, flat_ids, row_ids, col_ids, cosine, sine, down_mine,
        *gate_up_packed,
    )

    queries, kv_own = project(x_rows, qkv_own, cosine, sine)
    kv_other = send(kv_own, OTHER_CORE)
    out_other = send(out_got, OTHER_CORE)
    kv_other, out_other, *gate_up_packed = join(kv_other, out_other, *gate_up_packed)
    attended, logs = attend(flat_ids, row_ids, col_ids, queries, kv_own, kv_other)
    gate_up_first = [send(part, ROUND[i]) for i, part in enumerate(gate_up_packed)]
    attended, logs, *gate_up_first = join(attended, logs, *gate_up_first)
    out_own = jnp.concatenate(
        [
            pick(core_is_one, out_got, out_other),
            pick(core_is_one, out_other, out_got),
            jnp.zeros((WIDE - NARROW, D), BF),
        ],
        axis=0,
    )

    branch_parts = square_parts(attended, out_own, 0)
    gate_up_mine, down_mine, *branch_parts = join(
        jnp.stack(gate_up_first), down_mine, *branch_parts
    )
    gate_up_second = send(gate_up_mine, OTHER_X)
    down_got = send(down_mine, OTHER_X)
    branch = reduce_square(attended, out_own, 0, branch_parts)
    vectors_full = jnp.transpose(vectors_got.reshape(D, 4)).astype(F32)
    gain_one, bias_one, gain_two, bias_two = (vectors_full[i] for i in range(4))
    first_out, first_normed, first_scale = norm_forward(
        inputs_bf.astype(F32) + branch, gain_one, bias_one
    )
    first_bf, gate_up_second, down_got, out_cotangent = join(
        first_out.astype(BF), gate_up_second, down_got, out_cotangent
    )

    first_tiles = gather_square(first_bf)
    gate_up_near = jnp.concatenate([gate_up_mine, gate_up_second], axis=0)
    gate_up_far = send(gate_up_near, OTHER_CORE)
    gate_up_own = unpack(places, gate_up_near, gate_up_far).reshape(D, 2 * slice_f)
    down_got = after(down_got, first_tiles[1])
    down_pair = jnp.concatenate(
        [pick(x_is_one, down_mine, down_got), pick(x_is_one, down_got, down_mine)], axis=0
    )
    down_other = send(down_pair, OTHER_CORE)
    down_far = jnp.concatenate(
        [pick(core_is_one, down_pair, down_other), pick(core_is_one, down_other, down_pair)], axis=0
    )
    down_own = jnp.concatenate(
        [pick(half_is_one, w_down, down_far), pick(half_is_one, down_far, w_down)], axis=0
    )
    first_rows = jnp.concatenate(first_tiles, axis=0)
    acts = contract(first_rows, gate_up_own, 1, 0)
    gate_act, up_act = acts[:, :slice_f], acts[:, slice_f:]
    hidden_bf = (jax.nn.silu(gate_act) * up_act).astype(BF)
    cotangent = send(after(out_cotangent, hidden_bf).reshape(token_count, D), SPREAD)
    down_act = reduce_square(hidden_bf, down_own, 0)
    result, second_normed, second_scale = norm_forward(first_out + down_act, gain_two, bias_two)

    upstream = cotangent.astype(F32)
    grad_gain_two = jnp.sum(upstream * second_normed, axis=0, keepdims=True)
    grad_bias_two = jnp.sum(upstream, axis=0, keepdims=True)
    grad_second = norm_backward(upstream, second_normed, second_scale, gain_two)
    grad_down_rows = jnp.concatenate(gather_square(grad_second.astype(BF)), axis=0)
    grad_hidden = contract(grad_down_rows, down_own, 1, 1)
    sigmoid_gate = jax.nn.sigmoid(gate_act)
    grad_gate_bf = (
        grad_hidden * up_act * sigmoid_gate * (1.0 + gate_act * (1.0 - sigmoid_gate))
    ).astype(BF)
    grad_up_bf = (grad_hidden * (gate_act * sigmoid_gate)).astype(BF)
    grad_acts = jnp.concatenate([grad_gate_bf, grad_up_bf], axis=1)
    first_parts = square_parts(grad_acts, gate_up_own, 1)

    quarter = rows_d // 2
    step_square = jnp.arange(GROUP, dtype=jnp.int32) ^ j
    x_flag = x.reshape(1)
    home_flags = jnp.stack([x, at_home.astype(jnp.int32)])

    def over_cores(partial):
        keep = pick(core_is_one, partial[0], partial[1])
        away = pick(core_is_one, partial[1], partial[0])
        return keep, send(away.astype(BF), OTHER_CORE)

    by_x_rows = (GROUP, 2, quarter)
    gate_up_keep, gate_up_got = over_cores(
        contract(first_rows, after(grad_acts, *first_parts), 0, 0).reshape(
            2, D // 2, 2 * slice_f
        )
    )
    down_keep, down_got = over_cores(
        contract(hidden_bf, after(grad_down_rows, *first_parts), 0, 0).reshape(2, rows_f, D)
    )
    bundle_shape = ((3 * GROUP, quarter, D), BF)
    grad_first = grad_second + reduce_square(grad_acts, gate_up_own, 1, first_parts)
    grad_gain_one = jnp.sum(grad_first * first_normed, axis=0, keepdims=True)
    grad_bias_one = jnp.sum(grad_first, axis=0, keepdims=True)
    grad_res = norm_backward(grad_first, first_normed, first_scale, gain_one)
    grad_res_bf, down_got, gate_up_got = join(grad_res.astype(BF), down_got, gate_up_got)
    grad_branch_tiles = gather_square(grad_res_bf)
    feed_keep, feed_away = whole_call(
        split_feed_kernel, "split_feed", [bundle_shape] * 2, x_flag,
        down_keep.reshape(by_x_rows + (D,)), down_got.reshape(by_x_rows + (D,)),
        gate_up_keep.reshape(by_x_rows + (2 * slice_f,)),
        gate_up_got.reshape(by_x_rows + (2 * slice_f,)),
    )
    feed_got = send(feed_away, OTHER_X)

    grad_branch_rows = jnp.concatenate(grad_branch_tiles, axis=0)
    grad_attended = contract(grad_branch_rows, out_own, 1, 1).astype(BF)
    out_keep, out_got = over_cores(
        contract(attended, grad_branch_rows, 0, 0)[:NARROW].reshape(2, rows_d, D)
    )
    grad_attended, out_got = join(grad_attended, out_got)
    out_total = (out_keep + out_got.astype(F32)).astype(BF)
    grad_attended, out_total, result_bf = join(grad_attended, out_total, result.astype(BF))
    grad_queries, kv_grad_own, kv_grad_away = attend_back(
        flat_ids, row_ids, col_ids, queries, grad_attended, attended, logs, kv_own, kv_other,
        cosine, sine,
    )
    out_far = send(out_total, OTHER_X)
    result_home = send(result_bf, SPREAD)
    vector_part = jnp.concatenate(
        [grad_gain_one, grad_bias_one, grad_gain_two, grad_bias_two]
        + [jnp.zeros((4, D), F32)], axis=0
    )
    grad_queries, kv_grad_own, kv_grad_away, feed_got, out_far, result_home = join(
        grad_queries, kv_grad_own, kv_grad_away, feed_got, out_far, result_home
    )
    kv_grad_got = send(kv_grad_away, OTHER_CORE)
    feed_mine = feed_keep + feed_got
    out_total = (out_total.astype(F32) + out_far.astype(F32)).astype(BF)
    kv_grad_got, feed_mine, out_total = join(kv_grad_got, feed_mine, out_total)
    feed_home = send(feed_mine, HOME_HALF)
    out_got = send(out_total, OTHER_HALF)

    grad_projected, qkv_keep, qkv_away = grad_qkv(
        c.reshape(1), x_rows, grad_queries, kv_grad_own, kv_grad_got, cosine, sine, vector_part
    )
    moved_rows = D // 4 + 16
    qkv_got = send(qkv_away, OTHER_CORE)
    input_parts = square_parts(grad_projected, qkv_own, 1)
    qkv_got, *input_parts = join(qkv_got, *input_parts)

    input_sum = reduce_square(grad_projected, qkv_own, 1, input_parts)
    qkv_keep, qkv_away = whole_call(
        split_x_kernel, "split_x", [((moved_rows, 3 * WIDE), BF)] * 2, x_flag,
        qkv_keep, vector_part, qkv_got,
    )
    qkv_mine, feed_home = join(qkv_keep + send(qkv_away, OTHER_X), feed_home)
    qkv_home = send(qkv_mine, HOME_HALF)
    feed_kept, *feed_sends = whole_call(
        square_feed_kernel, "square_feed",
        [((GROUP + 2, quarter, D), BF)] + [((2, quarter, D), BF)] * 3,
        step_square, feed_mine, feed_home,
    )
    feed_gots = [send(part, HOME_SQUARE[k + 1]) for k, part in enumerate(feed_sends)]
    inputs_back, qkv_home, out_got, *feed_gots = join(
        (grad_res + input_sum).astype(BF), qkv_home, out_got, *feed_gots
    )
    grad_inputs_home = send(inputs_back, SPREAD)
    grad_w_out = send(out_total + out_got, OUT_RETURN)
    qkv_sends = whole_call(
        square_qkv_kernel, "square_qkv", [((quarter + 16, 3 * WIDE), BF)] * GROUP,
        step_square, qkv_mine, qkv_home,
    )
    feed_kept, *qkv_sends = join(feed_kept, *qkv_sends)
    qkv_gots = [qkv_sends[0]] + [send(qkv_sends[k], HOME_SQUARE[k]) for k in range(1, GROUP)]
    (feed_bundle,) = whole_call(
        join_feed_kernel, "join_feed", [bundle_shape], step_square, feed_kept, *feed_gots
    )
    feed_other = send(feed_bundle, HOME_X)
    feed_far = send(feed_bundle, OTHER_CORE)
    grad_inputs_home, grad_w_out, feed_other, feed_far, *qkv_gots = join(
        grad_inputs_home, grad_w_out, feed_other, feed_far, *qkv_gots
    )
    feed_far_other = send(feed_other, OTHER_CORE)
    grad_w_down, grad_w_gate, grad_w_up = whole_call(
        finish_feed_kernel, "finish_feed",
        [(by_x_rows + (D,), F32)] + [((2, quarter, w_gate.shape[1]), F32)] * 2,
        home_flags, feed_bundle, feed_other, feed_far, feed_far_other,
    )
    (qkv_bundle,) = whole_call(
        join_qkv_kernel, "join_qkv", [((moved_rows, 3 * WIDE), BF)], step_square, *qkv_gots
    )
    qkv_other, grad_w_down, grad_w_gate, grad_w_up = join(
        send(qkv_bundle, HOME_X), grad_w_down, grad_w_gate, grad_w_up
    )
    grad_w_qkv, vector_grads = whole_call(
        finish_qkv_kernel, "finish_qkv", [((2, quarter, 3 * D), F32), ((8, D), F32)],
        home_flags, qkv_bundle, qkv_other, send(qkv_bundle, OTHER_CORE), send(qkv_other, OTHER_CORE),
    )
    vector_grads = lax.dynamic_slice_in_dim(vector_grads, shard * rows_d, rows_d, 1)

    return (
        result_home.reshape(tokens_in.shape),
        grad_inputs_home.astype(F32).reshape(tokens_in.shape),
        grad_w_qkv.reshape(w_qkv.shape),
        grad_w_out.astype(F32),
        vector_grads[0],
        vector_grads[1],
        grad_w_gate.reshape(w_gate.shape),
        grad_w_up.reshape(w_up.shape),
        grad_w_down.reshape(w_down.shape),
        vector_grads[2],
        vector_grads[3],
    )


def solution(mesh):
    sizes = dict(mesh.shape)
    clustered = (sizes["rep"], sizes["shard"]) == (4, 8)
    plan = per_device_clustered if clustered else per_device
    return jax.shard_map(
        plan,
        mesh=mesh,
        in_specs=(
            P("rep", "shard", None),
            P("rep", None),
            P("shard", None),
            P("shard", None),
            P("shard"),
            P("shard"),
            P("shard", None),
            P("shard", None),
            P("shard", None),
            P("shard"),
            P("shard"),
            P("rep", "shard", None),
        ),
        out_specs=(
            P("rep", "shard", None),
            P("rep", "shard", None),
            P("shard", None),
            P("shard", None),
            P("shard"),
            P("shard"),
            P("shard", None),
            P("shard", None),
            P("shard", None),
            P("shard"),
            P("shard"),
        ),
        check_vma=False,
    )
```
